32 devices in a mesh: section: 4 (over z), seq: 8 (over y, x, core).
Axes of the slice: x: 2, y: 2, z: 4, core: 2. Of those that a mesh axis runs over, the one named last changes fastest.
Arguments:
- x_a: bfloat16 [1024, 4096], P('seq'), may hold values from -6 to 6
- x_b: bfloat16 [1024, 4096], P('seq'), may hold values from -6 to 6
- grad_a: bfloat16 [1024, 4096], P('seq'), may hold values from -6 to 6
- grad_b: bfloat16 [1024, 4096], P('seq'), may hold values from -6 to 6
- gains: float32 [4, 2, 4096], P('section'), may hold values from 0.5 to 1.5
- kv_weights: bfloat16 [4, 2, 4096, 1024], P('section'), may hold values from -0.09375 to 0.09375
- doc_lengths: int32 [2, 16], replicated, may hold values from 1 to 128, 1024 in all within a row
Outputs:
- acts: bfloat16 [2, 4, 1024, 4096], P(None, 'section', 'seq')
- in_grads: bfloat16 [2, 4, 1024, 4096], P(None, 'section', 'seq')
- kv_grads: bfloat16 [2, 4, 1024, 1024], P(None, 'section', 'seq')
The draws below stay inside these ranges and needn't reach their ends.
Inputs may be any that keep to these rules, and one draw needn't show every extreme that they name: `doc_lengths`: each row lists 16 documents that fill the 1024 tokens of its sequence in order; in each row some document is exactly 128 tokens long.
All inputs are finite; a program needn't handle non-finite values.
Results may differ from the reference program's by a relative error of at most 0.024.
Values may be sent and summed in bfloat16 or wider, within the bound.
A program may use at most 320 MiB of HBM per device.

```python
import math
import jax
import jax.numpy as jnp
import numpy as np
from jax import lax

HEADS = 32
HEAD_DIM = 128
KV_HEADS = 4
REACH = 1
TOK_DEV = 128
D = 4096
KV_WIDTH = 1024
TOKENS = 1024
DOCS = 16
N_SECTION = 4
N_SEQ = 8


def block_scale(own_key, shape, pieces, smallest, high):
    def one(axis_at, blocks):
        steps = jax.random.uniform(jax.random.fold_in(jax.random.fold_in(own_key, 6), axis_at), (blocks,), jnp.float32, smallest / len(pieces), high / len(pieces))
        return jnp.repeat(jnp.exp(steps), shape[axis_at] // blocks).reshape((-1,) + (1,) * (len(shape) - axis_at - 1))

    level = one(*pieces[0])
    for cut in pieces[1:]:
        level = level * one(*cut)
    return level


def profile(count, total, reach, lean):
    portions = [(1 << 20) // math.isqrt(grade ** lean) + 1 for grade in range(2, count + 1)]
    rest, given = total - reach - (count - 1), [1] * (count - 1)
    while rest > 0:
        candidates = [i for i in range(count - 1) if given[i] < reach]
        whole, left = sum([portions[i] for i in candidates]), rest
        for i in candidates:
            addition = min(reach - given[i], max(1, left * portions[i] // whole), rest)
            given[i] = given[i] + addition
            rest = rest - addition
    return np.array([reach] + given)


def uneven(stream_key, count, total, bound, slope):
    if count == 2:
        one = jax.random.randint(stream_key, (), max(1, total - bound), min(bound, total - 1) + 1)
        return jnp.stack([one, total - one])
    tallies = jnp.asarray(profile(count, total, bound, slope), jnp.int32)
    twos = (count - 1) // 2
    donor, taker = tallies[1:1 + 2 * twos:2], tallies[2:2 + 2 * twos:2]
    slack = jnp.minimum(donor - 1, bound - taker)
    moved = jax.random.randint(jax.random.fold_in(stream_key, 1), (twos,), 0, 1 << 20) % (slack + 1)
    tallies = tallies.at[1:1 + 2 * twos:2].set(donor - moved).at[2:2 + 2 * twos:2].set(taker + moved)
    return tallies[jax.random.permutation(jax.random.fold_in(stream_key, 2), count)]


def bell_draw(own_key, extent, spread, most, cuts=(), held_as=jnp.bfloat16):
    result = jax.random.normal(own_key, extent, jnp.float32) * spread
    if len(cuts) > 0:
        result = block_scale(own_key, extent, cuts, -0.22, 0.18) * result
    return jnp.clip(result, min=-most, max=most).astype(held_as)


def setup_inputs(seed: int = 0) -> dict:
    key_of = jax.random.split(jax.random.key(seed), 8)
    x_a = bell_draw(key_of[0], (TOKENS, D), 1.0, 6.0, ((0, 8),))
    x_b = bell_draw(key_of[1], (TOKENS, D), 1.0, 6.0, ((0, 8),))
    grad_a = bell_draw(key_of[2], (TOKENS, D), 1.0, 6.0, ((0, 8),))
    grad_b = bell_draw(key_of[3], (TOKENS, D), 1.0, 6.0, ((0, 8),))
    gains = jnp.clip(1.0 + 0.1 * jax.random.normal(key_of[4], (N_SECTION, 2, D), jnp.float32), 0.5, 1.5)
    kv_weights = bell_draw(key_of[5], (N_SECTION, 2, D, KV_WIDTH), D ** -0.5, 0.09375, ((0, 4),))
    doc_lengths = jax.vmap(lambda own: uneven(own, DOCS, TOKENS, REACH * TOK_DEV, 1))(jax.random.split(key_of[6], 2)).reshape((2, DOCS)).astype(jnp.int32)
    return {"x_a": x_a, "x_b": x_b, "grad_a": grad_a, "grad_b": grad_b, "gains": gains, "kv_weights": kv_weights, "doc_lengths": doc_lengths}


epsilon = 1e-05

def normalize(stream, gain_row):
    widened = stream.astype(jnp.float32)
    square_mean = lax.optimization_barrier(jnp.mean(widened * widened, axis=-1, keepdims=True))
    return (widened * lax.rsqrt(square_mean + epsilon) * gain_row).astype(jnp.bfloat16)

def project_kv(stream, gain_row, weight_mat):
    return jnp.dot(normalize(stream, gain_row), weight_mat, preferred_element_type=jnp.float32).astype(jnp.bfloat16)

def doc_index(ends_row, places):
    return lax.optimization_barrier(jnp.sum((ends_row[None, :] <= places[:, None]).astype(jnp.int32), axis=1)).astype(jnp.int32)

def mix(stream, gain_row, pair_rows, docs_query, place_query, docs_key, place_key):
    row_count = stream.shape[0]
    widened = stream.astype(jnp.float32)
    normed = normalize(stream, gain_row)
    group_size = HEADS // KV_HEADS
    queries = normed.reshape(row_count, KV_HEADS, group_size, HEAD_DIM).astype(jnp.float32)
    key_count = pair_rows.shape[0]
    key_heads = pair_rows[:, :KV_HEADS * HEAD_DIM].reshape(key_count, KV_HEADS, HEAD_DIM).astype(jnp.float32)
    value_heads = pair_rows[:, KV_HEADS * HEAD_DIM:].reshape(key_count, KV_HEADS, HEAD_DIM).astype(jnp.float32)
    scores = jnp.einsum('tkgd,skd->kgts', queries, key_heads) * (1.0 / math.sqrt(HEAD_DIM))
    allowed = (docs_query[:, None] == docs_key[None, :]) & (place_key[None, :] <= place_query[:, None]) & (place_key[None, :] >= 0)
    scores = jnp.where(allowed, scores, -1e+30)
    largest = lax.optimization_barrier(jnp.max(scores, axis=-1, keepdims=True))
    powers = jnp.exp(scores - largest)
    weights = (powers / lax.optimization_barrier(jnp.sum(powers, axis=-1, keepdims=True))).astype(jnp.bfloat16)
    mixture = jnp.einsum('kgts,skd->tkgd', weights.astype(jnp.float32), value_heads)
    return (widened + mixture.reshape(row_count, HEADS * HEAD_DIM)).astype(jnp.bfloat16)

def whole_mix(stream, key_values, gain_row, ends_row):
    width = key_values.shape[-1]
    padded = jnp.concatenate([jnp.zeros((REACH * TOK_DEV, width), key_values.dtype), key_values], axis=0)

    def one_block(block):
        start = (block * TOK_DEV).astype(jnp.int32)
        rows = lax.dynamic_slice_in_dim(stream, start, TOK_DEV, 0)
        pairs = lax.dynamic_slice_in_dim(padded, start, (REACH + 1) * TOK_DEV, 0)
        query_places = (start + jnp.arange(TOK_DEV, dtype=jnp.int32)).astype(jnp.int32)
        key_places = (start - REACH * TOK_DEV + jnp.arange((REACH + 1) * TOK_DEV, dtype=jnp.int32)).astype(jnp.int32)
        return mix(rows, gain_row, pairs, doc_index(ends_row, query_places), query_places, doc_index(ends_row, key_places), key_places)
    outputs = lax.map(one_block, jnp.arange(N_SEQ, dtype=jnp.int32))
    return outputs.reshape(TOKENS, stream.shape[-1])

def reference(x_a, x_b, grad_a, grad_b, gains, kv_weights, doc_lengths):
    acts_all = []
    inputs_all = []
    pairs_all = []
    for direction in range(2):
        ends_row = jnp.cumsum(doc_lengths[direction]).astype(jnp.int32)
        stream = (x_a, x_b)[direction]
        cotangent = (grad_a, grad_b)[direction]
        owners = [layer_index if direction == 0 else N_SECTION - 1 - layer_index for layer_index in range(N_SECTION)]
        inputs_kept = []
        acts_by = [None] * N_SECTION
        ingrad_by = [None] * N_SECTION
        kvgrad_by = [None] * N_SECTION
        for layer_index in range(N_SECTION):
            owner_section = owners[layer_index]
            gain_row = gains[owner_section, direction]
            weight_mat = kv_weights[owner_section, direction]
            inputs_kept.append(stream)
            key_values = project_kv(stream, gain_row, weight_mat)
            stream = whole_mix(stream, key_values, gain_row, ends_row)
            acts_by[owner_section] = stream
        for layer_index in reversed(range(N_SECTION)):
            owner_section = owners[layer_index]
            gain_row = gains[owner_section, direction]
            weight_mat = kv_weights[owner_section, direction]
            layer_input = inputs_kept[layer_index]
            key_values = project_kv(layer_input, gain_row, weight_mat)
            _, pull_mix = jax.vjp(lambda stream_arg, pairs_arg: whole_mix(stream_arg, pairs_arg, gain_row, ends_row), layer_input, key_values)
            grad_stream, grad_pairs = pull_mix(cotangent)
            _, pull_proj = jax.vjp(lambda stream_arg: project_kv(stream_arg, gain_row, weight_mat), layer_input)
            cotangent = grad_stream + pull_proj(grad_pairs)[0]
            ingrad_by[owner_section] = cotangent
            kvgrad_by[owner_section] = grad_pairs
        acts_all.append(jnp.stack(acts_by))
        inputs_all.append(jnp.stack(ingrad_by))
        pairs_all.append(jnp.stack(kvgrad_by))
    return (jnp.stack(acts_all), jnp.stack(inputs_all), jnp.stack(pairs_all))
```

```python
import functools
import math

import jax
import jax.numpy as jnp
from jax import lax
from jax.experimental import pallas as pl
from jax.experimental.pallas import tpu as pltpu
from jax.sharding import PartitionSpec as P

HEADS = 32
HEAD_DIM = 128
KV_HEADS = 4
GROUP = HEADS // KV_HEADS
SCALE = 1.0 / math.sqrt(HEAD_DIM)
LOG2E = math.log2(math.e)

epsilon = 1e-05

F32 = jnp.float32
BF16 = jnp.bfloat16
MESH = pl.DeviceIdType.MESH


def dot(a, b, dims):
    return lax.dot_general(a, b, (dims, ((), ())), preferred_element_type=F32)


def relay_kernel(
    count, shards,
    lengths_ref, xa_ref, xb_ref, ga_ref, gb_ref, gains_ref, weights_ref,
    acts_ref, ingrad_ref, kvgrad_ref,
    wbuf, hbuf, nbuf, kv, wsave, cbuf, outc, dqbuf, gnbuf, gbuf, bias, rstd_buf,
    dsend, drecv, downs, dtot,
    x_sem, w_sem, c_sem, g_sem, gs_sem, gr_sem,
    zs_sem, zr_sem, ss_sem, sr_sem, cs_sem, cr_sem, ds_sem, dr_sem,
    act_sem, ing_sem, kvg_sem,
):
    section = lax.axis_index("section")
    shard = lax.axis_index("seq")
    rows = xa_ref.shape[0]
    width = xa_ref.shape[1]
    tile = width // KV_HEADS
    half = KV_HEADS * HEAD_DIM
    near = lax.div(2 * section, count)
    near_depth = section + near * (count - 1 - 2 * section)
    far = 1 - near
    far_depth = count - 1 - near_depth
    following = lax.rem(shard + 1, shards)
    preceding = lax.rem(shard + shards - 1, shards)

    def depth_of(d):
        return section + d * (count - 1 - 2 * section)

    def x_copy(d, t):
        ref = (xa_ref, xb_ref)[d]
        return pltpu.make_async_copy(
            ref.at[:, pl.ds(t * tile, tile)], hbuf.at[d, 0, t], x_sem.at[d, t]
        )

    def grad_copy(d, t):
        ref = (ga_ref, gb_ref)[d]
        return pltpu.make_async_copy(
            ref.at[:, pl.ds(t * tile, tile)], cbuf.at[d, t], c_sem.at[d, t]
        )

    def weight_copy(d, k, part):
        return pltpu.make_async_copy(
            weights_ref.at[0, d, :, pl.ds(pl.multiple_of(part * half + k * HEAD_DIM, HEAD_DIM), HEAD_DIM)],
            wbuf.at[d, k, :, pl.ds(part * HEAD_DIM, HEAD_DIM)],
            w_sem.at[d, k, part],
        )

    def gain_copy(distance):
        return pltpu.make_async_remote_copy(
            src_ref=gains_ref,
            dst_ref=gbuf.at[section],
            send_sem=gs_sem.at[distance - 1],
            recv_sem=gr_sem.at[distance - 1],
            device_id={"section": lax.rem(section + distance, count)},
            device_id_type=MESH,
        )

    def z_copy(d, l, k):
        own = kv.at[d, l, k, :, pl.ds(rows, rows), :]
        return pltpu.make_async_remote_copy(
            src_ref=own, dst_ref=own, send_sem=zs_sem.at[d, l, k], recv_sem=zr_sem.at[d, l, k],
            device_id={"section": section + 1 - 2 * d}, device_id_type=MESH,
        )

    def s_copy(d, l, k):
        return pltpu.make_async_remote_copy(
            src_ref=kv.at[d, l, k, :, pl.ds(rows, rows), :],
            dst_ref=kv.at[d, l, k, :, pl.ds(0, rows), :],
            send_sem=ss_sem.at[d, l, k], recv_sem=sr_sem.at[d, l, k],
            device_id={"seq": following}, device_id_type=MESH,
        )

    def c_copy(d, t):
        return pltpu.make_async_remote_copy(
            src_ref=outc.at[d, t], dst_ref=cbuf.at[d, t],
            send_sem=cs_sem.at[d, t], recv_sem=cr_sem.at[d, t],
            device_id={"section": section - 1 + 2 * d}, device_id_type=MESH,
        )

    def d_copy(d, k):
        return pltpu.make_async_remote_copy(
            src_ref=dsend.at[d, k], dst_ref=drecv.at[d, k],
            send_sem=ds_sem.at[d, k], recv_sem=dr_sem.at[d, k],
            device_id={"seq": preceding}, device_id_type=MESH,
        )

    def column_slice(t):
        return pl.ds(pl.multiple_of(t * tile, tile), tile)

    def act_copy(d, parity, t):
        return pltpu.make_async_copy(
            hbuf.at[d, parity, t], acts_ref.at[d, 0, :, column_slice(t)], act_sem.at[d, t]
        )

    def ing_copy(d, t):
        return pltpu.make_async_copy(
            outc.at[d, t], ingrad_ref.at[d, 0, :, column_slice(t)], ing_sem.at[d, t]
        )

    def kvg_copy(d, k, part):
        start = pl.multiple_of(part * half + k * HEAD_DIM, HEAD_DIM)
        return pltpu.make_async_copy(
            dtot.at[d, k, :, pl.ds(part * HEAD_DIM, HEAD_DIM)],
            kvgrad_ref.at[d, 0, :, pl.ds(start, HEAD_DIM)],
            kvg_sem.at[d, k, part],
        )

    for t in range(KV_HEADS):
        x_copy(0, t).start()
        x_copy(1, t).start()
    own_gain = pltpu.make_async_copy(gains_ref, gbuf.at[section], g_sem)
    own_gain.start()
    for d in (near, far):
        for k in range(KV_HEADS):
            for part in range(2):
                weight_copy(d, k, part).start()
    for d, last in ((0, count - 1), (1, 0)):
        @pl.when(section == last)
        def _():
            for t in range(KV_HEADS):
                grad_copy(d, t).start()

    barrier = pltpu.get_barrier_semaphore()
    for neighbour in (following, preceding):
        pl.semaphore_signal(barrier, inc=1, device_id={"seq": neighbour}, device_id_type=MESH)
    for distance in range(1, count):
        pl.semaphore_signal(
            barrier, inc=1, device_id={"section": lax.rem(section + distance, count)},
            device_id_type=MESH,
        )

    key_places = (shard - 1) * rows + lax.broadcasted_iota(jnp.int32, (2 * rows, rows), 0)
    places = shard * rows + lax.broadcasted_iota(jnp.int32, (2 * rows, rows), 1)
    for d in range(2):
        end = jnp.int32(0)
        docs_k = jnp.zeros((2 * rows, rows), jnp.int32)
        docs_q = jnp.zeros((2 * rows, rows), jnp.int32)
        for j in range(lengths_ref.shape[1]):
            end = end + lengths_ref[d, j]
            docs_k = docs_k + jnp.where(key_places >= end, 1, 0)
            docs_q = docs_q + jnp.where(places >= end, 1, 0)
        allowed = (docs_k == docs_q) & (key_places <= places) & (key_places >= 0)
        bias[d] = jnp.where(allowed, 0.0, -1e30).astype(F32)

    pl.semaphore_wait(barrier, count + 1)
    for distance in range(1, count):
        gain_copy(distance).start()
    for t in range(KV_HEADS):
        x_copy(0, t).wait()
        x_copy(1, t).wait()
    own_gain.wait()

    def normalize(d, l, parity):
        home = l + d * (count - 1 - 2 * l)
        squares = jnp.zeros((rows, HEAD_DIM), F32)
        for t in range(KV_HEADS):
            for g in range(GROUP):
                part = hbuf[d, parity, t, :, g * HEAD_DIM:(g + 1) * HEAD_DIM].astype(F32)
                squares = squares + part * part
        rstd = lax.rsqrt(jnp.sum(squares, axis=-1, keepdims=True) * (1.0 / width) + epsilon)
        rstd = jnp.broadcast_to(rstd, (rows, HEAD_DIM))
        rstd_buf[d] = rstd
        for t in range(KV_HEADS):
            for g in range(GROUP):
                cols = slice(g * HEAD_DIM, (g + 1) * HEAD_DIM)
                gain = gbuf[home, d, :, t * tile + g * HEAD_DIM:t * tile + (g + 1) * HEAD_DIM]
                part = hbuf[d, parity, t, :, cols].astype(F32)
                nbuf[d, t, :, cols] = (part * rstd * gain).astype(BF16)

    def project(d, depth):
        normalize(d, depth, lax.rem(depth, 2))

        def chunk(k, carry):
            weight_copy(d, k, 0).wait()
            weight_copy(d, k, 1).wait()
            pair = jnp.zeros((rows, 2 * HEAD_DIM), F32)
            for t in range(KV_HEADS):
                pair = pair + dot(
                    nbuf[d, t], wbuf[d, k, t * tile:(t + 1) * tile, :], ((1,), (0,))
                )
            pair = pair.astype(BF16)
            kv[d, depth, k, 0, rows:, :] = pair[:, :HEAD_DIM]
            kv[d, depth, k, 1, rows:, :] = pair[:, HEAD_DIM:]

            @pl.when(depth < count - 1)
            def _():
                z_copy(d, depth, k).start()

            s_copy(d, depth, k).start()
            return carry

        lax.fori_loop(0, KV_HEADS, chunk, 0)

    def mix(d, l, depth):
        parity = lax.rem(l, 2)

        @pl.when(l < depth)
        def _():
            normalize(d, l, parity)

        def arrive(k):
            @pl.when(l < depth)
            def _():
                z_copy(d, l, k).wait_recv()

                @pl.when(depth < count - 1)
                def _():
                    z_copy(d, l, k).start()

                s_copy(d, l, k).start()

        arrive(0)

        def chunk(k, carry):
            @pl.when(k + 1 < KV_HEADS)
            def _():
                arrive(k + 1)

            s_copy(d, l, k).wait_recv()
            keys = kv[d, l, k, 0]
            values = kv[d, l, k, 1]
            masked = bias[d]
            for g in range(GROUP):
                cols = slice(g * HEAD_DIM, (g + 1) * HEAD_DIM)
                scores = dot(keys, nbuf[d, k, :, cols], ((1,), (1,))) + masked
                powers = jnp.exp2((scores - jnp.max(scores, axis=0, keepdims=True)) * (SCALE * LOG2E))
                weights = (powers * (1.0 / jnp.sum(powers, axis=0, keepdims=True))).astype(BF16)
                wsave[d, k, g] = weights
                mixture = dot(weights, values, ((0,), (0,)))
                hbuf[d, 1 - parity, k, :, cols] = (
                    hbuf[d, parity, k, :, cols].astype(F32) + mixture
                ).astype(BF16)

            @pl.when(l == depth)
            def _():
                act_copy(d, 1 - parity, k).start()

            return carry

        lax.fori_loop(0, KV_HEADS, chunk, 0)

    def forward(v, carry):
        p = near_depth
        is_near = (v < p) | (v == 2 * p)
        d = jnp.where(is_near, near, far)
        depth = jnp.where(is_near, near_depth, far_depth)
        l = jnp.where(v < p, v, jnp.where(v < 2 * p, v - p, jnp.where(v == 2 * p, p, v - p - 1)))

        @pl.when((v == p) | (v == count))
        def _():
            pd = jnp.where(v == p, near, far)
            project(pd, jnp.where(v == p, near_depth, far_depth))

        @pl.when(v == 0)
        def _():
            for distance in range(1, count):
                gain_copy(distance).wait_recv()

        mix(d, l, depth)
        return carry

    lax.fori_loop(0, count + 1, forward, 0)

    def backward(i, carry):
        d = jnp.where(i == 0, far, near)
        depth = jnp.where(i == 0, far_depth, near_depth)
        parity = lax.rem(depth, 2)

        def chunk(k, inner_carry):
            @pl.when(depth < count - 1)
            def _():
                c_copy(d, k).wait_recv()

            @pl.when(depth == count - 1)
            def _():
                pltpu.make_async_copy(cbuf.at[d, k], cbuf.at[d, k], c_sem.at[d, k]).wait()

            keys = kv[d, depth, k, 0]
            values = kv[d, depth, k, 1]
            grads, queries, probs, cots = [], [], [], []
            for g in range(GROUP):
                cols = slice(g * HEAD_DIM, (g + 1) * HEAD_DIM)
                query = nbuf[d, k, :, cols]
                cot = cbuf[d, k, :, cols]
                weights = wsave[d, k, g]
                wide = weights.astype(F32)
                grad_w = dot(values, cot, ((1,), (1,)))
                mean = jnp.sum(grad_w * wide, axis=0, keepdims=True)
                grad_s = (wide * (grad_w - mean) * SCALE).astype(BF16)
                dqbuf[k, :, cols] = dot(grad_s, keys, ((0,), (0,))).astype(BF16)
                grads.append(grad_s)
                queries.append(query)
                probs.append(weights)
                cots.append(cot)
            grad_k = dot(
                jnp.concatenate(grads, axis=1), jnp.concatenate(queries, axis=0), ((1,), (0,))
            )
            grad_v = dot(
                jnp.concatenate(probs, axis=1), jnp.concatenate(cots, axis=0), ((1,), (0,))
            )
            dsend[d, k, 0] = grad_k[:rows].astype(BF16)
            dsend[d, k, 1] = grad_v[:rows].astype(BF16)
            downs[k, 0] = grad_k[rows:].astype(BF16)
            downs[k, 1] = grad_v[rows:].astype(BF16)
            d_copy(d, k).start()
            return inner_carry

        lax.fori_loop(0, KV_HEADS, chunk, 0)

        for k in range(KV_HEADS):
            d_copy(d, k).wait_recv()
            for part in range(2):
                total = downs[k, part].astype(F32) + drecv[d, k, part].astype(F32)
                dtot[d, k, :, part * HEAD_DIM:(part + 1) * HEAD_DIM] = total.astype(BF16)
                kvg_copy(d, k, part).start()

        home = section
        rstd = rstd_buf[d]

        def grad_tile(t, inner):
            grad = jnp.zeros((rows, tile), F32)
            start = pl.multiple_of(t * tile, tile)
            for k in range(KV_HEADS):
                grad = grad + dot(
                    dtot[d, k], wbuf[d, k, pl.ds(start, tile), :], ((1,), (1,))
                )
            for g in range(GROUP):
                cols = slice(g * HEAD_DIM, (g + 1) * HEAD_DIM)
                gain = gbuf[home, d, :, pl.ds(pl.multiple_of(start + g * HEAD_DIM, HEAD_DIM), HEAD_DIM)]
                grad_n = (grad[:, cols] + dqbuf[t, :, cols].astype(F32)) * gain
                gnbuf[t, :, cols] = grad_n
                inner = inner + grad_n * hbuf[d, parity, t, :, cols].astype(F32)
            return inner

        inner = lax.fori_loop(0, KV_HEADS, grad_tile, jnp.zeros((rows, HEAD_DIM), F32))
        inner = jnp.broadcast_to(jnp.sum(inner, axis=-1, keepdims=True), (rows, HEAD_DIM))
        factor = inner * (1.0 / width) * rstd * rstd * rstd

        def total_tile(t, inner_carry):
            for g in range(GROUP):
                cols = slice(g * HEAD_DIM, (g + 1) * HEAD_DIM)
                grad_h = gnbuf[t, :, cols] * rstd - hbuf[d, parity, t, :, cols].astype(F32) * factor
                outc[d, t, :, cols] = (cbuf[d, t, :, cols].astype(F32) + grad_h).astype(BF16)

            @pl.when(depth > 0)
            def _():
                c_copy(d, t).start()

            ing_copy(d, t).start()
            return inner_carry

        lax.fori_loop(0, KV_HEADS, total_tile, 0)
        return carry

    lax.fori_loop(0, 2, backward, 0)

    for distance in range(1, count):
        gain_copy(distance).wait_send()
    for d in range(2):
        depth = depth_of(d)

        def layer_drain(l, carry):
            for k in range(KV_HEADS):
                @pl.when(depth < count - 1)
                def _():
                    z_copy(d, l, k).wait_send()

                s_copy(d, l, k).wait_send()
            return carry

        lax.fori_loop(0, depth + 1, layer_drain, 0)
        for k in range(KV_HEADS):
            d_copy(d, k).wait_send()

            @pl.when(depth > 0)
            def _():
                c_copy(d, k).wait_send()

            act_copy(d, lax.rem(depth + 1, 2), k).wait()
            ing_copy(d, k).wait()
            kvg_copy(d, k, 0).wait()
            kvg_copy(d, k, 1).wait()


def per_device(x_a, x_b, grad_a, grad_b, gains, kv_weights, doc_lengths):
    count = lax.axis_size("section")
    shards = lax.axis_size("seq")
    rows, width = x_a.shape
    pair_width = kv_weights.shape[-1]
    tile = width // KV_HEADS
    gains = gains[0][:, None, :]
    dma = pltpu.SemaphoreType.DMA
    anywhere = pl.BlockSpec(memory_space=pl.ANY)
    return pl.pallas_call(
        functools.partial(relay_kernel, count, shards),
        in_specs=[pl.BlockSpec(memory_space=pltpu.SMEM)] + [anywhere] * 6,
        out_specs=[anywhere] * 3,
        out_shape=[
            jax.ShapeDtypeStruct((2, 1, rows, width), BF16),
            jax.ShapeDtypeStruct((2, 1, rows, width), BF16),
            jax.ShapeDtypeStruct((2, 1, rows, pair_width), BF16),
        ],
        scratch_shapes=[
            pltpu.VMEM((2, KV_HEADS, width, 2 * HEAD_DIM), BF16),
            pltpu.VMEM((2, 2, KV_HEADS, rows, tile), BF16),
            pltpu.VMEM((2, KV_HEADS, rows, tile), BF16),
            pltpu.VMEM((2, count, KV_HEADS, 2, 2 * rows, HEAD_DIM), BF16),
            pltpu.VMEM((2, KV_HEADS, GROUP, 2 * rows, rows), BF16),
            pltpu.VMEM((2, KV_HEADS, rows, tile), BF16),
            pltpu.VMEM((2, KV_HEADS, rows, tile), BF16),
            pltpu.VMEM((KV_HEADS, rows, tile), BF16),
            pltpu.VMEM((KV_HEADS, rows, tile), F32),
            pltpu.VMEM((count, 2, 1, width), F32),
            pltpu.VMEM((2, 2 * rows, rows), F32),
            pltpu.VMEM((2, rows, HEAD_DIM), F32),
            pltpu.VMEM((2, KV_HEADS, 2, rows, HEAD_DIM), BF16),
            pltpu.VMEM((2, KV_HEADS, 2, rows, HEAD_DIM), BF16),
            pltpu.VMEM((KV_HEADS, 2, rows, HEAD_DIM), BF16),
            pltpu.VMEM((2, KV_HEADS, rows, 2 * HEAD_DIM), BF16),
            dma((2, KV_HEADS)),
            dma((2, KV_HEADS, 2)),
            dma((2, KV_HEADS)),
            dma(()),
            dma((count - 1,)),
            dma((count - 1,)),
            dma((2, count, KV_HEADS)),
            dma((2, count, KV_HEADS)),
            dma((2, count, KV_HEADS)),
            dma((2, count, KV_HEADS)),
            dma((2, KV_HEADS)),
            dma((2, KV_HEADS)),
            dma((2, KV_HEADS)),
            dma((2, KV_HEADS)),
            dma((2, KV_HEADS)),
            dma((2, KV_HEADS)),
            dma((2, KV_HEADS, 2)),
        ],
        compiler_params=pltpu.CompilerParams(
            collective_id=0, has_side_effects=True, vmem_limit_bytes=60 * 1024 * 1024
        ),
        name="relay",
    )(doc_lengths, x_a, x_b, grad_a, grad_b, gains, kv_weights)


def solution(mesh):
    in_specs = (
        P("seq", None),
        P("seq", None),
        P("seq", None),
        P("seq", None),
        P("section", None, None),
        P("section", None, None, None),
        P(),
    )
    out_specs = (
        P(None, "section", "seq", None),
        P(None, "section", "seq", None),
        P(None, "section", "seq", None),
    )
    return jax.shard_map(
        per_device, mesh=mesh, in_specs=in_specs, out_specs=out_specs, check_vma=False
    )
```

```python
import functools
import math

import jax
import jax.numpy as jnp
from jax import lax
from jax.experimental import pallas as pl
from jax.experimental.pallas import tpu as pltpu
from jax.sharding import PartitionSpec as P

HEADS = 32
HEAD_DIM = 128
KV_HEADS = 4
GROUP = HEADS // KV_HEADS
SCALE = 1.0 / math.sqrt(HEAD_DIM)
LOG2E = math.log2(math.e)

epsilon = 1e-05

F32 = jnp.float32
BF16 = jnp.bfloat16
MESH = pl.DeviceIdType.MESH


def dot(a, b, dims):
    return lax.dot_general(a, b, (dims, ((), ())), preferred_element_type=F32)


def relay_kernel(
    count, shards,
    lengths_ref, xa_ref, xb_ref, ga_ref, gb_ref, gains_ref, weights_ref,
    acts_ref, ingrad_ref, kvgrad_ref,
    wbuf, hbuf, nbuf, kv, wsave, cbuf, outc, dqbuf, gnbuf, gbuf, bias, rstd_buf,
    dsend, drecv, downs, dtot, triangle, squares_buf,
    x_sem, w_sem, c_sem, g_sem, gs_sem, gr_sem,
    zs_sem, zr_sem, ss_sem, sr_sem, cs_sem, cr_sem, ds_sem, dr_sem,
    act_sem, ing_sem, kvg_sem,
):
    section = lax.axis_index("section")
    shard = lax.axis_index("seq")
    rows = xa_ref.shape[0]
    width = xa_ref.shape[1]
    tile = width // KV_HEADS
    half = KV_HEADS * HEAD_DIM
    near = lax.div(2 * section, count)
    near_depth = section + near * (count - 1 - 2 * section)
    far = 1 - near
    far_depth = count - 1 - near_depth
    following = lax.rem(shard + 1, shards)
    preceding = lax.rem(shard + shards - 1, shards)

    def depth_of(d):
        return section + d * (count - 1 - 2 * section)

    def x_copy(d, t):
        ref = (xa_ref, xb_ref)[d]
        return pltpu.make_async_copy(
            ref.at[:, pl.ds(t * tile, tile)], hbuf.at[d, 0, t], x_sem.at[d, t]
        )

    def grad_copy(d, t):
        ref = (ga_ref, gb_ref)[d]
        return pltpu.make_async_copy(
            ref.at[:, pl.ds(t * tile, tile)], cbuf.at[d, t], c_sem.at[d, t]
        )

    def weight_copy(d, k, part):
        return pltpu.make_async_copy(
            weights_ref.at[0, d, :, pl.ds(pl.multiple_of(part * half + k * HEAD_DIM, HEAD_DIM), HEAD_DIM)],
            wbuf.at[d, k, :, pl.ds(part * HEAD_DIM, HEAD_DIM)],
            w_sem.at[d, k, part],
        )

    def gain_copy(distance):
        return pltpu.make_async_remote_copy(
            src_ref=gains_ref.at[0],
            dst_ref=gbuf.at[section],
            send_sem=gs_sem.at[distance - 1],
            recv_sem=gr_sem.at[distance - 1],
            device_id={"section": lax.rem(section + distance, count)},
            device_id_type=MESH,
        )

    def z_copy(d, l, k):
        own = kv.at[d, l, k, :, pl.ds(rows, rows), :]
        return pltpu.make_async_remote_copy(
            src_ref=own, dst_ref=own, send_sem=zs_sem.at[d, l, k], recv_sem=zr_sem.at[d, l, k],
            device_id={"section": section + 1 - 2 * d}, device_id_type=MESH,
        )

    def s_copy(d, l, k):
        return pltpu.make_async_remote_copy(
            src_ref=kv.at[d, l, k, :, pl.ds(rows, rows), :],
            dst_ref=kv.at[d, l, k, :, pl.ds(0, rows), :],
            send_sem=ss_sem.at[d, l, k], recv_sem=sr_sem.at[d, l, k],
            device_id={"seq": following}, device_id_type=MESH,
        )

    def c_copy(d, t):
        return pltpu.make_async_remote_copy(
            src_ref=outc.at[d, t], dst_ref=cbuf.at[d, t],
            send_sem=cs_sem.at[d, t], recv_sem=cr_sem.at[d, t],
            device_id={"section": section - 1 + 2 * d}, device_id_type=MESH,
        )

    def d_copy(d, k):
        return pltpu.make_async_remote_copy(
            src_ref=dsend.at[d, k], dst_ref=drecv.at[d, k],
            send_sem=ds_sem.at[d, k], recv_sem=dr_sem.at[d, k],
            device_id={"seq": preceding}, device_id_type=MESH,
        )

    def column_slice(t):
        return pl.ds(pl.multiple_of(t * tile, tile), tile)

    def act_copy(d, parity, t):
        return pltpu.make_async_copy(
            hbuf.at[d, parity, t], acts_ref.at[d, 0, :, column_slice(t)], act_sem.at[d, t]
        )

    def ing_copy(d, t):
        return pltpu.make_async_copy(
            outc.at[d, t], ingrad_ref.at[d, 0, :, column_slice(t)], ing_sem.at[d, t]
        )

    def kvg_copy(d, k, part):
        start = pl.multiple_of(part * half + k * HEAD_DIM, HEAD_DIM)
        return pltpu.make_async_copy(
            dtot.at[d, k, :, pl.ds(part * HEAD_DIM, HEAD_DIM)],
            kvgrad_ref.at[d, 0, :, pl.ds(start, HEAD_DIM)],
            kvg_sem.at[d, k, part],
        )

    for t in range(KV_HEADS):
        x_copy(0, t).start()
        x_copy(1, t).start()
    own_gain = pltpu.make_async_copy(gains_ref.at[0], gbuf.at[section], g_sem)
    own_gain.start()
    for d in (near, far):
        for k in range(KV_HEADS):
            for part in range(2):
                weight_copy(d, k, part).start()
    for d, last in ((0, count - 1), (1, 0)):
        @pl.when(section == last)
        def _():
            for t in range(KV_HEADS):
                grad_copy(d, t).start()

    barrier = pltpu.get_barrier_semaphore()
    for neighbour in (following, preceding):
        pl.semaphore_signal(barrier, inc=1, device_id={"seq": neighbour}, device_id_type=MESH)
    for distance in range(1, count):
        pl.semaphore_signal(
            barrier, inc=1, device_id={"section": lax.rem(section + distance, count)},
            device_id_type=MESH,
        )

    key_places = (shard - 1) * rows + lax.broadcasted_iota(jnp.int32, (2 * rows, rows), 0)
    places = shard * rows + lax.broadcasted_iota(jnp.int32, (2 * rows, rows), 1)
    for d in range(2):
        end = jnp.int32(0)
        docs_k = jnp.zeros((2 * rows, rows), jnp.int32)
        docs_q = jnp.zeros((2 * rows, rows), jnp.int32)
        for j in range(lengths_ref.shape[1]):
            end = end + lengths_ref[d, j]
            docs_k = docs_k + jnp.where(key_places >= end, 1, 0)
            docs_q = docs_q + jnp.where(places >= end, 1, 0)
        allowed = (docs_k == docs_q) & (key_places <= places) & (key_places >= 0)
        bias[d] = jnp.where(allowed, 0.0, -1e30).astype(F32)
    sublane = lax.broadcasted_iota(jnp.int32, (rows, rows), 0)
    lane = lax.broadcasted_iota(jnp.int32, (rows, rows), 1)
    triangle[0] = jnp.where(sublane > lane, 1.0, 0.0).astype(BF16)
    triangle[1] = jnp.where(sublane <= lane, 1.0, 0.0).astype(BF16)
    triangle[2] = jnp.where(lane > sublane, 1.0, 0.0).astype(BF16)
    triangle[3] = jnp.where(lane <= sublane, 1.0, 0.0).astype(BF16)

    pl.semaphore_wait(barrier, count + 1)
    for distance in range(1, count):
        gain_copy(distance).start()
    for t in range(KV_HEADS):
        x_copy(0, t).wait()
        x_copy(1, t).wait()
    own_gain.wait()

    def gain_of(home, d, cols):
        return jnp.where(d == 0, gbuf[home, 0:1, cols], gbuf[home, 1:2, cols])

    def normalize(d, l, parity):
        home = l + d * (count - 1 - 2 * l)

        @pl.when(l == 0)
        def _():
            squares = jnp.zeros((rows, HEAD_DIM), F32)
            for t in range(KV_HEADS):
                for g in range(GROUP):
                    part = hbuf[d, parity, t, :, g * HEAD_DIM:(g + 1) * HEAD_DIM].astype(F32)
                    squares = squares + part * part
            squares_buf[d] = squares

        square_mean = jnp.sum(squares_buf[d], axis=-1, keepdims=True) * (1.0 / width)
        rstd = jnp.broadcast_to(lax.rsqrt(square_mean + epsilon), (rows, HEAD_DIM))
        rstd_buf[d] = rstd
        for t in range(KV_HEADS):
            for g in range(GROUP):
                cols = slice(g * HEAD_DIM, (g + 1) * HEAD_DIM)
                gain = gain_of(home, d, slice(t * tile + g * HEAD_DIM, t * tile + (g + 1) * HEAD_DIM))
                part = hbuf[d, parity, t, :, cols].astype(F32)
                nbuf[d, t, :, cols] = (part * rstd * gain).astype(BF16)

    def project(d, depth):
        normalize(d, depth, lax.rem(depth, 2))

        def chunk(k, carry):
            weight_copy(d, k, 0).wait()
            weight_copy(d, k, 1).wait()
            normed = jnp.concatenate([nbuf[d, t] for t in range(KV_HEADS)], axis=1)
            pair = dot(normed, wbuf[d, k], ((1,), (0,))).astype(BF16)
            kv[d, depth, k, 0, rows:, :] = pair[:, :HEAD_DIM]
            kv[d, depth, k, 1, rows:, :] = pair[:, HEAD_DIM:]

            @pl.when(depth < count - 1)
            def _():
                z_copy(d, depth, k).start()

            s_copy(d, depth, k).start()
            return carry

        lax.fori_loop(0, KV_HEADS, chunk, 0)

    def mix(d, l, depth):
        parity = lax.rem(l, 2)

        @pl.when(l < depth)
        def _():
            normalize(d, l, parity)

        squares_buf[d] = jnp.zeros((rows, HEAD_DIM), F32)

        def arrive(k):
            @pl.when(l < depth)
            def _():
                z_copy(d, l, k).wait_recv()

                @pl.when(depth < count - 1)
                def _():
                    z_copy(d, l, k).start()

                s_copy(d, l, k).start()

        arrive(0)

        def chunk(k, carry):
            @pl.when(k + 1 < KV_HEADS)
            def _():
                arrive(k + 1)

            s_copy(d, l, k).wait_recv()
            keys = kv[d, l, k, 0]
            values = kv[d, l, k, 1]
            spreads = []
            for g in range(GROUP):
                both = dot(keys, nbuf[d, k, :, g * HEAD_DIM:(g + 1) * HEAD_DIM], ((1,), (1,)))
                scores = jnp.maximum(both[:rows] + bias[d, :rows, :], both[rows:] + bias[d, rows:, :])
                powers = jnp.exp2((scores - jnp.max(scores, axis=0, keepdims=True)) * (SCALE * LOG2E))
                weights = (powers * (1.0 / jnp.sum(powers, axis=0, keepdims=True))).astype(BF16)
                wsave[d, k, g] = weights
                turned = weights.T
                spreads.append(jnp.concatenate([turned * triangle[2], turned * triangle[3]], axis=1))
            for g in range(GROUP):
                cols = slice(g * HEAD_DIM, (g + 1) * HEAD_DIM)
                total = hbuf[d, parity, k, :, cols].astype(F32) + dot(spreads[g], values, ((1,), (0,)))
                hbuf[d, 1 - parity, k, :, cols] = total.astype(BF16)
                squares_buf[d] += total * total

            @pl.when(l == depth)
            def _():
                act_copy(d, 1 - parity, k).start()

            return carry

        lax.fori_loop(0, KV_HEADS, chunk, 0)

    def forward(v, carry):
        p = near_depth
        is_near = (v < p) | (v == 2 * p)
        d = jnp.where(is_near, near, far)
        depth = jnp.where(is_near, near_depth, far_depth)
        l = jnp.where(v < p, v, jnp.where(v < 2 * p, v - p, jnp.where(v == 2 * p, p, v - p - 1)))

        @pl.when((v == p) | (v == count))
        def _():
            pd = jnp.where(v == p, near, far)
            project(pd, jnp.where(v == p, near_depth, far_depth))

        @pl.when(v == 0)
        def _():
            for distance in range(1, count):
                gain_copy(distance).wait_recv()

        mix(d, l, depth)
        return carry

    lax.fori_loop(0, count + 1, forward, 0)

    def backward(i, carry):
        d = jnp.where(i == 0, far, near)
        depth = jnp.where(i == 0, far_depth, near_depth)
        parity = lax.rem(depth, 2)

        def chunk(k, inner_carry):
            @pl.when(depth < count - 1)
            def _():
                c_copy(d, k).wait_recv()

            @pl.when(depth == count - 1)
            def _():
                pltpu.make_async_copy(cbuf.at[d, k], cbuf.at[d, k], c_sem.at[d, k]).wait()

            keys = kv[d, depth, k, 0]
            values = kv[d, depth, k, 1]
            earlier_s, own_s, earlier_w, own_w, queries, cots, spreads = [], [], [], [], [], [], []
            own_first = lax.broadcasted_iota(jnp.int32, (rows, rows), 0) <= (
                lax.broadcasted_iota(jnp.int32, (rows, rows), 1)
            )
            for g in range(GROUP):
                cols = slice(g * HEAD_DIM, (g + 1) * HEAD_DIM)
                cot = cbuf[d, k, :, cols]
                both = dot(values, cot, ((1,), (1,)))
                weights = wsave[d, k, g]
                wide = weights.astype(F32)
                grad_w = jnp.where(own_first, both[rows:], both[:rows]) * wide
                mean = jnp.sum(grad_w, axis=0, keepdims=True)
                grad_s = ((grad_w - wide * mean) * SCALE).astype(BF16)
                earlier_s.append(grad_s * triangle[0])
                own_s.append(grad_s * triangle[1])
                earlier_w.append(weights * triangle[0])
                own_w.append(weights * triangle[1])
                queries.append(nbuf[d, k, :, cols])
                cots.append(cot)
                turned = grad_s.T
                spreads.append(jnp.concatenate([turned * triangle[2], turned * triangle[3]], axis=1))
            for g in range(GROUP):
                cols = slice(g * HEAD_DIM, (g + 1) * HEAD_DIM)
                dqbuf[k, :, cols] = dot(spreads[g], keys, ((1,), (0,))).astype(BF16)
            all_s = jnp.concatenate(
                [jnp.concatenate(earlier_s, axis=1), jnp.concatenate(own_s, axis=1)], axis=0
            )
            all_w = jnp.concatenate(
                [jnp.concatenate(earlier_w, axis=1), jnp.concatenate(own_w, axis=1)], axis=0
            )
            grad_k = dot(all_s, jnp.concatenate(queries, axis=0), ((1,), (0,)))
            grad_v = dot(all_w, jnp.concatenate(cots, axis=0), ((1,), (0,)))
            dsend[d, k, 0] = grad_k[:rows].astype(BF16)
            dsend[d, k, 1] = grad_v[:rows].astype(BF16)
            downs[k, 0] = grad_k[rows:].astype(BF16)
            downs[k, 1] = grad_v[rows:].astype(BF16)
            d_copy(d, k).start()
            return inner_carry

        lax.fori_loop(0, KV_HEADS, chunk, 0)

        for k in range(KV_HEADS):
            d_copy(d, k).wait_recv()
            for part in range(2):
                total = downs[k, part].astype(F32) + drecv[d, k, part].astype(F32)
                dtot[d, k, :, part * HEAD_DIM:(part + 1) * HEAD_DIM] = total.astype(BF16)
                kvg_copy(d, k, part).start()

        home = section
        rstd = rstd_buf[d]

        def grad_tile(t, inner):
            pairs = jnp.concatenate([dtot[d, k] for k in range(KV_HEADS)], axis=1)
            step = 2 * HEAD_DIM
            for u in range(tile // step):
                start = pl.multiple_of(t * tile + u * step, step)
                weights = jnp.concatenate(
                    [wbuf[d, k, pl.ds(start, step), :] for k in range(KV_HEADS)], axis=1
                )
                cols = slice(u * step, (u + 1) * step)
                gain = gain_of(home, d, pl.ds(start, step))
                grad_n = (dot(pairs, weights, ((1,), (1,))) + dqbuf[t, :, cols].astype(F32)) * gain
                gnbuf[t, :, cols] = grad_n
                product = grad_n * hbuf[d, parity, t, :, cols].astype(F32)
                inner = inner + product[:, :HEAD_DIM] + product[:, HEAD_DIM:]
            return inner

        inner = lax.fori_loop(0, KV_HEADS, grad_tile, jnp.zeros((rows, HEAD_DIM), F32))
        inner = jnp.broadcast_to(jnp.sum(inner, axis=-1, keepdims=True), (rows, HEAD_DIM))
        factor = inner * (1.0 / width) * rstd * rstd * rstd

        def total_tile(t, inner_carry):
            for g in range(GROUP):
                cols = slice(g * HEAD_DIM, (g + 1) * HEAD_DIM)
                grad_h = gnbuf[t, :, cols] * rstd - hbuf[d, parity, t, :, cols].astype(F32) * factor
                outc[d, t, :, cols] = (cbuf[d, t, :, cols].astype(F32) + grad_h).astype(BF16)

            @pl.when(depth > 0)
            def _():
                c_copy(d, t).start()

            ing_copy(d, t).start()
            return inner_carry

        lax.fori_loop(0, KV_HEADS, total_tile, 0)
        return carry

    lax.fori_loop(0, 2, backward, 0)

    for distance in range(1, count):
        gain_copy(distance).wait_send()
    for d in range(2):
        depth = depth_of(d)

        def layer_drain(l, carry):
            for k in range(KV_HEADS):
                @pl.when(depth < count - 1)
                def _():
                    z_copy(d, l, k).wait_send()

                s_copy(d, l, k).wait_send()
            return carry

        lax.fori_loop(0, depth + 1, layer_drain, 0)
        for k in range(KV_HEADS):
            d_copy(d, k).wait_send()

            @pl.when(depth > 0)
            def _():
                c_copy(d, k).wait_send()

            act_copy(d, lax.rem(depth + 1, 2), k).wait()
            ing_copy(d, k).wait()
            kvg_copy(d, k, 0).wait()
            kvg_copy(d, k, 1).wait()


def per_device(x_a, x_b, grad_a, grad_b, gains, kv_weights, doc_lengths):
    count = lax.axis_size("section")
    shards = lax.axis_size("seq")
    rows, width = x_a.shape
    pair_width = kv_weights.shape[-1]
    tile = width // KV_HEADS
    dma = pltpu.SemaphoreType.DMA
    anywhere = pl.BlockSpec(memory_space=pl.ANY)
    return pl.pallas_call(
        functools.partial(relay_kernel, count, shards),
        in_specs=[pl.BlockSpec(memory_space=pltpu.SMEM)] + [anywhere] * 6,
        out_specs=[anywhere] * 3,
        out_shape=[
            jax.ShapeDtypeStruct((2, 1, rows, width), BF16),
            jax.ShapeDtypeStruct((2, 1, rows, width), BF16),
            jax.ShapeDtypeStruct((2, 1, rows, pair_width), BF16),
        ],
        scratch_shapes=[
            pltpu.VMEM((2, KV_HEADS, width, 2 * HEAD_DIM), BF16),
            pltpu.VMEM((2, 2, KV_HEADS, rows, tile), BF16),
            pltpu.VMEM((2, KV_HEADS, rows, tile), BF16),
            pltpu.VMEM((2, count, KV_HEADS, 2, 2 * rows, HEAD_DIM), BF16),
            pltpu.VMEM((2, KV_HEADS, GROUP, rows, rows), BF16),
            pltpu.VMEM((2, KV_HEADS, rows, tile), BF16),
            pltpu.VMEM((2, KV_HEADS, rows, tile), BF16),
            pltpu.VMEM((KV_HEADS, rows, tile), BF16),
            pltpu.VMEM((KV_HEADS, rows, tile), F32),
            pltpu.VMEM((count, 2, width), F32),
            pltpu.VMEM((2, 2 * rows, rows), F32),
            pltpu.VMEM((2, rows, HEAD_DIM), F32),
            pltpu.VMEM((2, KV_HEADS, 2, rows, HEAD_DIM), BF16),
            pltpu.VMEM((2, KV_HEADS, 2, rows, HEAD_DIM), BF16),
            pltpu.VMEM((KV_HEADS, 2, rows, HEAD_DIM), BF16),
            pltpu.VMEM((2, KV_HEADS, rows, 2 * HEAD_DIM), BF16),
            pltpu.VMEM((4, rows, rows), BF16),
            pltpu.VMEM((2, rows, HEAD_DIM), F32),
            dma((2, KV_HEADS)),
            dma((2, KV_HEADS, 2)),
            dma((2, KV_HEADS)),
            dma(()),
            dma((count - 1,)),
            dma((count - 1,)),
            dma((2, count, KV_HEADS)),
            dma((2, count, KV_HEADS)),
            dma((2, count, KV_HEADS)),
            dma((2, count, KV_HEADS)),
            dma((2, KV_HEADS)),
            dma((2, KV_HEADS)),
            dma((2, KV_HEADS)),
            dma((2, KV_HEADS)),
            dma((2, KV_HEADS)),
            dma((2, KV_HEADS)),
            dma((2, KV_HEADS, 2)),
        ],
        compiler_params=pltpu.CompilerParams(
            collective_id=0, has_side_effects=True, vmem_limit_bytes=60 * 1024 * 1024
        ),
        name="relay",
    )(doc_lengths, x_a, x_b, grad_a, grad_b, gains, kv_weights)


def solution(mesh):
    in_specs = (
        P("seq", None),
        P("seq", None),
        P("seq", None),
        P("seq", None),
        P("section", None, None),
        P("section", None, None, None),
        P(),
    )
    out_specs = (
        P(None, "section", "seq", None),
        P(None, "section", "seq", None),
        P(None, "section", "seq", None),
    )
    return jax.shard_map(
        per_device, mesh=mesh, in_specs=in_specs, out_specs=out_specs, check_vma=False
    )
```

```python
import functools
import math

import jax
import jax.numpy as jnp
from jax import lax
from jax.experimental import pallas as pl
from jax.experimental.pallas import tpu as pltpu
from jax.sharding import PartitionSpec as P

HEADS = 32
HEAD_DIM = 128
KV_HEADS = 4
GROUP = HEADS // KV_HEADS
SCALE = 1.0 / math.sqrt(HEAD_DIM)
LOG2E = math.log2(math.e)
PIECES = 8

epsilon = 1e-05

F32 = jnp.float32
BF16 = jnp.bfloat16
MESH = pl.DeviceIdType.MESH


def dot(a, b, dims):
    return lax.dot_general(a, b, (dims, ((), ())), preferred_element_type=F32)


def relay_kernel(
    count, shards,
    lengths_ref, xa_ref, xb_ref, ga_ref, gb_ref, gains_ref, weights_ref,
    acts_ref, ingrad_ref, kvgrad_ref,
    wbuf, hbuf, nbuf, kv, wsave, cbuf, dqbuf, gnbuf, gbuf, bias, rstd_buf,
    dsend, drecv, downs, dtot, triangle, squares_buf,
    x_sem, w_sem, c_sem, g_sem, gs_sem, gr_sem,
    zs_sem, zr_sem, ss_sem, sr_sem, cs_sem, cr_sem, ds_sem, dr_sem,
    act_sem, ing_sem, kvg_sem,
    bs_sem, ps_sem, pr_sem, ys_sem, yr_sem, es_sem, er_sem,
):
    section = lax.axis_index("section")
    shard = lax.axis_index("seq")
    rows = xa_ref.shape[0]
    width = xa_ref.shape[1]
    tile = width // KV_HEADS
    half = KV_HEADS * HEAD_DIM
    near = lax.div(2 * section, count)
    near_depth = section + near * (count - 1 - 2 * section)
    far = 1 - near
    far_depth = count - 1 - near_depth
    following = lax.rem(shard + 1, shards)
    preceding = lax.rem(shard + shards - 1, shards)
    core = lax.rem(shard, 2)
    side = lax.div(2 * shard, shards)
    sibling = shard + 1 - 2 * core
    opposite = lax.rem(shard + shards // 2, shards)
    extra = 2
    piece = width // PIECES

    def depth_of(d):
        return section + d * (count - 1 - 2 * section)

    def x_copy(d, t):
        ref = (xa_ref, xb_ref)[d]
        return pltpu.make_async_copy(
            ref.at[:, pl.ds(t * tile, tile)], hbuf.at[d, 0, t], x_sem.at[d, t]
        )

    def grad_copy(d, t):
        ref = (ga_ref, gb_ref)[d]
        return pltpu.make_async_copy(
            ref.at[:, pl.ds(t * tile, tile)], cbuf.at[d, t], c_sem.at[d, t]
        )

    def weight_copy(d, k, part):
        return pltpu.make_async_copy(
            weights_ref.at[0, d, :, pl.ds(pl.multiple_of(part * half + k * HEAD_DIM, HEAD_DIM), HEAD_DIM)],
            wbuf.at[d, k, :, pl.ds(part * HEAD_DIM, HEAD_DIM)],
            w_sem.at[d, k, part],
        )

    def gain_copy(distance):
        return pltpu.make_async_remote_copy(
            src_ref=gains_ref.at[0],
            dst_ref=gbuf.at[section],
            send_sem=gs_sem.at[distance - 1],
            recv_sem=gr_sem.at[distance - 1],
            device_id={"section": lax.rem(section + distance, count)},
            device_id_type=MESH,
        )

    def z_copy(d, l, k):
        own = kv.at[d, l, k, :, pl.ds(rows, rows), :]
        return pltpu.make_async_remote_copy(
            src_ref=own, dst_ref=own, send_sem=zs_sem.at[d, l, k], recv_sem=zr_sem.at[d, l, k],
            device_id={"section": section + 1 - 2 * d}, device_id_type=MESH,
        )

    def s_copy(d, l, k):
        return pltpu.make_async_remote_copy(
            src_ref=kv.at[d, l, k, :, pl.ds(rows, rows), :],
            dst_ref=kv.at[d, l, k, :, pl.ds(0, rows), :],
            send_sem=ss_sem.at[d, l, k], recv_sem=sr_sem.at[d, l, k],
            device_id={"seq": following}, device_id_type=MESH,
        )

    def c_copy(d, t, slot):
        return pltpu.make_async_remote_copy(
            src_ref=cbuf.at[slot, t], dst_ref=cbuf.at[d, t],
            send_sem=cs_sem.at[d, t], recv_sem=cr_sem.at[d, t],
            device_id={"section": section - 1 + 2 * d}, device_id_type=MESH,
        )

    def d_copy(slot, k):
        return pltpu.make_async_remote_copy(
            src_ref=dsend.at[slot, k], dst_ref=drecv.at[slot, k],
            send_sem=ds_sem.at[slot, k], recv_sem=dr_sem.at[slot, k],
            device_id={"seq": preceding}, device_id_type=MESH,
        )

    def back_copy(k):
        own = kv.at[near, 1, k, :, pl.ds(rows, rows), :]
        return pltpu.make_async_remote_copy(
            src_ref=own, dst_ref=own, send_sem=bs_sem.at[k], recv_sem=zr_sem.at[near, 1, k],
            device_id={"section": section - 1 + 2 * near}, device_id_type=MESH,
        )

    def piece_of(slot, on_side, on_core, i):
        return wbuf.at[slot, 2 * on_side + on_core, pl.ds(pl.multiple_of(i * piece, piece), piece), :]

    def quarter_copy(i):
        return pltpu.make_async_remote_copy(
            src_ref=piece_of(near, side, core, i), dst_ref=piece_of(extra, side, core, i),
            send_sem=ps_sem.at[i], recv_sem=pr_sem.at[i],
            device_id={"section": section - 1 + 2 * near}, device_id_type=MESH,
        )

    def opposite_copy(i, on_side):
        ref = piece_of(extra, on_side, core, i)
        return pltpu.make_async_remote_copy(
            src_ref=ref, dst_ref=ref, send_sem=ys_sem.at[i], recv_sem=yr_sem.at[i],
            device_id={"seq": opposite}, device_id_type=MESH,
        )

    def sibling_copy(i, part, on_core):
        ref = piece_of(extra, side + part * (1 - 2 * side), on_core, i)
        return pltpu.make_async_remote_copy(
            src_ref=ref, dst_ref=ref, send_sem=es_sem.at[part, i], recv_sem=er_sem.at[part, i],
            device_id={"seq": sibling}, device_id_type=MESH,
        )

    def column_slice(t):
        return pl.ds(pl.multiple_of(t * tile, tile), tile)

    def act_copy(d, parity, t):
        return pltpu.make_async_copy(
            hbuf.at[d, parity, t], acts_ref.at[d, 0, :, column_slice(t)], act_sem.at[d, t]
        )

    def ing_copy(d, t):
        return pltpu.make_async_copy(
            cbuf.at[3 + d, t], ingrad_ref.at[d, 0, :, column_slice(t)], ing_sem.at[d, t]
        )

    def kvg_copy(d, k, part):
        start = pl.multiple_of(part * half + k * HEAD_DIM, HEAD_DIM)
        return pltpu.make_async_copy(
            dtot.at[d, k, :, pl.ds(part * HEAD_DIM, HEAD_DIM)],
            kvgrad_ref.at[d, 0, :, pl.ds(start, HEAD_DIM)],
            kvg_sem.at[d, k, part],
        )

    for t in range(KV_HEADS):
        x_copy(0, t).start()
        x_copy(1, t).start()
    own_gain = pltpu.make_async_copy(gains_ref.at[0], gbuf.at[section], g_sem)
    own_gain.start()
    for d in (near, far):
        for k in range(KV_HEADS):
            for part in range(2):
                weight_copy(d, k, part).start()
    for d, last in ((0, count - 1), (1, 0)):
        @pl.when(section == last)
        def _():
            for t in range(KV_HEADS):
                grad_copy(d, t).start()

    barrier = pltpu.get_barrier_semaphore()
    for neighbour in (following, preceding, opposite):
        pl.semaphore_signal(barrier, inc=1, device_id={"seq": neighbour}, device_id_type=MESH)
    for distance in range(1, count):
        pl.semaphore_signal(
            barrier, inc=1, device_id={"section": lax.rem(section + distance, count)},
            device_id_type=MESH,
        )

    for t in range(KV_HEADS):
        x_copy(0, t).wait()
        x_copy(1, t).wait()
    own_gain.wait()

    def gain_of(home, d, cols):
        return jnp.where(d == 0, gbuf[home, 0:1, cols], gbuf[home, 1:2, cols])

    def normalize(d, l, parity, slot):
        home = l + d * (count - 1 - 2 * l)

        @pl.when(l == 0)
        def _():
            squares = jnp.zeros((rows, HEAD_DIM), F32)
            for t in range(KV_HEADS):
                for g in range(GROUP):
                    part = hbuf[d, parity, t, :, g * HEAD_DIM:(g + 1) * HEAD_DIM].astype(F32)
                    squares = squares + part * part
            squares_buf[d] = squares

        square_mean = jnp.sum(squares_buf[d], axis=-1, keepdims=True) * (1.0 / width)
        rstd = jnp.broadcast_to(lax.rsqrt(square_mean + epsilon), (rows, HEAD_DIM))
        rstd_buf[slot] = rstd
        for t in range(KV_HEADS):
            for g in range(GROUP):
                cols = slice(g * HEAD_DIM, (g + 1) * HEAD_DIM)
                gain = gain_of(home, d, slice(t * tile + g * HEAD_DIM, t * tile + (g + 1) * HEAD_DIM))
                part = hbuf[d, parity, t, :, cols].astype(F32)
                nbuf[slot, t, :, cols] = (part * rstd * gain).astype(BF16)

    def make_masks():
        key_places = (shard - 1) * rows + lax.broadcasted_iota(jnp.int32, (2 * rows, rows), 0)
        places = shard * rows + lax.broadcasted_iota(jnp.int32, (2 * rows, rows), 1)
        for d in range(2):
            end = jnp.int32(0)
            docs_k = jnp.zeros((2 * rows, rows), jnp.int32)
            docs_q = jnp.zeros((2 * rows, rows), jnp.int32)
            for j in range(lengths_ref.shape[1]):
                end = end + lengths_ref[d, j]
                docs_k = docs_k + jnp.where(key_places >= end, 1, 0)
                docs_q = docs_q + jnp.where(places >= end, 1, 0)
            allowed = (docs_k == docs_q) & (key_places <= places) & (key_places >= 0)
            bias[d] = jnp.where(allowed, 0.0, -1e30).astype(F32)
        sublane = lax.broadcasted_iota(jnp.int32, (rows, rows), 0)
        lane = lax.broadcasted_iota(jnp.int32, (rows, rows), 1)
        triangle[0] = jnp.where(sublane > lane, 1.0, 0.0).astype(BF16)
        triangle[1] = jnp.where(sublane <= lane, 1.0, 0.0).astype(BF16)
        triangle[2] = jnp.where(lane > sublane, 1.0, 0.0).astype(BF16)
        triangle[3] = jnp.where(lane <= sublane, 1.0, 0.0).astype(BF16)

    def project(d, depth):
        @pl.when(depth > 0)
        def _():
            normalize(d, depth, lax.rem(depth, 2), d)

        def chunk(k, carry):
            weight_copy(d, k, 0).wait()
            weight_copy(d, k, 1).wait()
            normed = jnp.concatenate([nbuf[d, t] for t in range(KV_HEADS)], axis=1)
            pair = dot(normed, wbuf[d, k], ((1,), (0,))).astype(BF16)
            kv[d, depth, k, 0, rows:, :] = pair[:, :HEAD_DIM]
            kv[d, depth, k, 1, rows:, :] = pair[:, HEAD_DIM:]

            @pl.when(depth < count - 1)
            def _():
                z_copy(d, depth, k).start()

            s_copy(d, depth, k).start()

            @pl.when(depth == 1)
            def _():
                back_copy(k).start()

            return carry

        lax.fori_loop(0, KV_HEADS, chunk, 0)

    def softmax(d, l, k, slot, g):
        both = dot(kv[d, l, k, 0], nbuf[slot, k, :, g * HEAD_DIM:(g + 1) * HEAD_DIM], ((1,), (1,)))
        scores = jnp.maximum(both[:rows] + bias[d, :rows, :], both[rows:] + bias[d, rows:, :])
        powers = jnp.exp2((scores - jnp.max(scores, axis=0, keepdims=True)) * (SCALE * LOG2E))
        weights = (powers * (1.0 / jnp.sum(powers, axis=0, keepdims=True))).astype(BF16)
        wsave[slot, k, g] = weights
        return weights

    def mix(d, l, depth):
        parity = lax.rem(l, 2)

        @pl.when(l < depth)
        def _():
            normalize(d, l, parity, d)

        squares_buf[d] = jnp.zeros((rows, HEAD_DIM), F32)

        def arrive(k):
            @pl.when(l < depth)
            def _():
                z_copy(d, l, k).wait_recv()

                @pl.when(depth < count - 1)
                def _():
                    z_copy(d, l, k).start()

                s_copy(d, l, k).start()

        arrive(0)

        def chunk(k, carry):
            @pl.when(k + 1 < KV_HEADS)
            def _():
                arrive(k + 1)

            s_copy(d, l, k).wait_recv()
            values = kv[d, l, k, 1]
            spreads = []
            for g in range(GROUP):
                weights = softmax(d, l, k, d, g)
                turned = weights.T
                spreads.append(jnp.concatenate([turned * triangle[2], turned * triangle[3]], axis=1))
            for g in range(GROUP):
                cols = slice(g * HEAD_DIM, (g + 1) * HEAD_DIM)
                total = hbuf[d, parity, k, :, cols].astype(F32) + dot(spreads[g], values, ((1,), (0,)))
                hbuf[d, 1 - parity, k, :, cols] = total.astype(BF16)
                squares_buf[d] += total * total

            @pl.when(l == depth)
            def _():
                act_copy(d, 1 - parity, k).start()

            return carry

        lax.fori_loop(0, KV_HEADS, chunk, 0)

    @pl.when(near_depth == 0)
    def _():
        normalize(near, 0, 0, near)

    pl.semaphore_wait(barrier, count + 2)
    for distance in range(1, count):
        gain_copy(distance).start()

    def forward(v, carry):
        p = near_depth
        is_near = (v < p) | (v == 2 * p)
        d = jnp.where(is_near, near, far)
        depth = jnp.where(is_near, near_depth, far_depth)
        l = jnp.where(v < p, v, jnp.where(v < 2 * p, v - p, jnp.where(v == 2 * p, p, v - p - 1)))

        @pl.when((v == p) | (v == count))
        def _():
            pd = jnp.where(v == p, near, far)
            project(pd, jnp.where(v == p, near_depth, far_depth))

            @pl.when((v == count) & (near_depth == 1))
            def _():
                for i in range(PIECES):
                    quarter_copy(i).start()

        @pl.when(v == 0)
        def _():
            for distance in range(1, count):
                gain_copy(distance).wait_recv()
            make_masks()

        mix(d, l, depth)
        return carry

    lax.fori_loop(0, count + 1, forward, 0)

    def prepare():
        d = near

        def pass_quarter(i, carry):
            quarter_copy(i).wait_recv()
            opposite_copy(i, side).start()
            sibling_copy(i, 0, core).start()
            return carry

        def pass_opposite(i, carry):
            opposite_copy(i, 1 - side).wait_recv()
            sibling_copy(i, 1, core).start()
            return carry

        def take_sibling(i, carry):
            sibling_copy(i, 0, 1 - core).wait_recv()
            sibling_copy(i, 1, 1 - core).wait_recv()
            return carry

        for k in range(KV_HEADS):
            back_copy(k).wait_recv()
            s_copy(d, 1, k).start()
        normalize(d, 1, 1, extra)

        def chunk(k, carry):
            s_copy(d, 1, k).wait_recv()
            for g in range(GROUP):
                softmax(d, 1, k, extra, g)
            return carry

        lax.fori_loop(0, KV_HEADS, chunk, 0)
        lax.fori_loop(0, PIECES, pass_quarter, 0)
        lax.fori_loop(0, PIECES, pass_opposite, 0)
        lax.fori_loop(0, PIECES, take_sibling, 0)

    def backward(i, carry):
        @pl.when((i != 1) | (near_depth == 0))
        def _():
            reverse_layer(i)

        return carry

    def reverse_layer(i):
        repeated = i == 1
        local = (i == 2) & (near_depth == 0)
        d = jnp.where(i == 0, far, near)
        depth = jnp.where(i == 0, far_depth, jnp.where(repeated, 1, near_depth))
        slot = jnp.where(repeated, extra, d)
        coming = jnp.where(local, 2, d)
        leaving = jnp.where(repeated, 2, 3 + d)
        first = depth == count - 1
        streamed = (depth < count - 1) & ((i != 2) | (near_depth > 0))
        parity = lax.rem(depth, 2)
        step = 2 * HEAD_DIM

        @pl.when(repeated)
        def _():
            prepare()

        def settle(k):
            d_copy(slot, k).wait_recv()
            for part in range(2):
                total = downs[k, part].astype(F32) + drecv[slot, k, part].astype(F32)
                dtot[slot, k, :, part * HEAD_DIM:(part + 1) * HEAD_DIM] = total.astype(BF16)

                @pl.when(i != 1)
                def _():
                    kvg_copy(d, k, part).start()

        def grad_part(k, t, u):
            start = pl.multiple_of(t * tile + u * step, step)
            return dot(dtot[slot, k], wbuf[slot, k, pl.ds(start, step), :], ((1,), (1,)))

        def finish(k):
            settle(k)

            def part_tile(t, tile_carry):
                for u in range(tile // step):
                    cols = slice(u * step, (u + 1) * step)
                    part = grad_part(k, t, u)
                    gnbuf[t, :, cols] = jnp.where(k == 0, part, part + gnbuf[t, :, cols])
                return tile_carry

            lax.fori_loop(0, KV_HEADS, part_tile, 0)

        def chunk(k, inner_carry):
            @pl.when((k > 0) & streamed)
            def _():
                finish(k - 1)

            @pl.when(streamed)
            def _():
                c_copy(d, k, d).wait_recv()

                @pl.when((depth == 1) & (i != 1))
                def _():
                    c_copy(d, k, d).start()

            @pl.when(first)
            def _():
                pltpu.make_async_copy(cbuf.at[d, k], cbuf.at[d, k], c_sem.at[d, k]).wait()

            keys = kv[d, depth, k, 0]
            values = kv[d, depth, k, 1]
            earlier_s, own_s, earlier_w, own_w, queries, cots, spreads = [], [], [], [], [], [], []
            own_first = lax.broadcasted_iota(jnp.int32, (rows, rows), 0) <= (
                lax.broadcasted_iota(jnp.int32, (rows, rows), 1)
            )
            for g in range(GROUP):
                cols = slice(g * HEAD_DIM, (g + 1) * HEAD_DIM)
                cot = cbuf[coming, k, :, cols]
                both = dot(values, cot, ((1,), (1,)))
                weights = wsave[slot, k, g]
                wide = weights.astype(F32)
                grad_w = jnp.where(own_first, both[rows:], both[:rows]) * wide
                mean = jnp.sum(grad_w, axis=0, keepdims=True)
                grad_s = ((grad_w - wide * mean) * SCALE).astype(BF16)
                earlier_s.append(grad_s * triangle[0])
                own_s.append(grad_s * triangle[1])
                earlier_w.append(weights * triangle[0])
                own_w.append(weights * triangle[1])
                queries.append(nbuf[slot, k, :, cols])
                cots.append(cot)
                turned = grad_s.T
                spreads.append(jnp.concatenate([turned * triangle[2], turned * triangle[3]], axis=1))
            for g in range(GROUP):
                cols = slice(g * HEAD_DIM, (g + 1) * HEAD_DIM)
                dqbuf[k, :, cols] = dot(spreads[g], keys, ((1,), (0,))).astype(BF16)
            all_s = jnp.concatenate(
                [jnp.concatenate(earlier_s, axis=1), jnp.concatenate(own_s, axis=1)], axis=0
            )
            all_w = jnp.concatenate(
                [jnp.concatenate(earlier_w, axis=1), jnp.concatenate(own_w, axis=1)], axis=0
            )
            grad_k = dot(all_s, jnp.concatenate(queries, axis=0), ((1,), (0,)))
            grad_v = dot(all_w, jnp.concatenate(cots, axis=0), ((1,), (0,)))
            dsend[slot, k, 0] = grad_k[:rows].astype(BF16)
            dsend[slot, k, 1] = grad_v[:rows].astype(BF16)
            downs[k, 0] = grad_k[rows:].astype(BF16)
            downs[k, 1] = grad_v[rows:].astype(BF16)
            d_copy(slot, k).start()

            @pl.when((k > 0) & ((i == 2) & (near_depth == 0) | first))
            def _():
                finish(k - 1)

            return inner_carry

        lax.fori_loop(0, KV_HEADS, chunk, 0)
        settle(KV_HEADS - 1)
        home = depth + d * (count - 1 - 2 * depth)
        rstd = rstd_buf[slot]

        def grad_tile(t, inner):
            for u in range(tile // step):
                cols = slice(u * step, (u + 1) * step)
                gain = gain_of(home, d, pl.ds(pl.multiple_of(t * tile + u * step, step), step))
                grad = grad_part(KV_HEADS - 1, t, u) + gnbuf[t, :, cols]
                grad_n = (grad + dqbuf[t, :, cols].astype(F32)) * gain
                gnbuf[t, :, cols] = grad_n
                product = grad_n * hbuf[d, parity, t, :, cols].astype(F32)
                inner = inner + product[:, :HEAD_DIM] + product[:, HEAD_DIM:]
            return inner

        inner = lax.fori_loop(0, KV_HEADS, grad_tile, jnp.zeros((rows, HEAD_DIM), F32))
        inner = jnp.broadcast_to(jnp.sum(inner, axis=-1, keepdims=True), (rows, HEAD_DIM))
        factor = inner * (1.0 / width) * rstd * rstd * rstd

        def total_tile(t, inner_carry):
            for g in range(GROUP):
                cols = slice(g * HEAD_DIM, (g + 1) * HEAD_DIM)
                grad_h = gnbuf[t, :, cols] * rstd - hbuf[d, parity, t, :, cols].astype(F32) * factor
                cbuf[leaving, t, :, cols] = (cbuf[coming, t, :, cols].astype(F32) + grad_h).astype(BF16)

            @pl.when(depth > 1)
            def _():
                c_copy(d, t, 3 + d).start()

            @pl.when(i != 1)
            def _():
                ing_copy(d, t).start()

            return inner_carry

        lax.fori_loop(0, KV_HEADS, total_tile, 0)

    lax.fori_loop(0, 3, backward, 0)

    for distance in range(1, count):
        gain_copy(distance).wait_send()

    @pl.when(near_depth == 1)
    def _():
        for k in range(KV_HEADS):
            back_copy(k).wait_send()
        for i in range(PIECES):
            quarter_copy(i).wait_send()

    @pl.when(near_depth == 0)
    def _():
        for k in range(KV_HEADS):
            s_copy(near, 1, k).wait_send()
            d_copy(extra, k).wait_send()
        for i in range(PIECES):
            opposite_copy(i, side).wait_send()
            sibling_copy(i, 0, core).wait_send()
            sibling_copy(i, 1, core).wait_send()

    for d in range(2):
        depth = depth_of(d)

        def layer_drain(l, carry):
            for k in range(KV_HEADS):
                @pl.when(depth < count - 1)
                def _():
                    z_copy(d, l, k).wait_send()

                s_copy(d, l, k).wait_send()
            return carry

        lax.fori_loop(0, depth + 1, layer_drain, 0)
        for k in range(KV_HEADS):
            d_copy(d, k).wait_send()

            @pl.when(depth > 0)
            def _():
                c_copy(d, k, d).wait_send()

            act_copy(d, lax.rem(depth + 1, 2), k).wait()
            ing_copy(d, k).wait()
            kvg_copy(d, k, 0).wait()
            kvg_copy(d, k, 1).wait()


def per_device(x_a, x_b, grad_a, grad_b, gains, kv_weights, doc_lengths):
    count = lax.axis_size("section")
    shards = lax.axis_size("seq")
    rows, width = x_a.shape
    pair_width = kv_weights.shape[-1]
    tile = width // KV_HEADS
    dma = pltpu.SemaphoreType.DMA
    anywhere = pl.BlockSpec(memory_space=pl.ANY)
    return pl.pallas_call(
        functools.partial(relay_kernel, count, shards),
        in_specs=[pl.BlockSpec(memory_space=pltpu.SMEM)] + [anywhere] * 6,
        out_specs=[anywhere] * 3,
        out_shape=[
            jax.ShapeDtypeStruct((2, 1, rows, width), BF16),
            jax.ShapeDtypeStruct((2, 1, rows, width), BF16),
            jax.ShapeDtypeStruct((2, 1, rows, pair_width), BF16),
        ],
        scratch_shapes=[
            pltpu.VMEM((3, KV_HEADS, width, 2 * HEAD_DIM), BF16),
            pltpu.VMEM((2, 2, KV_HEADS, rows, tile), BF16),
            pltpu.VMEM((3, KV_HEADS, rows, tile), BF16),
            pltpu.VMEM((2, count, KV_HEADS, 2, 2 * rows, HEAD_DIM), BF16),
            pltpu.VMEM((3, KV_HEADS, GROUP, rows, rows), BF16),
            pltpu.VMEM((5, KV_HEADS, rows, tile), BF16),
            pltpu.VMEM((KV_HEADS, rows, tile), BF16),
            pltpu.VMEM((KV_HEADS, rows, tile), F32),
            pltpu.VMEM((count, 2, width), F32),
            pltpu.VMEM((2, 2 * rows, rows), F32),
            pltpu.VMEM((3, rows, HEAD_DIM), F32),
            pltpu.VMEM((3, KV_HEADS, 2, rows, HEAD_DIM), BF16),
            pltpu.VMEM((3, KV_HEADS, 2, rows, HEAD_DIM), BF16),
            pltpu.VMEM((KV_HEADS, 2, rows, HEAD_DIM), BF16),
            pltpu.VMEM((3, KV_HEADS, rows, 2 * HEAD_DIM), BF16),
            pltpu.VMEM((4, rows, rows), BF16),
            pltpu.VMEM((2, rows, HEAD_DIM), F32),
            dma((2, KV_HEADS)),
            dma((2, KV_HEADS, 2)),
            dma((2, KV_HEADS)),
            dma(()),
            dma((count - 1,)),
            dma((count - 1,)),
            dma((2, count, KV_HEADS)),
            dma((2, count, KV_HEADS)),
            dma((2, count, KV_HEADS)),
            dma((2, count, KV_HEADS)),
            dma((2, KV_HEADS)),
            dma((2, KV_HEADS)),
            dma((3, KV_HEADS)),
            dma((3, KV_HEADS)),
            dma((2, KV_HEADS)),
            dma((2, KV_HEADS)),
            dma((2, KV_HEADS, 2)),
            dma((KV_HEADS,)),
            dma((PIECES,)),
            dma((PIECES,)),
            dma((PIECES,)),
            dma((PIECES,)),
            dma((2, PIECES)),
            dma((2, PIECES)),
        ],
        compiler_params=pltpu.CompilerParams(
            collective_id=0, has_side_effects=True, vmem_limit_bytes=60 * 1024 * 1024
        ),
        name="relay",
    )(doc_lengths, x_a, x_b, grad_a, grad_b, gains, kv_weights)


def solution(mesh):
    in_specs = (
        P("seq", None),
        P("seq", None),
        P("seq", None),
        P("seq", None),
        P("section", None, None),
        P("section", None, None, None),
        P(),
    )
    out_specs = (
        P(None, "section", "seq", None),
        P(None, "section", "seq", None),
        P(None, "section", "seq", None),
    )
    return jax.shard_map(
        per_device, mesh=mesh, in_specs=in_specs, out_specs=out_specs, check_vma=False
    )
```

```python
import functools
import math

import jax
import jax.numpy as jnp
from jax import lax
from jax.experimental import pallas as pl
from jax.experimental.pallas import tpu as pltpu
from jax.sharding import PartitionSpec as P

HEADS = 32
HEAD_DIM = 128
KV_HEADS = 4
GROUP = HEADS // KV_HEADS
SCALE = 1.0 / math.sqrt(HEAD_DIM)
LOG2E = math.log2(math.e)
PIECES = 8

epsilon = 1e-05

F32 = jnp.float32
BF16 = jnp.bfloat16
MESH = pl.DeviceIdType.MESH


def dot(a, b, dims):
    return lax.dot_general(a, b, (dims, ((), ())), preferred_element_type=F32)


def relay_kernel(
    count, shards,
    lengths_ref, xa_ref, xb_ref, ga_ref, gb_ref, gains_ref, weights_ref,
    acts_ref, ingrad_ref, kvgrad_ref,
    wbuf, hbuf, nbuf, kv, wsave, cbuf, dqbuf, gnbuf, gbuf, bias, rstd_buf,
    dsend, drecv, downs, dtot, triangle, squares_buf,
    x_sem, w_sem, c_sem, g_sem, gs_sem, gr_sem,
    zs_sem, zr_sem, ss_sem, sr_sem, cs_sem, cr_sem, ds_sem, dr_sem,
    act_sem, ing_sem, kvg_sem,
    bs_sem, ps_sem, pr_sem, ys_sem, yr_sem, es_sem, er_sem,
):
    section = lax.axis_index("section")
    shard = lax.axis_index("seq")
    rows = xa_ref.shape[0]
    width = xa_ref.shape[1]
    tile = width // KV_HEADS
    half = KV_HEADS * HEAD_DIM
    near = lax.div(2 * section, count)
    near_depth = section + near * (count - 1 - 2 * section)
    far = 1 - near
    far_depth = count - 1 - near_depth
    following = lax.rem(shard + 1, shards)
    preceding = lax.rem(shard + shards - 1, shards)
    core = lax.rem(shard, 2)
    side = lax.div(2 * shard, shards)
    sibling = shard + 1 - 2 * core
    opposite = lax.rem(shard + shards // 2, shards)
    extra = 2
    piece = width // PIECES

    def depth_of(d):
        return section + d * (count - 1 - 2 * section)

    def x_copy(d, t):
        ref = (xa_ref, xb_ref)[d]
        return pltpu.make_async_copy(
            ref.at[:, pl.ds(t * tile, tile)], hbuf.at[d, 0, t], x_sem.at[d, t]
        )

    def grad_copy(d, t):
        ref = (ga_ref, gb_ref)[d]
        return pltpu.make_async_copy(
            ref.at[:, pl.ds(t * tile, tile)], cbuf.at[d, t], c_sem.at[d, t]
        )

    def weight_copy(d, k, part):
        return pltpu.make_async_copy(
            weights_ref.at[0, d, :, pl.ds(pl.multiple_of(part * half + k * HEAD_DIM, HEAD_DIM), HEAD_DIM)],
            wbuf.at[d, k, :, pl.ds(part * HEAD_DIM, HEAD_DIM)],
            w_sem.at[d, k, part],
        )

    def gain_copy(distance):
        return pltpu.make_async_remote_copy(
            src_ref=gains_ref.at[0],
            dst_ref=gbuf.at[section],
            send_sem=gs_sem.at[distance - 1],
            recv_sem=gr_sem.at[distance - 1],
            device_id={"section": lax.rem(section + distance, count)},
            device_id_type=MESH,
        )

    def z_copy(d, l, k):
        own = kv.at[d, l, k, :, pl.ds(rows, rows), :]
        return pltpu.make_async_remote_copy(
            src_ref=own, dst_ref=own, send_sem=zs_sem.at[d, l, k], recv_sem=zr_sem.at[d, l, k],
            device_id={"section": section + 1 - 2 * d}, device_id_type=MESH,
        )

    def s_copy(d, l, k):
        return pltpu.make_async_remote_copy(
            src_ref=kv.at[d, l, k, :, pl.ds(rows, rows), :],
            dst_ref=kv.at[d, l, k, :, pl.ds(0, rows), :],
            send_sem=ss_sem.at[d, l, k], recv_sem=sr_sem.at[d, l, k],
            device_id={"seq": following}, device_id_type=MESH,
        )

    def c_copy(d, t, slot):
        return pltpu.make_async_remote_copy(
            src_ref=cbuf.at[slot, t], dst_ref=cbuf.at[d, t],
            send_sem=cs_sem.at[d, t], recv_sem=cr_sem.at[d, t],
            device_id={"section": section - 1 + 2 * d}, device_id_type=MESH,
        )

    def d_copy(slot, k):
        return pltpu.make_async_remote_copy(
            src_ref=dsend.at[slot, k], dst_ref=drecv.at[slot, k],
            send_sem=ds_sem.at[slot, k], recv_sem=dr_sem.at[slot, k],
            device_id={"seq": preceding}, device_id_type=MESH,
        )

    def back_copy(k):
        own = kv.at[near, 1, k, :, pl.ds(rows, rows), :]
        return pltpu.make_async_remote_copy(
            src_ref=own, dst_ref=own, send_sem=bs_sem.at[k], recv_sem=zr_sem.at[near, 1, k],
            device_id={"section": section - 1 + 2 * near}, device_id_type=MESH,
        )

    def piece_of(slot, on_side, on_core, i):
        return wbuf.at[slot, 2 * on_side + on_core, pl.ds(pl.multiple_of(i * piece, piece), piece), :]

    def quarter_copy(i):
        return pltpu.make_async_remote_copy(
            src_ref=piece_of(near, side, core, i), dst_ref=piece_of(extra, side, core, i),
            send_sem=ps_sem.at[i], recv_sem=pr_sem.at[i],
            device_id={"section": section - 1 + 2 * near}, device_id_type=MESH,
        )

    def opposite_copy(i, on_side):
        ref = piece_of(extra, on_side, core, i)
        return pltpu.make_async_remote_copy(
            src_ref=ref, dst_ref=ref, send_sem=ys_sem.at[i], recv_sem=yr_sem.at[i],
            device_id={"seq": opposite}, device_id_type=MESH,
        )

    def sibling_copy(i, part, on_core):
        ref = piece_of(extra, side + part * (1 - 2 * side), on_core, i)
        return pltpu.make_async_remote_copy(
            src_ref=ref, dst_ref=ref, send_sem=es_sem.at[part, i], recv_sem=er_sem.at[part, i],
            device_id={"seq": sibling}, device_id_type=MESH,
        )

    def column_slice(t):
        return pl.ds(pl.multiple_of(t * tile, tile), tile)

    def act_copy(d, parity, t):
        return pltpu.make_async_copy(
            hbuf.at[d, parity, t], acts_ref.at[d, 0, :, column_slice(t)], act_sem.at[d, t]
        )

    def ing_copy(d, t):
        return pltpu.make_async_copy(
            cbuf.at[3 + d, t], ingrad_ref.at[d, 0, :, column_slice(t)], ing_sem.at[d, t]
        )

    def kvg_copy(d, k, part):
        start = pl.multiple_of(part * half + k * HEAD_DIM, HEAD_DIM)
        return pltpu.make_async_copy(
            dtot.at[d, k, :, pl.ds(part * HEAD_DIM, HEAD_DIM)],
            kvgrad_ref.at[d, 0, :, pl.ds(start, HEAD_DIM)],
            kvg_sem.at[d, k, part],
        )

    for t in range(KV_HEADS):
        x_copy(0, t).start()
        x_copy(1, t).start()
    own_gain = pltpu.make_async_copy(gains_ref.at[0], gbuf.at[section], g_sem)
    own_gain.start()
    for part in range(2):
        weight_copy(near, 0, part).start()

    barrier = pltpu.get_barrier_semaphore()
    for neighbour in (following, preceding, opposite):
        pl.semaphore_signal(barrier, inc=1, device_id={"seq": neighbour}, device_id_type=MESH)
    for distance in range(1, count):
        pl.semaphore_signal(
            barrier, inc=1, device_id={"section": lax.rem(section + distance, count)},
            device_id_type=MESH,
        )

    for t in range(KV_HEADS):
        x_copy(0, t).wait()
        x_copy(1, t).wait()
    own_gain.wait()
    for d, start in ((near, 1), (far, 0)):
        for k in range(start, KV_HEADS):
            for part in range(2):
                weight_copy(d, k, part).start()
    for d, last in ((0, count - 1), (1, 0)):
        @pl.when(section == last)
        def _():
            for t in range(KV_HEADS):
                grad_copy(d, t).start()

    def gain_of(home, d, cols):
        return jnp.where(d == 0, gbuf[home, 0:1, cols], gbuf[home, 1:2, cols])

    def normalize(d, l, parity, slot):
        home = l + d * (count - 1 - 2 * l)

        @pl.when(l == 0)
        def _():
            squares = jnp.zeros((rows, HEAD_DIM), F32)
            for t in range(KV_HEADS):
                for g in range(GROUP):
                    part = hbuf[d, parity, t, :, g * HEAD_DIM:(g + 1) * HEAD_DIM].astype(F32)
                    squares = squares + part * part
            squares_buf[d] = squares

        square_mean = jnp.sum(squares_buf[d], axis=-1, keepdims=True) * (1.0 / width)
        rstd = jnp.broadcast_to(lax.rsqrt(square_mean + epsilon), (rows, HEAD_DIM))
        rstd_buf[slot] = rstd
        for t in range(KV_HEADS):
            for g in range(GROUP):
                cols = slice(g * HEAD_DIM, (g + 1) * HEAD_DIM)
                gain = gain_of(home, d, slice(t * tile + g * HEAD_DIM, t * tile + (g + 1) * HEAD_DIM))
                part = hbuf[d, parity, t, :, cols].astype(F32)
                nbuf[slot, t, :, cols] = (part * rstd * gain).astype(BF16)

    def make_masks():
        key_places = (shard - 1) * rows + lax.broadcasted_iota(jnp.int32, (2 * rows, rows), 0)
        places = shard * rows + lax.broadcasted_iota(jnp.int32, (2 * rows, rows), 1)
        for d in range(2):
            end = jnp.int32(0)
            docs_k = jnp.zeros((2 * rows, rows), jnp.int32)
            docs_q = jnp.zeros((2 * rows, rows), jnp.int32)
            for j in range(lengths_ref.shape[1]):
                end = end + lengths_ref[d, j]
                docs_k = docs_k + jnp.where(key_places >= end, 1, 0)
                docs_q = docs_q + jnp.where(places >= end, 1, 0)
            allowed = (docs_k == docs_q) & (key_places <= places) & (key_places >= 0)
            bias[d] = jnp.where(allowed, 0.0, -1e30).astype(F32)
        sublane = lax.broadcasted_iota(jnp.int32, (rows, rows), 0)
        lane = lax.broadcasted_iota(jnp.int32, (rows, rows), 1)
        triangle[0] = jnp.where(sublane > lane, 1.0, 0.0).astype(BF16)
        triangle[1] = jnp.where(sublane <= lane, 1.0, 0.0).astype(BF16)
        triangle[2] = jnp.where(lane > sublane, 1.0, 0.0).astype(BF16)
        triangle[3] = jnp.where(lane <= sublane, 1.0, 0.0).astype(BF16)

    middle = (near_depth == far_depth - 1) & (near_depth > 0)

    def arrive(d, l, depth, k):
        z_copy(d, l, k).wait_recv()
        s_copy(d, l, k).start()

        @pl.when(depth < count - 1)
        def _():
            z_copy(d, l, k).start()

    def project(d, depth):
        @pl.when(depth > 0)
        def _():
            normalize(d, depth, lax.rem(depth, 2), d)

        def chunk(k, carry):
            weight_copy(d, k, 0).wait()
            weight_copy(d, k, 1).wait()
            normed = jnp.concatenate([nbuf[d, t] for t in range(KV_HEADS)], axis=1)
            pair = dot(normed, wbuf[d, k], ((1,), (0,))).astype(BF16)
            kv[d, depth, k, 0, rows:, :] = pair[:, :HEAD_DIM]
            kv[d, depth, k, 1, rows:, :] = pair[:, HEAD_DIM:]

            @pl.when(depth < count - 1)
            def _():
                z_copy(d, depth, k).start()

            @pl.when(jnp.logical_not(middle & (depth == near_depth)))
            def _():
                s_copy(d, depth, k).start()

            @pl.when(middle & (depth == near_depth))
            def _():
                arrive(far, 0, far_depth, k)

            return carry

        lax.fori_loop(0, KV_HEADS, chunk, 0)

    def softmax(d, l, k, slot, g):
        both = dot(kv[d, l, k, 0], nbuf[slot, k, :, g * HEAD_DIM:(g + 1) * HEAD_DIM], ((1,), (1,)))
        scores = jnp.maximum(both[:rows] + bias[d, :rows, :], both[rows:] + bias[d, rows:, :])
        powers = jnp.exp2((scores - jnp.max(scores, axis=0, keepdims=True)) * (SCALE * LOG2E))
        weights = (powers * (1.0 / jnp.sum(powers, axis=0, keepdims=True))).astype(BF16)
        wsave[slot, k, g] = weights
        return weights

    def mix(d, l, depth):
        parity = lax.rem(l, 2)

        @pl.when(l < depth)
        def _():
            home = l + d * (count - 1 - 2 * l)
            gain_copy(lax.rem(section - home + count, count)).wait_recv()
            normalize(d, l, parity, d)

        squares_buf[d] = jnp.zeros((rows, HEAD_DIM), F32)

        coming = (l < depth) & ((l > 0) | (d == near) | jnp.logical_not(middle))

        @pl.when(coming)
        def _():
            arrive(d, l, depth, 0)

        def chunk(k, carry):
            @pl.when((k + 1 < KV_HEADS) & coming)
            def _():
                arrive(d, l, depth, k + 1)

            s_copy(d, l, k).wait_recv()
            values = kv[d, l, k, 1]
            spreads = []
            for g in range(GROUP):
                weights = softmax(d, l, k, d, g)
                turned = weights.T
                spreads.append(jnp.concatenate([turned * triangle[2], turned * triangle[3]], axis=1))
            for g in range(GROUP):
                cols = slice(g * HEAD_DIM, (g + 1) * HEAD_DIM)
                total = hbuf[d, parity, k, :, cols].astype(F32) + dot(spreads[g], values, ((1,), (0,)))
                hbuf[d, 1 - parity, k, :, cols] = total.astype(BF16)
                squares_buf[d] += total * total

            @pl.when(l == depth)
            def _():
                act_copy(d, 1 - parity, k).start()

            return carry

        lax.fori_loop(0, KV_HEADS, chunk, 0)

    @pl.when(near_depth == 0)
    def _():
        normalize(near, 0, 0, near)

    pl.semaphore_wait(barrier, count + 2)
    for distance in range(1, count):
        gain_copy(distance).start()

    def forward(v, carry):
        p = near_depth
        is_near = (v < p) | (v == jnp.where(p == 0, 0, count))
        d = jnp.where(is_near, near, far)
        depth = jnp.where(is_near, near_depth, far_depth)
        l = jnp.where(is_near, jnp.where(v < p, v, p), jnp.where(p == 0, v - 1, v - p))
        far_turn = jnp.where(p == 0, count, count - 1)

        @pl.when((v == p) | (v == far_turn))
        def _():
            pd = jnp.where(v == p, near, far)
            project(pd, jnp.where(v == p, near_depth, far_depth))

            @pl.when((v == far_turn) & middle)
            def _():
                for k in range(KV_HEADS):
                    s_copy(near, near_depth, k).start()

            @pl.when((v == far_turn) & (near_depth == 1))
            def _():
                for k in range(KV_HEADS):
                    back_copy(k).start()
                for i in range(PIECES):
                    quarter_copy(i).start()

        @pl.when(v == 0)
        def _():
            make_masks()

        mix(d, l, depth)
        return carry

    lax.fori_loop(0, count + 1, forward, 0)

    def drain_forward():
        for distance in range(1, count):
            gain_copy(distance).wait_send()
        for d in range(2):
            depth = depth_of(d)

            def layer_drain(l, carry):
                for k in range(KV_HEADS):
                    @pl.when(depth < count - 1)
                    def _():
                        z_copy(d, l, k).wait_send()

                    s_copy(d, l, k).wait_send()
                return carry

            lax.fori_loop(0, depth + 1, layer_drain, 0)
            for k in range(KV_HEADS):
                act_copy(d, lax.rem(depth + 1, 2), k).wait()

    def drain_reverse(d, depth):
        for k in range(KV_HEADS):
            d_copy(d, k).wait_send()

            @pl.when(depth > 0)
            def _():
                c_copy(d, k, d).wait_send()

            ing_copy(d, k).wait()
            kvg_copy(d, k, 0).wait()
            kvg_copy(d, k, 1).wait()

    def pass_opposite(i, carry):
        opposite_copy(i, 1 - side).wait_recv()
        sibling_copy(i, 1, core).start()
        return carry

    def take_sibling(i, carry):
        sibling_copy(i, 0, 1 - core).wait_recv()
        sibling_copy(i, 1, 1 - core).wait_recv()
        return carry

    def prepare():
        d = near

        def pass_quarter(i, carry):
            quarter_copy(i).wait_recv()
            opposite_copy(i, side).start()
            sibling_copy(i, 0, core).start()
            return carry

        for k in range(KV_HEADS):
            back_copy(k).wait_recv()
            s_copy(d, 1, k).start()
        normalize(d, 1, 1, extra)

        def chunk(k, carry):
            s_copy(d, 1, k).wait_recv()
            for g in range(GROUP):
                softmax(d, 1, k, extra, g)
            return carry

        lax.fori_loop(0, KV_HEADS, chunk, 0)
        lax.fori_loop(0, PIECES, pass_quarter, 0)
        drain_forward()
        drain_reverse(far, far_depth)

    def backward(i, carry):
        @pl.when((i != 1) | (near_depth == 0))
        def _():
            reverse_layer(i)

        return carry

    def reverse_layer(i):
        repeated = i == 1
        local = (i == 2) & (near_depth == 0)
        d = jnp.where(i == 0, far, near)
        depth = jnp.where(i == 0, far_depth, jnp.where(repeated, 1, near_depth))
        slot = jnp.where(repeated, extra, d)
        coming = jnp.where(local, 2, d)
        leaving = jnp.where(repeated, 2, 3 + d)
        first = depth == count - 1
        streamed = (depth < count - 1) & ((i != 2) | (near_depth > 0))
        added = streamed & (i != 1)
        parity = lax.rem(depth, 2)
        step = 2 * HEAD_DIM

        @pl.when(repeated)
        def _():
            prepare()

        def settle(k):
            d_copy(slot, k).wait_recv()
            for part in range(2):
                total = downs[k, part].astype(F32) + drecv[slot, k, part].astype(F32)
                dtot[slot, k, :, part * HEAD_DIM:(part + 1) * HEAD_DIM] = total.astype(BF16)

                @pl.when(i != 1)
                def _():
                    kvg_copy(d, k, part).start()

        def grad_part(k, t, u):
            start = pl.multiple_of(t * tile + u * step, step)
            return dot(dtot[slot, k], wbuf[slot, k, pl.ds(start, step), :], ((1,), (1,)))

        def finish(k):
            settle(k)

            def part_tile(t, tile_carry):
                for u in range(tile // step):
                    cols = slice(u * step, (u + 1) * step)
                    part = grad_part(k, t, u)
                    gnbuf[t, :, cols] = jnp.where(k == 0, part, part + gnbuf[t, :, cols])
                return tile_carry

            lax.fori_loop(0, KV_HEADS, part_tile, 0)

        def chunk(k, inner_carry):
            @pl.when((k > 0) & added)
            def _():
                finish(k - 1)

            @pl.when(streamed)
            def _():
                c_copy(d, k, d).wait_recv()

                @pl.when((depth == 1) & (i != 1))
                def _():
                    c_copy(d, k, d).start()

            @pl.when(first)
            def _():
                pltpu.make_async_copy(cbuf.at[d, k], cbuf.at[d, k], c_sem.at[d, k]).wait()

            keys = kv[d, depth, k, 0]
            values = kv[d, depth, k, 1]
            earlier_s, own_s, earlier_w, own_w, queries, cots, spreads = [], [], [], [], [], [], []
            own_first = lax.broadcasted_iota(jnp.int32, (rows, rows), 0) <= (
                lax.broadcasted_iota(jnp.int32, (rows, rows), 1)
            )
            for g in range(GROUP):
                cols = slice(g * HEAD_DIM, (g + 1) * HEAD_DIM)
                cot = cbuf[coming, k, :, cols]
                both = dot(values, cot, ((1,), (1,)))
                weights = wsave[slot, k, g]
                wide = weights.astype(F32)
                grad_w = jnp.where(own_first, both[rows:], both[:rows]) * wide
                mean = jnp.sum(grad_w, axis=0, keepdims=True)
                grad_s = ((grad_w - wide * mean) * SCALE).astype(BF16)
                earlier_s.append(grad_s * triangle[0])
                own_s.append(grad_s * triangle[1])
                earlier_w.append(weights * triangle[0])
                own_w.append(weights * triangle[1])
                queries.append(nbuf[slot, k, :, cols])
                cots.append(cot)
                turned = grad_s.T
                spreads.append(jnp.concatenate([turned * triangle[2], turned * triangle[3]], axis=1))
            for g in range(GROUP):
                cols = slice(g * HEAD_DIM, (g + 1) * HEAD_DIM)
                dqbuf[k, :, cols] = dot(spreads[g], keys, ((1,), (0,))).astype(BF16)
            all_s = jnp.concatenate(
                [jnp.concatenate(earlier_s, axis=1), jnp.concatenate(own_s, axis=1)], axis=0
            )
            all_w = jnp.concatenate(
                [jnp.concatenate(earlier_w, axis=1), jnp.concatenate(own_w, axis=1)], axis=0
            )
            grad_k = dot(all_s, jnp.concatenate(queries, axis=0), ((1,), (0,)))
            grad_v = dot(all_w, jnp.concatenate(cots, axis=0), ((1,), (0,)))
            dsend[slot, k, 0] = grad_k[:rows].astype(BF16)
            dsend[slot, k, 1] = grad_v[:rows].astype(BF16)
            downs[k, 0] = grad_k[rows:].astype(BF16)
            downs[k, 1] = grad_v[rows:].astype(BF16)
            d_copy(slot, k).start()

            @pl.when(repeated & (k > 0) & (k < 3))
            def _():
                lax.fori_loop((k - 1) * (PIECES // 2), k * (PIECES // 2), pass_opposite, 0)

            return inner_carry

        lax.fori_loop(0, KV_HEADS, chunk, 0)

        @pl.when(repeated)
        def _():
            lax.fori_loop(0, PIECES, take_sibling, 0)

        @pl.when(jnp.logical_not(added))
        def _():
            for heads in (range(2), range(2, KV_HEADS - 1)):
                for k in heads:
                    settle(k)

                def base_tile(t, tile_carry):
                    for u in range(tile // step):
                        start = pl.multiple_of(t * tile + u * step, step)
                        cols = slice(u * step, (u + 1) * step)
                        pairs = jnp.concatenate([dtot[slot, k] for k in heads], axis=1)
                        weights = jnp.concatenate(
                            [wbuf[slot, k, pl.ds(start, step), :] for k in heads], axis=1
                        )
                        part = dot(pairs, weights, ((1,), (1,)))
                        gnbuf[t, :, cols] = part if heads[0] == 0 else part + gnbuf[t, :, cols]
                    return tile_carry

                lax.fori_loop(0, KV_HEADS, base_tile, 0)

        settle(KV_HEADS - 1)
        home = depth + d * (count - 1 - 2 * depth)
        rstd = rstd_buf[slot]

        def grad_tile(t, inner):
            for u in range(tile // step):
                cols = slice(u * step, (u + 1) * step)
                gain = gain_of(home, d, pl.ds(pl.multiple_of(t * tile + u * step, step), step))
                grad = grad_part(KV_HEADS - 1, t, u) + gnbuf[t, :, cols]
                grad_n = (grad + dqbuf[t, :, cols].astype(F32)) * gain
                gnbuf[t, :, cols] = grad_n
                product = grad_n * hbuf[d, parity, t, :, cols].astype(F32)
                inner = inner + product[:, :HEAD_DIM] + product[:, HEAD_DIM:]
            return inner

        inner = lax.fori_loop(0, KV_HEADS, grad_tile, jnp.zeros((rows, HEAD_DIM), F32))
        inner = jnp.broadcast_to(jnp.sum(inner, axis=-1, keepdims=True), (rows, HEAD_DIM))
        factor = inner * (1.0 / width) * rstd * rstd * rstd

        def total_tile(t, inner_carry):
            for g in range(GROUP):
                cols = slice(g * HEAD_DIM, (g + 1) * HEAD_DIM)
                grad_h = gnbuf[t, :, cols] * rstd - hbuf[d, parity, t, :, cols].astype(F32) * factor
                cbuf[leaving, t, :, cols] = (cbuf[coming, t, :, cols].astype(F32) + grad_h).astype(BF16)

            @pl.when(depth > 1)
            def _():
                c_copy(d, t, 3 + d).start()

            @pl.when(i != 1)
            def _():
                ing_copy(d, t).start()

            return inner_carry

        lax.fori_loop(0, KV_HEADS, total_tile, 0)

    lax.fori_loop(0, 3, backward, 0)

    @pl.when(near_depth == 1)
    def _():
        for k in range(KV_HEADS):
            back_copy(k).wait_send()
        for i in range(PIECES):
            quarter_copy(i).wait_send()

    @pl.when(near_depth == 0)
    def _():
        for k in range(KV_HEADS):
            s_copy(near, 1, k).wait_send()
            d_copy(extra, k).wait_send()
        for i in range(PIECES):
            opposite_copy(i, side).wait_send()
            sibling_copy(i, 0, core).wait_send()
            sibling_copy(i, 1, core).wait_send()

    @pl.when(near_depth > 0)
    def _():
        drain_forward()
        drain_reverse(far, far_depth)

    drain_reverse(near, near_depth)


def per_device(x_a, x_b, grad_a, grad_b, gains, kv_weights, doc_lengths):
    count = lax.axis_size("section")
    shards = lax.axis_size("seq")
    rows, width = x_a.shape
    pair_width = kv_weights.shape[-1]
    tile = width // KV_HEADS
    dma = pltpu.SemaphoreType.DMA
    anywhere = pl.BlockSpec(memory_space=pl.ANY)
    return pl.pallas_call(
        functools.partial(relay_kernel, count, shards),
        in_specs=[pl.BlockSpec(memory_space=pltpu.SMEM)] + [anywhere] * 6,
        out_specs=[anywhere] * 3,
        out_shape=[
            jax.ShapeDtypeStruct((2, 1, rows, width), BF16),
            jax.ShapeDtypeStruct((2, 1, rows, width), BF16),
            jax.ShapeDtypeStruct((2, 1, rows, pair_width), BF16),
        ],
        scratch_shapes=[
            pltpu.VMEM((3, KV_HEADS, width, 2 * HEAD_DIM), BF16),
            pltpu.VMEM((2, 2, KV_HEADS, rows, tile), BF16),
            pltpu.VMEM((3, KV_HEADS, rows, tile), BF16),
            pltpu.VMEM((2, count, KV_HEADS, 2, 2 * rows, HEAD_DIM), BF16),
            pltpu.VMEM((3, KV_HEADS, GROUP, rows, rows), BF16),
            pltpu.VMEM((5, KV_HEADS, rows, tile), BF16),
            pltpu.VMEM((KV_HEADS, rows, tile), BF16),
            pltpu.VMEM((KV_HEADS, rows, tile), F32),
            pltpu.VMEM((count, 2, width), F32),
            pltpu.VMEM((2, 2 * rows, rows), F32),
            pltpu.VMEM((3, rows, HEAD_DIM), F32),
            pltpu.VMEM((3, KV_HEADS, 2, rows, HEAD_DIM), BF16),
            pltpu.VMEM((3, KV_HEADS, 2, rows, HEAD_DIM), BF16),
            pltpu.VMEM((KV_HEADS, 2, rows, HEAD_DIM), BF16),
            pltpu.VMEM((3, KV_HEADS, rows, 2 * HEAD_DIM), BF16),
            pltpu.VMEM((4, rows, rows), BF16),
            pltpu.VMEM((2, rows, HEAD_DIM), F32),
            dma((2, KV_HEADS)),
            dma((2, KV_HEADS, 2)),
            dma((2, KV_HEADS)),
            dma(()),
            dma((count - 1,)),
            dma((count - 1,)),
            dma((2, count, KV_HEADS)),
            dma((2, count, KV_HEADS)),
            dma((2, count, KV_HEADS)),
            dma((2, count, KV_HEADS)),
            dma((2, KV_HEADS)),
            dma((2, KV_HEADS)),
            dma((3, KV_HEADS)),
            dma((3, KV_HEADS)),
            dma((2, KV_HEADS)),
            dma((2, KV_HEADS)),
            dma((2, KV_HEADS, 2)),
            dma((KV_HEADS,)),
            dma((PIECES,)),
            dma((PIECES,)),
            dma((PIECES,)),
            dma((PIECES,)),
            dma((2, PIECES)),
            dma((2, PIECES)),
        ],
        compiler_params=pltpu.CompilerParams(
            collective_id=0, has_side_effects=True, vmem_limit_bytes=60 * 1024 * 1024
        ),
        name="relay",
    )(doc_lengths, x_a, x_b, grad_a, grad_b, gains, kv_weights)


def solution(mesh):
    in_specs = (
        P("seq", None),
        P("seq", None),
        P("seq", None),
        P("seq", None),
        P("section", None, None),
        P("section", None, None, None),
        P(),
    )
    out_specs = (
        P(None, "section", "seq", None),
        P(None, "section", "seq", None),
        P(None, "section", "seq", None),
    )
    return jax.shard_map(
        per_device, mesh=mesh, in_specs=in_specs, out_specs=out_specs, check_vma=False
    )
```

```python
import functools
import math

import jax
import jax.numpy as jnp
from jax import lax
from jax.experimental import pallas as pl
from jax.experimental.pallas import tpu as pltpu
from jax.sharding import PartitionSpec as P

HEADS = 32
HEAD_DIM = 128
KV_HEADS = 4
GROUP = HEADS // KV_HEADS
SCALE = 1.0 / math.sqrt(HEAD_DIM)
LOG2E = math.log2(math.e)
PIECES = 8

epsilon = 1e-05

F32 = jnp.float32
BF16 = jnp.bfloat16
MESH = pl.DeviceIdType.MESH


def dot(a, b, dims):
    return lax.dot_general(a, b, (dims, ((), ())), preferred_element_type=F32)


def relay_kernel(
    count, shards,
    lengths_ref, xa_ref, xb_ref, ga_ref, gb_ref, gains_ref, weights_ref,
    acts_ref, ingrad_ref, kvgrad_ref,
    wbuf, hbuf, nbuf, kv, wsave, cbuf, dqbuf, gnbuf, gbuf, bias, rstd_buf,
    dsend, drecv, downs, dtot, triangle, squares_buf,
    x_sem, w_sem, c_sem, g_sem, gs_sem, gr_sem,
    zs_sem, zr_sem, ss_sem, sr_sem, cs_sem, cr_sem, ds_sem, dr_sem,
    act_sem, ing_sem, kvg_sem,
    bs_sem, ps_sem, pr_sem, ys_sem, yr_sem, es_sem, er_sem,
):
    section = lax.axis_index("section")
    shard = lax.axis_index("seq")
    rows = xa_ref.shape[0]
    width = xa_ref.shape[1]
    tile = width // KV_HEADS
    half = KV_HEADS * HEAD_DIM
    near = lax.div(2 * section, count)
    near_depth = section + near * (count - 1 - 2 * section)
    far = 1 - near
    far_depth = count - 1 - near_depth
    following = lax.rem(shard + 1, shards)
    preceding = lax.rem(shard + shards - 1, shards)
    core = lax.rem(shard, 2)
    side = lax.div(2 * shard, shards)
    sibling = shard + 1 - 2 * core
    opposite = lax.rem(shard + shards // 2, shards)
    extra = 2
    piece = width // PIECES

    def depth_of(d):
        return section + d * (count - 1 - 2 * section)

    def x_copy(d, t):
        ref = (xa_ref, xb_ref)[d]
        return pltpu.make_async_copy(
            ref.at[:, pl.ds(t * tile, tile)], hbuf.at[d, 0, t], x_sem.at[d, t]
        )

    def grad_copy(d, t):
        ref = (ga_ref, gb_ref)[d]
        return pltpu.make_async_copy(
            ref.at[:, pl.ds(t * tile, tile)], cbuf.at[d, t], c_sem.at[d, t]
        )

    def weight_copy(d, k, part):
        return pltpu.make_async_copy(
            weights_ref.at[0, d, :, pl.ds(pl.multiple_of(part * half + k * HEAD_DIM, HEAD_DIM), HEAD_DIM)],
            wbuf.at[d, k, :, pl.ds(part * HEAD_DIM, HEAD_DIM)],
            w_sem.at[d, k, part],
        )

    def gain_copy(distance):
        return pltpu.make_async_remote_copy(
            src_ref=gains_ref.at[0],
            dst_ref=gbuf.at[section],
            send_sem=gs_sem.at[distance - 1],
            recv_sem=gr_sem.at[distance - 1],
            device_id={"section": lax.rem(section + distance, count)},
            device_id_type=MESH,
        )

    def z_copy(d, l, k):
        own = kv.at[d, l, k, :, pl.ds(rows, rows), :]
        return pltpu.make_async_remote_copy(
            src_ref=own, dst_ref=own, send_sem=zs_sem.at[d, l, k], recv_sem=zr_sem.at[d, l, k],
            device_id={"section": section + 1 - 2 * d}, device_id_type=MESH,
        )

    def s_copy(d, l, k):
        return pltpu.make_async_remote_copy(
            src_ref=kv.at[d, l, k, :, pl.ds(rows, rows), :],
            dst_ref=kv.at[d, l, k, :, pl.ds(0, rows), :],
            send_sem=ss_sem.at[d, l, k], recv_sem=sr_sem.at[d, l, k],
            device_id={"seq": following}, device_id_type=MESH,
        )

    def c_copy(d, t, slot, part):
        lines = pl.ds(part * (rows // 2), rows // 2)
        return pltpu.make_async_remote_copy(
            src_ref=cbuf.at[slot, t, lines, :], dst_ref=cbuf.at[d, t, lines, :],
            send_sem=cs_sem.at[d, t, part], recv_sem=cr_sem.at[d, t, part],
            device_id={"section": section - 1 + 2 * d}, device_id_type=MESH,
        )

    def d_copy(slot, k):
        return pltpu.make_async_remote_copy(
            src_ref=dsend.at[slot, k], dst_ref=drecv.at[slot, k],
            send_sem=ds_sem.at[slot, k], recv_sem=dr_sem.at[slot, k],
            device_id={"seq": preceding}, device_id_type=MESH,
        )

    def back_copy(k):
        own = kv.at[near, 1, k, :, pl.ds(rows, rows), :]
        return pltpu.make_async_remote_copy(
            src_ref=own, dst_ref=own, send_sem=bs_sem.at[k], recv_sem=zr_sem.at[near, 1, k],
            device_id={"section": section - 1 + 2 * near}, device_id_type=MESH,
        )

    def piece_of(slot, on_side, on_core, i):
        return wbuf.at[slot, 2 * on_side + on_core, pl.ds(pl.multiple_of(i * piece, piece), piece), :]

    def quarter_copy(i):
        return pltpu.make_async_remote_copy(
            src_ref=piece_of(near, side, core, i), dst_ref=piece_of(extra, side, core, i),
            send_sem=ps_sem.at[i], recv_sem=pr_sem.at[i],
            device_id={"section": section - 1 + 2 * near}, device_id_type=MESH,
        )

    def opposite_copy(i, on_side):
        ref = piece_of(extra, on_side, core, i)
        return pltpu.make_async_remote_copy(
            src_ref=ref, dst_ref=ref, send_sem=ys_sem.at[i], recv_sem=yr_sem.at[i],
            device_id={"seq": opposite}, device_id_type=MESH,
        )

    def sibling_copy(i, part, on_core):
        ref = piece_of(extra, side + part * (1 - 2 * side), on_core, i)
        return pltpu.make_async_remote_copy(
            src_ref=ref, dst_ref=ref, send_sem=es_sem.at[part, i], recv_sem=er_sem.at[part, i],
            device_id={"seq": sibling}, device_id_type=MESH,
        )

    def column_slice(t):
        return pl.ds(pl.multiple_of(t * tile, tile), tile)

    def act_copy(d, parity, t):
        return pltpu.make_async_copy(
            hbuf.at[d, parity, t], acts_ref.at[d, 0, :, column_slice(t)], act_sem.at[d, t]
        )

    def ing_copy(d, t):
        return pltpu.make_async_copy(
            cbuf.at[3 + d, t], ingrad_ref.at[d, 0, :, column_slice(t)], ing_sem.at[d, t]
        )

    def kvg_copy(d, k, part):
        start = pl.multiple_of(part * half + k * HEAD_DIM, HEAD_DIM)
        return pltpu.make_async_copy(
            dtot.at[d, k, :, pl.ds(part * HEAD_DIM, HEAD_DIM)],
            kvgrad_ref.at[d, 0, :, pl.ds(start, HEAD_DIM)],
            kvg_sem.at[d, k, part],
        )

    for t in range(KV_HEADS):
        x_copy(0, t).start()
        x_copy(1, t).start()
    own_gain = pltpu.make_async_copy(gains_ref.at[0], gbuf.at[section], g_sem)
    own_gain.start()
    for part in range(2):
        weight_copy(near, 0, part).start()

    barrier = pltpu.get_barrier_semaphore()
    for neighbour in (following, preceding, opposite):
        pl.semaphore_signal(barrier, inc=1, device_id={"seq": neighbour}, device_id_type=MESH)
    for distance in range(1, count):
        pl.semaphore_signal(
            barrier, inc=1, device_id={"section": lax.rem(section + distance, count)},
            device_id_type=MESH,
        )

    for t in range(KV_HEADS):
        x_copy(0, t).wait()
        x_copy(1, t).wait()
    own_gain.wait()
    for d, start in ((near, 1), (far, 0)):
        for k in range(start, KV_HEADS):
            for part in range(2):
                weight_copy(d, k, part).start()
    for d, last in ((0, count - 1), (1, 0)):
        @pl.when(section == last)
        def _():
            for t in range(KV_HEADS):
                grad_copy(d, t).start()

    def gain_of(home, d, cols):
        return jnp.where(d == 0, gbuf[home, 0:1, cols], gbuf[home, 1:2, cols])

    def normalize(d, l, parity, slot):
        home = l + d * (count - 1 - 2 * l)

        @pl.when(l == 0)
        def _():
            squares = jnp.zeros((rows, HEAD_DIM), F32)
            for t in range(KV_HEADS):
                for g in range(GROUP):
                    part = hbuf[d, parity, t, :, g * HEAD_DIM:(g + 1) * HEAD_DIM].astype(F32)
                    squares = squares + part * part
            squares_buf[d] = squares

        square_mean = jnp.sum(squares_buf[d], axis=-1, keepdims=True) * (1.0 / width)
        rstd = jnp.broadcast_to(lax.rsqrt(square_mean + epsilon), (rows, HEAD_DIM))
        rstd_buf[slot] = rstd
        for t in range(KV_HEADS):
            for g in range(GROUP):
                cols = slice(g * HEAD_DIM, (g + 1) * HEAD_DIM)
                gain = gain_of(home, d, slice(t * tile + g * HEAD_DIM, t * tile + (g + 1) * HEAD_DIM))
                part = hbuf[d, parity, t, :, cols].astype(F32)
                nbuf[slot, t, :, cols] = (part * rstd * gain).astype(BF16)

    def make_masks():
        key_places = (shard - 1) * rows + lax.broadcasted_iota(jnp.int32, (2 * rows, rows), 0)
        places = shard * rows + lax.broadcasted_iota(jnp.int32, (2 * rows, rows), 1)
        for d in range(2):
            end = jnp.int32(0)
            docs_k = jnp.zeros((2 * rows, rows), jnp.int32)
            docs_q = jnp.zeros((2 * rows, rows), jnp.int32)
            for j in range(lengths_ref.shape[1]):
                end = end + lengths_ref[d, j]
                docs_k = docs_k + jnp.where(key_places >= end, 1, 0)
                docs_q = docs_q + jnp.where(places >= end, 1, 0)
            allowed = (docs_k == docs_q) & (key_places <= places) & (key_places >= 0)
            bias[d] = jnp.where(allowed, 0.0, -1e30).astype(F32)
        sublane = lax.broadcasted_iota(jnp.int32, (rows, rows), 0)
        lane = lax.broadcasted_iota(jnp.int32, (rows, rows), 1)
        triangle[0] = jnp.where(sublane > lane, 1.0, 0.0).astype(BF16)
        triangle[1] = jnp.where(sublane <= lane, 1.0, 0.0).astype(BF16)
        triangle[2] = jnp.where(lane > sublane, 1.0, 0.0).astype(BF16)
        triangle[3] = jnp.where(lane <= sublane, 1.0, 0.0).astype(BF16)

    middle = (near_depth == far_depth - 1) & (near_depth > 0)

    def arrive(d, l, depth, k):
        z_copy(d, l, k).wait_recv()
        s_copy(d, l, k).start()

        @pl.when(depth < count - 1)
        def _():
            z_copy(d, l, k).start()

    def project(d, depth):
        @pl.when(depth > 0)
        def _():
            normalize(d, depth, lax.rem(depth, 2), d)

        def chunk(k, carry):
            weight_copy(d, k, 0).wait()
            weight_copy(d, k, 1).wait()
            normed = jnp.concatenate([nbuf[d, t] for t in range(KV_HEADS)], axis=1)
            pair = dot(normed, wbuf[d, k], ((1,), (0,))).astype(BF16)
            kv[d, depth, k, 0, rows:, :] = pair[:, :HEAD_DIM]
            kv[d, depth, k, 1, rows:, :] = pair[:, HEAD_DIM:]

            @pl.when(depth < count - 1)
            def _():
                z_copy(d, depth, k).start()

            @pl.when(jnp.logical_not(middle & (depth == near_depth)))
            def _():
                s_copy(d, depth, k).start()

            @pl.when(middle & (depth == near_depth))
            def _():
                arrive(far, 0, far_depth, k)

            return carry

        lax.fori_loop(0, KV_HEADS, chunk, 0)

    def softmax(d, l, k, slot, g):
        both = dot(kv[d, l, k, 0], nbuf[slot, k, :, g * HEAD_DIM:(g + 1) * HEAD_DIM], ((1,), (1,)))
        scores = jnp.maximum(both[:rows] + bias[d, :rows, :], both[rows:] + bias[d, rows:, :])
        powers = jnp.exp2((scores - jnp.max(scores, axis=0, keepdims=True)) * (SCALE * LOG2E))
        weights = (powers * (1.0 / jnp.sum(powers, axis=0, keepdims=True))).astype(BF16)
        wsave[slot, k, g] = weights
        return weights

    def mix(d, l, depth):
        parity = lax.rem(l, 2)

        @pl.when(l < depth)
        def _():
            home = l + d * (count - 1 - 2 * l)
            gain_copy(lax.rem(section - home + count, count)).wait_recv()
            normalize(d, l, parity, d)

        squares_buf[d] = jnp.zeros((rows, HEAD_DIM), F32)

        coming = (l < depth) & ((d == near) | ((l == 0) & jnp.logical_not(middle)))
        ahead = (d == far) & (l + 1 < far_depth)

        @pl.when(coming)
        def _():
            arrive(d, l, depth, 0)

        def chunk(k, carry):
            @pl.when((k + 1 < KV_HEADS) & coming)
            def _():
                arrive(d, l, depth, k + 1)

            s_copy(d, l, k).wait_recv()
            values = kv[d, l, k, 1]
            spreads = []
            for g in range(GROUP):
                weights = softmax(d, l, k, d, g)
                turned = weights.T
                spreads.append(jnp.concatenate([turned * triangle[2], turned * triangle[3]], axis=1))
            for g in range(GROUP):
                cols = slice(g * HEAD_DIM, (g + 1) * HEAD_DIM)
                total = hbuf[d, parity, k, :, cols].astype(F32) + dot(spreads[g], values, ((1,), (0,)))
                hbuf[d, 1 - parity, k, :, cols] = total.astype(BF16)
                squares_buf[d] += total * total

            @pl.when(l == depth)
            def _():
                act_copy(d, 1 - parity, k).start()

            @pl.when(ahead)
            def _():
                arrive(far, l + 1, far_depth, k)

            return carry

        lax.fori_loop(0, KV_HEADS, chunk, 0)

    @pl.when(near_depth == 0)
    def _():
        normalize(near, 0, 0, near)

    pl.semaphore_wait(barrier, count + 2)
    closest = lax.rem(1 - 2 * near + count, count)
    gain_copy(closest).start()

    def forward(v, carry):
        p = near_depth
        is_near = (v < p) | (v == jnp.where(p == 0, 0, count))
        d = jnp.where(is_near, near, far)
        depth = jnp.where(is_near, near_depth, far_depth)
        l = jnp.where(is_near, jnp.where(v < p, v, p), jnp.where(p == 0, v - 1, v - p))
        far_turn = jnp.where(p == 0, count, count - 1)

        @pl.when((v == p) | (v == far_turn))
        def _():
            pd = jnp.where(v == p, near, far)
            project(pd, jnp.where(v == p, near_depth, far_depth))

            @pl.when((v == far_turn) & middle)
            def _():
                for k in range(KV_HEADS):
                    s_copy(near, near_depth, k).start()

            @pl.when((v == far_turn) & (near_depth == 1))
            def _():
                for k in range(KV_HEADS):
                    back_copy(k).start()
                for i in range(PIECES):
                    quarter_copy(i).start()

        @pl.when(v == 0)
        def _():
            for further in range(1, count - 1):
                gain_copy(1 + lax.rem(closest - 1 + further, count - 1)).start()
            make_masks()

        mix(d, l, depth)
        return carry

    lax.fori_loop(0, count + 1, forward, 0)

    def drain_forward():
        for distance in range(1, count):
            gain_copy(distance).wait_send()
        for d in range(2):
            depth = depth_of(d)

            def layer_drain(l, carry):
                for k in range(KV_HEADS):
                    @pl.when(depth < count - 1)
                    def _():
                        z_copy(d, l, k).wait_send()

                    s_copy(d, l, k).wait_send()
                return carry

            lax.fori_loop(0, depth + 1, layer_drain, 0)
            for k in range(KV_HEADS):
                act_copy(d, lax.rem(depth + 1, 2), k).wait()

    def drain_reverse(d, depth):
        for k in range(KV_HEADS):
            d_copy(d, k).wait_send()

            @pl.when(depth > 0)
            def _():
                for part in range(2):
                    c_copy(d, k, d, part).wait_send()

            ing_copy(d, k).wait()
            kvg_copy(d, k, 0).wait()
            kvg_copy(d, k, 1).wait()

    def pass_opposite(i, carry):
        opposite_copy(i, 1 - side).wait_recv()
        sibling_copy(i, 1, core).start()
        return carry

    def take_sibling(i, carry):
        sibling_copy(i, 0, 1 - core).wait_recv()
        sibling_copy(i, 1, 1 - core).wait_recv()
        return carry

    def prepare():
        d = near

        def pass_quarter(i, carry):
            quarter_copy(i).wait_recv()
            opposite_copy(i, side).start()
            sibling_copy(i, 0, core).start()
            return carry

        for k in range(KV_HEADS):
            back_copy(k).wait_recv()
            s_copy(d, 1, k).start()
        normalize(d, 1, 1, extra)

        def chunk(k, carry):
            s_copy(d, 1, k).wait_recv()
            for g in range(GROUP):
                softmax(d, 1, k, extra, g)
            return carry

        lax.fori_loop(0, KV_HEADS, chunk, 0)
        lax.fori_loop(0, PIECES, pass_quarter, 0)
        drain_forward()
        drain_reverse(far, far_depth)

    def backward(i, carry):
        @pl.when((i != 1) | (near_depth == 0))
        def _():
            reverse_layer(i)

        return carry

    def reverse_layer(i):
        repeated = i == 1
        local = (i == 2) & (near_depth == 0)
        d = jnp.where(i == 0, far, near)
        depth = jnp.where(i == 0, far_depth, jnp.where(repeated, 1, near_depth))
        slot = jnp.where(repeated, extra, d)
        coming = jnp.where(local, 2, d)
        leaving = jnp.where(repeated, 2, 3 + d)
        first = depth == count - 1
        streamed = (depth < count - 1) & ((i != 2) | (near_depth > 0))
        added = streamed & (i != 1)
        parity = lax.rem(depth, 2)
        step = 2 * HEAD_DIM

        @pl.when(repeated)
        def _():
            prepare()

        def settle(k):
            d_copy(slot, k).wait_recv()
            for part in range(2):
                total = downs[k, part].astype(F32) + drecv[slot, k, part].astype(F32)
                dtot[slot, k, :, part * HEAD_DIM:(part + 1) * HEAD_DIM] = total.astype(BF16)

                @pl.when(i != 1)
                def _():
                    kvg_copy(d, k, part).start()

        def grad_part(k, t, u):
            start = pl.multiple_of(t * tile + u * step, step)
            return dot(dtot[slot, k], wbuf[slot, k, pl.ds(start, step), :], ((1,), (1,)))

        def finish(k):
            settle(k)

            def part_tile(t, tile_carry):
                for u in range(tile // step):
                    cols = slice(u * step, (u + 1) * step)
                    part = grad_part(k, t, u)
                    gnbuf[t, :, cols] = jnp.where(k == 0, part, part + gnbuf[t, :, cols])
                return tile_carry

            lax.fori_loop(0, KV_HEADS, part_tile, 0)

        def chunk(k, inner_carry):
            @pl.when(streamed)
            def _():
                for part in range(2):
                    c_copy(d, k, d, part).wait_recv()

                    @pl.when((depth == 1) & (i != 1))
                    def _():
                        c_copy(d, k, d, part).start()

            @pl.when(first)
            def _():
                pltpu.make_async_copy(cbuf.at[d, k], cbuf.at[d, k], c_sem.at[d, k]).wait()

            keys = kv[d, depth, k, 0]
            values = kv[d, depth, k, 1]
            earlier_s, own_s, earlier_w, own_w, queries, cots, spreads = [], [], [], [], [], [], []
            own_first = lax.broadcasted_iota(jnp.int32, (rows, rows), 0) <= (
                lax.broadcasted_iota(jnp.int32, (rows, rows), 1)
            )
            for g in range(GROUP):
                cols = slice(g * HEAD_DIM, (g + 1) * HEAD_DIM)
                cot = cbuf[coming, k, :, cols]
                both = dot(values, cot, ((1,), (1,)))
                weights = wsave[slot, k, g]
                wide = weights.astype(F32)
                grad_w = jnp.where(own_first, both[rows:], both[:rows]) * wide
                mean = jnp.sum(grad_w, axis=0, keepdims=True)
                grad_s = ((grad_w - wide * mean) * SCALE).astype(BF16)
                earlier_s.append(grad_s * triangle[0])
                own_s.append(grad_s * triangle[1])
                earlier_w.append(weights * triangle[0])
                own_w.append(weights * triangle[1])
                queries.append(nbuf[slot, k, :, cols])
                cots.append(cot)
                turned = grad_s.T
                spreads.append(jnp.concatenate([turned * triangle[2], turned * triangle[3]], axis=1))
            for g in range(GROUP):
                cols = slice(g * HEAD_DIM, (g + 1) * HEAD_DIM)
                dqbuf[k, :, cols] = dot(spreads[g], keys, ((1,), (0,))).astype(BF16)
            all_s = jnp.concatenate(
                [jnp.concatenate(earlier_s, axis=1), jnp.concatenate(own_s, axis=1)], axis=0
            )
            all_w = jnp.concatenate(
                [jnp.concatenate(earlier_w, axis=1), jnp.concatenate(own_w, axis=1)], axis=0
            )
            grad_k = dot(all_s, jnp.concatenate(queries, axis=0), ((1,), (0,)))
            grad_v = dot(all_w, jnp.concatenate(cots, axis=0), ((1,), (0,)))
            dsend[slot, k, 0] = grad_k[:rows].astype(BF16)
            dsend[slot, k, 1] = grad_v[:rows].astype(BF16)
            downs[k, 0] = grad_k[rows:].astype(BF16)
            downs[k, 1] = grad_v[rows:].astype(BF16)
            d_copy(slot, k).start()

            @pl.when((k > 0) & added)
            def _():
                finish(k - 1)

            @pl.when(repeated & (k > 0) & (k < 3))
            def _():
                lax.fori_loop((k - 1) * (PIECES // 2), k * (PIECES // 2), pass_opposite, 0)

            return inner_carry

        lax.fori_loop(0, KV_HEADS, chunk, 0)

        @pl.when(repeated)
        def _():
            lax.fori_loop(0, PIECES, take_sibling, 0)

        @pl.when(jnp.logical_not(added))
        def _():
            for heads in (range(2), range(2, KV_HEADS - 1)):
                for k in heads:
                    settle(k)

                def base_tile(t, tile_carry):
                    for u in range(tile // step):
                        start = pl.multiple_of(t * tile + u * step, step)
                        cols = slice(u * step, (u + 1) * step)
                        pairs = jnp.concatenate([dtot[slot, k] for k in heads], axis=1)
                        weights = jnp.concatenate(
                            [wbuf[slot, k, pl.ds(start, step), :] for k in heads], axis=1
                        )
                        part = dot(pairs, weights, ((1,), (1,)))
                        gnbuf[t, :, cols] = part if heads[0] == 0 else part + gnbuf[t, :, cols]
                    return tile_carry

                lax.fori_loop(0, KV_HEADS, base_tile, 0)

        settle(KV_HEADS - 1)
        home = depth + d * (count - 1 - 2 * depth)
        rstd = rstd_buf[slot]

        def grad_tile(t, inner):
            for u in range(tile // step):
                cols = slice(u * step, (u + 1) * step)
                gain = gain_of(home, d, pl.ds(pl.multiple_of(t * tile + u * step, step), step))
                grad = grad_part(KV_HEADS - 1, t, u) + gnbuf[t, :, cols]
                grad_n = (grad + dqbuf[t, :, cols].astype(F32)) * gain
                gnbuf[t, :, cols] = grad_n
                product = grad_n * hbuf[d, parity, t, :, cols].astype(F32)
                inner = inner + product[:, :HEAD_DIM] + product[:, HEAD_DIM:]
            return inner

        inner = lax.fori_loop(0, KV_HEADS, grad_tile, jnp.zeros((rows, HEAD_DIM), F32))
        inner = jnp.broadcast_to(jnp.sum(inner, axis=-1, keepdims=True), (rows, HEAD_DIM))
        factor = inner * (1.0 / width) * rstd * rstd * rstd

        def total_tile(t, inner_carry):
            for g in range(GROUP):
                cols = slice(g * HEAD_DIM, (g + 1) * HEAD_DIM)
                grad_h = gnbuf[t, :, cols] * rstd - hbuf[d, parity, t, :, cols].astype(F32) * factor
                cbuf[leaving, t, :, cols] = (cbuf[coming, t, :, cols].astype(F32) + grad_h).astype(BF16)

            @pl.when(depth > 1)
            def _():
                for part in range(2):
                    c_copy(d, t, 3 + d, part).start()

            @pl.when(i != 1)
            def _():
                ing_copy(d, t).start()

            return inner_carry

        lax.fori_loop(0, KV_HEADS, total_tile, 0)

    lax.fori_loop(0, 3, backward, 0)

    @pl.when(near_depth == 1)
    def _():
        for k in range(KV_HEADS):
            back_copy(k).wait_send()
        for i in range(PIECES):
            quarter_copy(i).wait_send()

    @pl.when(near_depth == 0)
    def _():
        for k in range(KV_HEADS):
            s_copy(near, 1, k).wait_send()
            d_copy(extra, k).wait_send()
        for i in range(PIECES):
            opposite_copy(i, side).wait_send()
            sibling_copy(i, 0, core).wait_send()
            sibling_copy(i, 1, core).wait_send()

    @pl.when(near_depth > 0)
    def _():
        drain_forward()
        drain_reverse(far, far_depth)

    drain_reverse(near, near_depth)


def hand_over_kernel(acts_ref, ingrad_ref, kvgrad_ref, acts_out, ingrad_out, kvgrad_out, wide, narrow, in_sem, out_sem):
    lines = acts_ref.shape[2] // 2
    moves = []
    for d in range(2):
        for part in range(2):
            block = (d, 0, pl.ds(part * lines, lines))
            for a, (source, target) in enumerate(((acts_ref, acts_out), (ingrad_ref, ingrad_out))):
                moves.append((source.at[block], wide.at[a, d, part], target.at[block]))
        moves.append((kvgrad_ref.at[d, 0], narrow.at[d], kvgrad_out.at[d, 0]))
    inward = [pltpu.make_async_copy(m[0], m[1], in_sem.at[i]) for i, m in enumerate(moves)]
    outward = [pltpu.make_async_copy(m[1], m[2], out_sem.at[i]) for i, m in enumerate(moves)]
    for copy in inward:
        copy.start()
    for taken, given in zip(inward, outward):
        taken.wait()
        given.start()
    for copy in outward:
        copy.wait()


def hand_over(acts, ingrads, kvgrads):
    rows, width = acts.shape[2:]
    anywhere = pl.BlockSpec(memory_space=pl.ANY)
    return pl.pallas_call(
        hand_over_kernel,
        in_specs=[anywhere] * 3,
        out_specs=[anywhere] * 3,
        out_shape=[jax.ShapeDtypeStruct(a.shape, a.dtype) for a in (acts, ingrads, kvgrads)],
        scratch_shapes=[
            pltpu.VMEM((2, 2, 2, rows // 2, width), BF16),
            pltpu.VMEM((2, rows, kvgrads.shape[3]), BF16),
            pltpu.SemaphoreType.DMA((10,)),
            pltpu.SemaphoreType.DMA((10,)),
        ],
        compiler_params=pltpu.CompilerParams(vmem_limit_bytes=60 * 1024 * 1024),
        name="hand_over",
    )(acts, ingrads, kvgrads)


def per_device(x_a, x_b, grad_a, grad_b, gains, kv_weights, doc_lengths):
    count = lax.axis_size("section")
    shards = lax.axis_size("seq")
    rows, width = x_a.shape
    pair_width = kv_weights.shape[-1]
    tile = width // KV_HEADS
    dma = pltpu.SemaphoreType.DMA
    anywhere = pl.BlockSpec(memory_space=pl.ANY)
    results = pl.pallas_call(
        functools.partial(relay_kernel, count, shards),
        in_specs=[pl.BlockSpec(memory_space=pltpu.SMEM)] + [anywhere] * 6,
        out_specs=[anywhere] * 3,
        out_shape=[
            jax.ShapeDtypeStruct((2, 1, rows, width), BF16),
            jax.ShapeDtypeStruct((2, 1, rows, width), BF16),
            jax.ShapeDtypeStruct((2, 1, rows, pair_width), BF16),
        ],
        scratch_shapes=[
            pltpu.VMEM((3, KV_HEADS, width, 2 * HEAD_DIM), BF16),
            pltpu.VMEM((2, 2, KV_HEADS, rows, tile), BF16),
            pltpu.VMEM((3, KV_HEADS, rows, tile), BF16),
            pltpu.VMEM((2, count, KV_HEADS, 2, 2 * rows, HEAD_DIM), BF16),
            pltpu.VMEM((3, KV_HEADS, GROUP, rows, rows), BF16),
            pltpu.VMEM((5, KV_HEADS, rows, tile), BF16),
            pltpu.VMEM((KV_HEADS, rows, tile), BF16),
            pltpu.VMEM((KV_HEADS, rows, tile), F32),
            pltpu.VMEM((count, 2, width), F32),
            pltpu.VMEM((2, 2 * rows, rows), F32),
            pltpu.VMEM((3, rows, HEAD_DIM), F32),
            pltpu.VMEM((3, KV_HEADS, 2, rows, HEAD_DIM), BF16),
            pltpu.VMEM((3, KV_HEADS, 2, rows, HEAD_DIM), BF16),
            pltpu.VMEM((KV_HEADS, 2, rows, HEAD_DIM), BF16),
            pltpu.VMEM((3, KV_HEADS, rows, 2 * HEAD_DIM), BF16),
            pltpu.VMEM((4, rows, rows), BF16),
            pltpu.VMEM((2, rows, HEAD_DIM), F32),
            dma((2, KV_HEADS)),
            dma((2, KV_HEADS, 2)),
            dma((2, KV_HEADS)),
            dma(()),
            dma((count - 1,)),
            dma((count - 1,)),
            dma((2, count, KV_HEADS)),
            dma((2, count, KV_HEADS)),
            dma((2, count, KV_HEADS)),
            dma((2, count, KV_HEADS)),
            dma((2, KV_HEADS, 2)),
            dma((2, KV_HEADS, 2)),
            dma((3, KV_HEADS)),
            dma((3, KV_HEADS)),
            dma((2, KV_HEADS)),
            dma((2, KV_HEADS)),
            dma((2, KV_HEADS, 2)),
            dma((KV_HEADS,)),
            dma((PIECES,)),
            dma((PIECES,)),
            dma((PIECES,)),
            dma((PIECES,)),
            dma((2, PIECES)),
            dma((2, PIECES)),
        ],
        compiler_params=pltpu.CompilerParams(
            collective_id=0, has_side_effects=True, vmem_limit_bytes=60 * 1024 * 1024
        ),
        name="relay",
    )(doc_lengths, x_a, x_b, grad_a, grad_b, gains, kv_weights)
    return hand_over(*results)


def solution(mesh):
    in_specs = (
        P("seq", None),
        P("seq", None),
        P("seq", None),
        P("seq", None),
        P("section", None, None),
        P("section", None, None, None),
        P(),
    )
    out_specs = (
        P(None, "section", "seq", None),
        P(None, "section", "seq", None),
        P(None, "section", "seq", None),
    )
    return jax.shard_map(
        per_device, mesh=mesh, in_specs=in_specs, out_specs=out_specs, check_vma=False
    )
```

```python
import functools
import math

import jax
import jax.numpy as jnp
from jax import lax
from jax.experimental import pallas as pl
from jax.experimental.pallas import tpu as pltpu
from jax.sharding import PartitionSpec as P

HEADS = 32
HEAD_DIM = 128
KV_HEADS = 4
GROUP = HEADS // KV_HEADS
SCALE = 1.0 / math.sqrt(HEAD_DIM)
LOG2E = math.log2(math.e)
PIECES = 8
PARTS = 4

epsilon = 1e-05

F32 = jnp.float32
BF16 = jnp.bfloat16
MESH = pl.DeviceIdType.MESH


def dot(a, b, dims):
    return lax.dot_general(a, b, (dims, ((), ())), preferred_element_type=F32)


def relay_kernel(
    count, shards,
    lengths_ref, xa_ref, xb_ref, ga_ref, gb_ref, gains_ref, weights_ref,
    acts_ref, ingrad_ref, kvgrad_ref,
    wbuf, hbuf, nbuf, kv, wsave, cbuf, dqbuf, gnbuf, gbuf, bias, rstd_buf,
    dsend, drecv, downs, dtot, triangle, squares_buf, inner_buf,
    x_sem, w_sem, c_sem, g_sem, gs_sem, gr_sem,
    zs_sem, zr_sem, ss_sem, sr_sem, cs_sem, cr_sem, ds_sem, dr_sem,
    act_sem, ing_sem, kvg_sem,
    bs_sem, ps_sem, pr_sem, ys_sem, yr_sem, es_sem, er_sem,
):
    section = lax.axis_index("section")
    shard = lax.axis_index("seq")
    rows = xa_ref.shape[0]
    width = xa_ref.shape[1]
    tile = width // KV_HEADS
    half = KV_HEADS * HEAD_DIM
    near = lax.div(2 * section, count)
    near_depth = section + near * (count - 1 - 2 * section)
    far = 1 - near
    far_depth = count - 1 - near_depth
    following = lax.rem(shard + 1, shards)
    preceding = lax.rem(shard + shards - 1, shards)
    core = lax.rem(shard, 2)
    side = lax.div(2 * shard, shards)
    sibling = shard + 1 - 2 * core
    opposite = lax.rem(shard + shards // 2, shards)
    extra = 2
    piece = width // PIECES

    def depth_of(d):
        return section + d * (count - 1 - 2 * section)

    def x_copy(d, t):
        ref = (xa_ref, xb_ref)[d]
        return pltpu.make_async_copy(
            ref.at[:, pl.ds(t * tile, tile)], hbuf.at[d, 0, t], x_sem.at[d, t]
        )

    def grad_copy(d, t):
        ref = (ga_ref, gb_ref)[d]
        return pltpu.make_async_copy(
            ref.at[:, pl.ds(t * tile, tile)], cbuf.at[d, t], c_sem.at[d, t]
        )

    def weight_copy(d, k, part):
        return pltpu.make_async_copy(
            weights_ref.at[0, d, :, pl.ds(pl.multiple_of(part * half + k * HEAD_DIM, HEAD_DIM), HEAD_DIM)],
            wbuf.at[d, k, :, pl.ds(part * HEAD_DIM, HEAD_DIM)],
            w_sem.at[d, k, part],
        )

    def gain_copy(distance):
        return pltpu.make_async_remote_copy(
            src_ref=gains_ref.at[0],
            dst_ref=gbuf.at[section],
            send_sem=gs_sem.at[distance - 1],
            recv_sem=gr_sem.at[distance - 1],
            device_id={"section": lax.rem(section + distance, count)},
            device_id_type=MESH,
        )

    def z_copy(d, l, k):
        own = kv.at[d, l, k, :, pl.ds(rows, rows), :]
        return pltpu.make_async_remote_copy(
            src_ref=own, dst_ref=own, send_sem=zs_sem.at[d, l, k], recv_sem=zr_sem.at[d, l, k],
            device_id={"section": section + 1 - 2 * d}, device_id_type=MESH,
        )

    def s_copy(d, l, k):
        return pltpu.make_async_remote_copy(
            src_ref=kv.at[d, l, k, :, pl.ds(rows, rows), :],
            dst_ref=kv.at[d, l, k, :, pl.ds(0, rows), :],
            send_sem=ss_sem.at[d, l, k], recv_sem=sr_sem.at[d, l, k],
            device_id={"seq": following}, device_id_type=MESH,
        )

    def c_copy(d, t, slot, part):
        lines = pl.ds(part * (rows // PARTS), rows // PARTS)
        return pltpu.make_async_remote_copy(
            src_ref=cbuf.at[slot, t, lines, :], dst_ref=cbuf.at[d, t, lines, :],
            send_sem=cs_sem.at[d, t, part], recv_sem=cr_sem.at[d, t, part],
            device_id={"section": section - 1 + 2 * d}, device_id_type=MESH,
        )

    def d_copy(slot, k):
        return pltpu.make_async_remote_copy(
            src_ref=dsend.at[slot, k], dst_ref=drecv.at[slot, k],
            send_sem=ds_sem.at[slot, k], recv_sem=dr_sem.at[slot, k],
            device_id={"seq": preceding}, device_id_type=MESH,
        )

    def back_copy(k):
        own = kv.at[near, 1, k, :, pl.ds(rows, rows), :]
        return pltpu.make_async_remote_copy(
            src_ref=own, dst_ref=own, send_sem=bs_sem.at[k], recv_sem=zr_sem.at[near, 1, k],
            device_id={"section": section - 1 + 2 * near}, device_id_type=MESH,
        )

    def piece_of(slot, on_side, on_core, i):
        return wbuf.at[slot, 2 * on_side + on_core, pl.ds(pl.multiple_of(i * piece, piece), piece), :]

    def quarter_copy(i):
        return pltpu.make_async_remote_copy(
            src_ref=piece_of(near, side, core, i), dst_ref=piece_of(extra, side, core, i),
            send_sem=ps_sem.at[i], recv_sem=pr_sem.at[i],
            device_id={"section": section - 1 + 2 * near}, device_id_type=MESH,
        )

    def opposite_copy(i, on_side):
        ref = piece_of(extra, on_side, core, i)
        return pltpu.make_async_remote_copy(
            src_ref=ref, dst_ref=ref, send_sem=ys_sem.at[i], recv_sem=yr_sem.at[i],
            device_id={"seq": opposite}, device_id_type=MESH,
        )

    def sibling_copy(i, part, on_core):
        ref = piece_of(extra, side + part * (1 - 2 * side), on_core, i)
        return pltpu.make_async_remote_copy(
            src_ref=ref, dst_ref=ref, send_sem=es_sem.at[part, i], recv_sem=er_sem.at[part, i],
            device_id={"seq": sibling}, device_id_type=MESH,
        )

    def column_slice(t):
        return pl.ds(pl.multiple_of(t * tile, tile), tile)

    def act_copy(d, parity, t):
        return pltpu.make_async_copy(
            hbuf.at[d, parity, t], acts_ref.at[d, 0, :, column_slice(t)], act_sem.at[d, t]
        )

    def ing_copy(d, t):
        return pltpu.make_async_copy(
            cbuf.at[3 + d, t], ingrad_ref.at[d, 0, :, column_slice(t)], ing_sem.at[d, t]
        )

    def kvg_copy(d, k, part):
        start = pl.multiple_of(part * half + k * HEAD_DIM, HEAD_DIM)
        return pltpu.make_async_copy(
            dtot.at[d, k, :, pl.ds(part * HEAD_DIM, HEAD_DIM)],
            kvgrad_ref.at[d, 0, :, pl.ds(start, HEAD_DIM)],
            kvg_sem.at[d, k, part],
        )

    for t in range(KV_HEADS):
        x_copy(0, t).start()
        x_copy(1, t).start()
    own_gain = pltpu.make_async_copy(gains_ref.at[0], gbuf.at[section], g_sem)
    own_gain.start()
    for part in range(2):
        weight_copy(near, 0, part).start()

    barrier = pltpu.get_barrier_semaphore()
    for neighbour in (following, preceding, opposite):
        pl.semaphore_signal(barrier, inc=1, device_id={"seq": neighbour}, device_id_type=MESH)
    for distance in range(1, count):
        pl.semaphore_signal(
            barrier, inc=1, device_id={"section": lax.rem(section + distance, count)},
            device_id_type=MESH,
        )

    for t in range(KV_HEADS):
        x_copy(0, t).wait()
        x_copy(1, t).wait()
    own_gain.wait()
    for d, start in ((near, 1), (far, 0)):
        for k in range(start, KV_HEADS):
            for part in range(2):
                weight_copy(d, k, part).start()
    for d, last in ((0, count - 1), (1, 0)):
        @pl.when(section == last)
        def _():
            for t in range(KV_HEADS):
                grad_copy(d, t).start()

    def gain_of(home, d, cols):
        return jnp.where(d == 0, gbuf[home, 0:1, cols], gbuf[home, 1:2, cols])

    def normalize(d, l, parity, slot):
        home = l + d * (count - 1 - 2 * l)

        @pl.when(l == 0)
        def _():
            squares = jnp.zeros((rows, HEAD_DIM), F32)
            for t in range(KV_HEADS):
                for g in range(GROUP):
                    part = hbuf[d, parity, t, :, g * HEAD_DIM:(g + 1) * HEAD_DIM].astype(F32)
                    squares = squares + part * part
            squares_buf[d] = squares

        square_mean = jnp.sum(squares_buf[d], axis=-1, keepdims=True) * (1.0 / width)
        rstd = jnp.broadcast_to(lax.rsqrt(square_mean + epsilon), (rows, HEAD_DIM))
        rstd_buf[slot] = rstd
        for t in range(KV_HEADS):
            for g in range(GROUP):
                cols = slice(g * HEAD_DIM, (g + 1) * HEAD_DIM)
                gain = gain_of(home, d, slice(t * tile + g * HEAD_DIM, t * tile + (g + 1) * HEAD_DIM))
                part = hbuf[d, parity, t, :, cols].astype(F32)
                nbuf[slot, t, :, cols] = (part * rstd * gain).astype(BF16)

    def make_masks():
        key_places = (shard - 1) * rows + lax.broadcasted_iota(jnp.int32, (2 * rows, rows), 0)
        places = shard * rows + lax.broadcasted_iota(jnp.int32, (2 * rows, rows), 1)
        for d in range(2):
            end = jnp.int32(0)
            docs_k = jnp.zeros((2 * rows, rows), jnp.int32)
            docs_q = jnp.zeros((2 * rows, rows), jnp.int32)
            for j in range(lengths_ref.shape[1]):
                end = end + lengths_ref[d, j]
                docs_k = docs_k + jnp.where(key_places >= end, 1, 0)
                docs_q = docs_q + jnp.where(places >= end, 1, 0)
            allowed = (docs_k == docs_q) & (key_places <= places) & (key_places >= 0)
            bias[d] = jnp.where(allowed, 0.0, -1e30).astype(F32)
        sublane = lax.broadcasted_iota(jnp.int32, (rows, rows), 0)
        lane = lax.broadcasted_iota(jnp.int32, (rows, rows), 1)
        triangle[0] = jnp.where(sublane > lane, 1.0, 0.0).astype(BF16)
        triangle[1] = jnp.where(sublane <= lane, 1.0, 0.0).astype(BF16)
        triangle[2] = jnp.where(lane > sublane, 1.0, 0.0).astype(BF16)
        triangle[3] = jnp.where(lane <= sublane, 1.0, 0.0).astype(BF16)

    middle = (near_depth == far_depth - 1) & (near_depth > 0)

    def arrive(d, l, depth, k):
        z_copy(d, l, k).wait_recv()
        s_copy(d, l, k).start()

        @pl.when(depth < count - 1)
        def _():
            z_copy(d, l, k).start()

    def project(d, depth):
        @pl.when(depth > 0)
        def _():
            normalize(d, depth, lax.rem(depth, 2), d)

        def chunk(k, carry):
            weight_copy(d, k, 0).wait()
            weight_copy(d, k, 1).wait()
            normed = jnp.concatenate([nbuf[d, t] for t in range(KV_HEADS)], axis=1)
            pair = dot(normed, wbuf[d, k], ((1,), (0,))).astype(BF16)
            kv[d, depth, k, 0, rows:, :] = pair[:, :HEAD_DIM]
            kv[d, depth, k, 1, rows:, :] = pair[:, HEAD_DIM:]

            @pl.when(depth < count - 1)
            def _():
                z_copy(d, depth, k).start()

            @pl.when(jnp.logical_not(middle & (depth == near_depth)))
            def _():
                s_copy(d, depth, k).start()

            @pl.when(middle & (depth == near_depth))
            def _():
                arrive(far, 0, far_depth, k)

            return carry

        lax.fori_loop(0, KV_HEADS, chunk, 0)

    def softmax(d, l, k, slot, g):
        both = dot(kv[d, l, k, 0], nbuf[slot, k, :, g * HEAD_DIM:(g + 1) * HEAD_DIM], ((1,), (1,)))
        scores = jnp.maximum(both[:rows] + bias[d, :rows, :], both[rows:] + bias[d, rows:, :])
        powers = jnp.exp2((scores - jnp.max(scores, axis=0, keepdims=True)) * (SCALE * LOG2E))
        weights = (powers * (1.0 / jnp.sum(powers, axis=0, keepdims=True))).astype(BF16)
        wsave[slot, k, g] = weights
        return weights

    def mix(d, l, depth):
        parity = lax.rem(l, 2)

        @pl.when(l < depth)
        def _():
            home = l + d * (count - 1 - 2 * l)
            gain_copy(lax.rem(section - home + count, count)).wait_recv()
            normalize(d, l, parity, d)

        squares_buf[d] = jnp.zeros((rows, HEAD_DIM), F32)

        coming = (l < depth) & ((d == near) | ((l == 0) & jnp.logical_not(middle)))
        ahead = (d == far) & (l + 1 < far_depth)

        @pl.when(coming)
        def _():
            for k in range(KV_HEADS):
                arrive(d, l, depth, k)

        def chunk(k, carry):
            s_copy(d, l, k).wait_recv()
            values = kv[d, l, k, 1]
            spreads = []
            for g in range(GROUP):
                weights = softmax(d, l, k, d, g)
                turned = weights.T
                spreads.append(jnp.concatenate([turned * triangle[2], turned * triangle[3]], axis=1))
            for g in range(GROUP):
                cols = slice(g * HEAD_DIM, (g + 1) * HEAD_DIM)
                total = hbuf[d, parity, k, :, cols].astype(F32) + dot(spreads[g], values, ((1,), (0,)))
                hbuf[d, 1 - parity, k, :, cols] = total.astype(BF16)
                squares_buf[d] += total * total

            @pl.when(l == depth)
            def _():
                act_copy(d, 1 - parity, k).start()

            @pl.when(ahead)
            def _():
                arrive(far, l + 1, far_depth, k)

            return carry

        lax.fori_loop(0, KV_HEADS, chunk, 0)

    @pl.when(near_depth == 0)
    def _():
        normalize(near, 0, 0, near)

    pl.semaphore_wait(barrier, count + 2)
    closest = lax.rem(1 - 2 * near + count, count)
    gain_copy(closest).start()

    def forward(v, carry):
        p = near_depth
        is_near = (v < p) | (v == jnp.where(p == 0, 0, count))
        d = jnp.where(is_near, near, far)
        depth = jnp.where(is_near, near_depth, far_depth)
        l = jnp.where(is_near, jnp.where(v < p, v, p), jnp.where(p == 0, v - 1, v - p))
        far_turn = jnp.where(p == 0, count, count - 1)

        @pl.when((v == p) | (v == far_turn))
        def _():
            pd = jnp.where(v == p, near, far)
            project(pd, jnp.where(v == p, near_depth, far_depth))

            @pl.when((v == far_turn) & middle)
            def _():
                for k in range(KV_HEADS):
                    s_copy(near, near_depth, k).start()

            @pl.when((v == far_turn) & (near_depth == 1))
            def _():
                for k in range(KV_HEADS):
                    back_copy(k).start()
                for i in range(PIECES):
                    quarter_copy(i).start()

        @pl.when(v == 0)
        def _():
            for further in range(1, count - 1):
                gain_copy(1 + lax.rem(closest - 1 + further, count - 1)).start()
            make_masks()

        mix(d, l, depth)
        return carry

    lax.fori_loop(0, count + 1, forward, 0)

    def drain_forward():
        for distance in range(1, count):
            gain_copy(distance).wait_send()
        for d in range(2):
            depth = depth_of(d)

            def layer_drain(l, carry):
                for k in range(KV_HEADS):
                    @pl.when(depth < count - 1)
                    def _():
                        z_copy(d, l, k).wait_send()

                    s_copy(d, l, k).wait_send()
                return carry

            lax.fori_loop(0, depth + 1, layer_drain, 0)
            for k in range(KV_HEADS):
                act_copy(d, lax.rem(depth + 1, 2), k).wait()

    def drain_reverse(d, depth):
        for k in range(KV_HEADS):
            d_copy(d, k).wait_send()

            @pl.when(depth > 0)
            def _():
                for part in range(PARTS):
                    c_copy(d, k, d, part).wait_send()

            ing_copy(d, k).wait()
            kvg_copy(d, k, 0).wait()
            kvg_copy(d, k, 1).wait()

    def pass_opposite(i, carry):
        opposite_copy(i, 1 - side).wait_recv()
        sibling_copy(i, 1, core).start()
        return carry

    def take_sibling(i, carry):
        sibling_copy(i, 0, 1 - core).wait_recv()
        sibling_copy(i, 1, 1 - core).wait_recv()
        return carry

    def prepare():
        d = near

        def pass_quarter(i, carry):
            quarter_copy(i).wait_recv()
            opposite_copy(i, side).start()
            sibling_copy(i, 0, core).start()
            return carry

        for k in range(KV_HEADS):
            back_copy(k).wait_recv()
            s_copy(d, 1, k).start()
        normalize(d, 1, 1, extra)

        def chunk(k, carry):
            s_copy(d, 1, k).wait_recv()
            for g in range(GROUP):
                softmax(d, 1, k, extra, g)
            return carry

        lax.fori_loop(0, KV_HEADS, chunk, 0)
        lax.fori_loop(0, PIECES, pass_quarter, 0)
        drain_forward()
        drain_reverse(far, far_depth)

    def backward(i, carry):
        @pl.when((i != 1) | (near_depth == 0))
        def _():
            reverse_layer(i)

        return carry

    def reverse_layer(i):
        repeated = i == 1
        local = (i == 2) & (near_depth == 0)
        d = jnp.where(i == 0, far, near)
        depth = jnp.where(i == 0, far_depth, jnp.where(repeated, 1, near_depth))
        slot = jnp.where(repeated, extra, d)
        coming = jnp.where(local, 2, d)
        leaving = jnp.where(repeated, 2, 3 + d)
        first = depth == count - 1
        streamed = (depth < count - 1) & ((i != 2) | (near_depth > 0))
        added = streamed & (i != 1)
        parity = lax.rem(depth, 2)
        step = 2 * HEAD_DIM

        @pl.when(repeated)
        def _():
            prepare()

        def settle(k):
            d_copy(slot, k).wait_recv()
            for part in range(2):
                total = downs[k, part].astype(F32) + drecv[slot, k, part].astype(F32)
                dtot[slot, k, :, part * HEAD_DIM:(part + 1) * HEAD_DIM] = total.astype(BF16)

                @pl.when(i != 1)
                def _():
                    kvg_copy(d, k, part).start()

        def grad_part(k, t, u):
            start = pl.multiple_of(t * tile + u * step, step)
            return dot(dtot[slot, k], wbuf[slot, k, pl.ds(start, step), :], ((1,), (1,)))

        def finish(k):
            settle(k)

            def part_tile(t, tile_carry):
                for u in range(tile // step):
                    cols = slice(u * step, (u + 1) * step)
                    part = grad_part(k, t, u)
                    gnbuf[t, :, cols] = jnp.where(k == 0, part, part + gnbuf[t, :, cols])
                return tile_carry

            lax.fori_loop(0, KV_HEADS, part_tile, 0)

        def chunk(k, inner_carry):
            @pl.when(streamed)
            def _():
                for part in range(PARTS):
                    c_copy(d, k, d, part).wait_recv()

                    @pl.when((depth == 1) & (i != 1))
                    def _():
                        c_copy(d, k, d, part).start()

            @pl.when(first)
            def _():
                pltpu.make_async_copy(cbuf.at[d, k], cbuf.at[d, k], c_sem.at[d, k]).wait()

            keys = kv[d, depth, k, 0]
            values = kv[d, depth, k, 1]
            earlier_s, own_s, earlier_w, own_w, queries, cots, spreads = [], [], [], [], [], [], []
            own_first = lax.broadcasted_iota(jnp.int32, (rows, rows), 0) <= (
                lax.broadcasted_iota(jnp.int32, (rows, rows), 1)
            )
            for g in range(GROUP):
                cols = slice(g * HEAD_DIM, (g + 1) * HEAD_DIM)
                cot = cbuf[coming, k, :, cols]
                both = dot(values, cot, ((1,), (1,)))
                weights = wsave[slot, k, g]
                wide = weights.astype(F32)
                grad_w = jnp.where(own_first, both[rows:], both[:rows]) * wide
                mean = jnp.sum(grad_w, axis=0, keepdims=True)
                grad_s = ((grad_w - wide * mean) * SCALE).astype(BF16)
                earlier_s.append(grad_s * triangle[0])
                own_s.append(grad_s * triangle[1])
                earlier_w.append(weights * triangle[0])
                own_w.append(weights * triangle[1])
                queries.append(nbuf[slot, k, :, cols])
                cots.append(cot)
                turned = grad_s.T
                spreads.append(jnp.concatenate([turned * triangle[2], turned * triangle[3]], axis=1))
            for g in range(GROUP):
                cols = slice(g * HEAD_DIM, (g + 1) * HEAD_DIM)
                dqbuf[k, :, cols] = dot(spreads[g], keys, ((1,), (0,))).astype(BF16)
            all_s = jnp.concatenate(
                [jnp.concatenate(earlier_s, axis=1), jnp.concatenate(own_s, axis=1)], axis=0
            )
            all_w = jnp.concatenate(
                [jnp.concatenate(earlier_w, axis=1), jnp.concatenate(own_w, axis=1)], axis=0
            )
            grad_k = dot(all_s, jnp.concatenate(queries, axis=0), ((1,), (0,)))
            grad_v = dot(all_w, jnp.concatenate(cots, axis=0), ((1,), (0,)))
            dsend[slot, k, 0] = grad_k[:rows].astype(BF16)
            dsend[slot, k, 1] = grad_v[:rows].astype(BF16)
            downs[k, 0] = grad_k[rows:].astype(BF16)
            downs[k, 1] = grad_v[rows:].astype(BF16)
            d_copy(slot, k).start()

            @pl.when((k > 0) & added)
            def _():
                finish(k - 1)

            @pl.when(repeated & (k > 0) & (k < 3))
            def _():
                lax.fori_loop((k - 1) * (PIECES // 2), k * (PIECES // 2), pass_opposite, 0)

            return inner_carry

        lax.fori_loop(0, KV_HEADS, chunk, 0)

        @pl.when(repeated)
        def _():
            lax.fori_loop(0, PIECES, take_sibling, 0)

        @pl.when(jnp.logical_not(added))
        def _():
            for k in range(KV_HEADS - 1):
                settle(k)

        settle(KV_HEADS - 1)
        home = depth + d * (count - 1 - 2 * depth)
        rstd = rstd_buf[slot]
        inner_buf[...] = jnp.zeros((rows, HEAD_DIM), F32)

        def grad_tile(heads, t, tile_carry):
            for u in range(tile // step):
                cols = slice(u * step, (u + 1) * step)
                start = pl.multiple_of(t * tile + u * step, step)
                pairs = jnp.concatenate([dtot[slot, k] for k in heads], axis=1)
                weights = jnp.concatenate([wbuf[slot, k, pl.ds(start, step), :] for k in heads], axis=1)
                grad = dot(pairs, weights, ((1,), (1,)))
                if len(heads) < KV_HEADS:
                    grad = grad + gnbuf[t, :, cols]
                grad_n = (grad + dqbuf[t, :, cols].astype(F32)) * gain_of(home, d, pl.ds(start, step))
                gnbuf[t, :, cols] = grad_n
                product = grad_n * hbuf[d, parity, t, :, cols].astype(F32)
                inner_buf[...] += product[:, :HEAD_DIM] + product[:, HEAD_DIM:]
            return tile_carry

        for whole, heads in ((False, range(KV_HEADS - 1, KV_HEADS)), (True, range(KV_HEADS))):
            @pl.when(added != whole)
            def _():
                lax.fori_loop(0, KV_HEADS, functools.partial(grad_tile, heads), 0)

        inner = inner_buf[...]
        inner = jnp.broadcast_to(jnp.sum(inner, axis=-1, keepdims=True), (rows, HEAD_DIM))
        factor = inner * (1.0 / width) * rstd * rstd * rstd

        def total_tile(t, inner_carry):
            for g in range(GROUP):
                cols = slice(g * HEAD_DIM, (g + 1) * HEAD_DIM)
                grad_h = gnbuf[t, :, cols] * rstd - hbuf[d, parity, t, :, cols].astype(F32) * factor
                cbuf[leaving, t, :, cols] = (cbuf[coming, t, :, cols].astype(F32) + grad_h).astype(BF16)

            @pl.when(depth > 1)
            def _():
                for part in range(PARTS):
                    c_copy(d, t, 3 + d, part).start()

            @pl.when(i != 1)
            def _():
                ing_copy(d, t).start()

            return inner_carry

        lax.fori_loop(0, KV_HEADS, total_tile, 0)

    lax.fori_loop(0, 3, backward, 0)

    @pl.when(near_depth == 1)
    def _():
        for k in range(KV_HEADS):
            back_copy(k).wait_send()
        for i in range(PIECES):
            quarter_copy(i).wait_send()

    @pl.when(near_depth == 0)
    def _():
        for k in range(KV_HEADS):
            s_copy(near, 1, k).wait_send()
            d_copy(extra, k).wait_send()
        for i in range(PIECES):
            opposite_copy(i, side).wait_send()
            sibling_copy(i, 0, core).wait_send()
            sibling_copy(i, 1, core).wait_send()

    @pl.when(near_depth > 0)
    def _():
        drain_forward()
        drain_reverse(far, far_depth)

    drain_reverse(near, near_depth)


def hand_over_kernel(acts_ref, ingrad_ref, kvgrad_ref, acts_out, ingrad_out, kvgrad_out, wide, narrow, in_sem, out_sem):
    lines = acts_ref.shape[2] // 2
    moves = []
    for d in range(2):
        for part in range(2):
            block = (d, 0, pl.ds(part * lines, lines))
            for a, (source, target) in enumerate(((acts_ref, acts_out), (ingrad_ref, ingrad_out))):
                moves.append((source.at[block], wide.at[a, d, part], target.at[block]))
        moves.append((kvgrad_ref.at[d, 0], narrow.at[d], kvgrad_out.at[d, 0]))
    inward = [pltpu.make_async_copy(m[0], m[1], in_sem.at[i]) for i, m in enumerate(moves)]
    outward = [pltpu.make_async_copy(m[1], m[2], out_sem.at[i]) for i, m in enumerate(moves)]
    for copy in inward:
        copy.start()
    for taken, given in zip(inward, outward):
        taken.wait()
        given.start()
    for copy in outward:
        copy.wait()


def hand_over(acts, ingrads, kvgrads):
    rows, width = acts.shape[2:]
    anywhere = pl.BlockSpec(memory_space=pl.ANY)
    return pl.pallas_call(
        hand_over_kernel,
        in_specs=[anywhere] * 3,
        out_specs=[anywhere] * 3,
        out_shape=[jax.ShapeDtypeStruct(a.shape, a.dtype) for a in (acts, ingrads, kvgrads)],
        scratch_shapes=[
            pltpu.VMEM((2, 2, 2, rows // 2, width), BF16),
            pltpu.VMEM((2, rows, kvgrads.shape[3]), BF16),
            pltpu.SemaphoreType.DMA((10,)),
            pltpu.SemaphoreType.DMA((10,)),
        ],
        compiler_params=pltpu.CompilerParams(vmem_limit_bytes=60 * 1024 * 1024),
        name="hand_over",
    )(acts, ingrads, kvgrads)


def per_device(x_a, x_b, grad_a, grad_b, gains, kv_weights, doc_lengths):
    count = lax.axis_size("section")
    shards = lax.axis_size("seq")
    rows, width = x_a.shape
    pair_width = kv_weights.shape[-1]
    tile = width // KV_HEADS
    dma = pltpu.SemaphoreType.DMA
    anywhere = pl.BlockSpec(memory_space=pl.ANY)
    results = pl.pallas_call(
        functools.partial(relay_kernel, count, shards),
        in_specs=[pl.BlockSpec(memory_space=pltpu.SMEM)] + [anywhere] * 6,
        out_specs=[anywhere] * 3,
        out_shape=[
            jax.ShapeDtypeStruct((2, 1, rows, width), BF16),
            jax.ShapeDtypeStruct((2, 1, rows, width), BF16),
            jax.ShapeDtypeStruct((2, 1, rows, pair_width), BF16),
        ],
        scratch_shapes=[
            pltpu.VMEM((3, KV_HEADS, width, 2 * HEAD_DIM), BF16),
            pltpu.VMEM((2, 2, KV_HEADS, rows, tile), BF16),
            pltpu.VMEM((3, KV_HEADS, rows, tile), BF16),
            pltpu.VMEM((2, count, KV_HEADS, 2, 2 * rows, HEAD_DIM), BF16),
            pltpu.VMEM((3, KV_HEADS, GROUP, rows, rows), BF16),
            pltpu.VMEM((5, KV_HEADS, rows, tile), BF16),
            pltpu.VMEM((KV_HEADS, rows, tile), BF16),
            pltpu.VMEM((KV_HEADS, rows, tile), F32),
            pltpu.VMEM((count, 2, width), F32),
            pltpu.VMEM((2, 2 * rows, rows), F32),
            pltpu.VMEM((3, rows, HEAD_DIM), F32),
            pltpu.VMEM((3, KV_HEADS, 2, rows, HEAD_DIM), BF16),
            pltpu.VMEM((3, KV_HEADS, 2, rows, HEAD_DIM), BF16),
            pltpu.VMEM((KV_HEADS, 2, rows, HEAD_DIM), BF16),
            pltpu.VMEM((3, KV_HEADS, rows, 2 * HEAD_DIM), BF16),
            pltpu.VMEM((4, rows, rows), BF16),
            pltpu.VMEM((2, rows, HEAD_DIM), F32),
            pltpu.VMEM((rows, HEAD_DIM), F32),
            dma((2, KV_HEADS)),
            dma((2, KV_HEADS, 2)),
            dma((2, KV_HEADS)),
            dma(()),
            dma((count - 1,)),
            dma((count - 1,)),
            dma((2, count, KV_HEADS)),
            dma((2, count, KV_HEADS)),
            dma((2, count, KV_HEADS)),
            dma((2, count, KV_HEADS)),
            dma((2, KV_HEADS, PARTS)),
            dma((2, KV_HEADS, PARTS)),
            dma((3, KV_HEADS)),
            dma((3, KV_HEADS)),
            dma((2, KV_HEADS)),
            dma((2, KV_HEADS)),
            dma((2, KV_HEADS, 2)),
            dma((KV_HEADS,)),
            dma((PIECES,)),
            dma((PIECES,)),
            dma((PIECES,)),
            dma((PIECES,)),
            dma((2, PIECES)),
            dma((2, PIECES)),
        ],
        compiler_params=pltpu.CompilerParams(
            collective_id=0, has_side_effects=True, vmem_limit_bytes=60 * 1024 * 1024
        ),
        name="relay",
    )(doc_lengths, x_a, x_b, grad_a, grad_b, gains, kv_weights)
    return hand_over(*results)


def solution(mesh):
    in_specs = (
        P("seq", None),
        P("seq", None),
        P("seq", None),
        P("seq", None),
        P("section", None, None),
        P("section", None, None, None),
        P(),
    )
    out_specs = (
        P(None, "section", "seq", None),
        P(None, "section", "seq", None),
        P(None, "section", "seq", None),
    )
    return jax.shard_map(
        per_device, mesh=mesh, in_specs=in_specs, out_specs=out_specs, check_vma=False
    )
```

```python
import functools
import math

import jax
import jax.numpy as jnp
from jax import lax
from jax.experimental import pallas as pl
from jax.experimental.pallas import tpu as pltpu
from jax.sharding import PartitionSpec as P

HEADS = 32
HEAD_DIM = 128
KV_HEADS = 4
GROUP = HEADS // KV_HEADS
SCALE = 1.0 / math.sqrt(HEAD_DIM)
LOG2E = math.log2(math.e)
PIECES = 8
PARTS = 4

epsilon = 1e-05

F32 = jnp.float32
BF16 = jnp.bfloat16
MESH = pl.DeviceIdType.MESH


def dot(a, b, dims):
    return lax.dot_general(a, b, (dims, ((), ())), preferred_element_type=F32)


def relay_kernel(
    count, shards,
    lengths_ref, xa_ref, xb_ref, ga_ref, gb_ref, gains_ref, weights_ref,
    acts_ref, ingrad_ref, kvgrad_ref,
    wbuf, hbuf, nbuf, kv, wsave, cbuf, dqbuf, gnbuf, gbuf, bias, rstd_buf,
    dsend, drecv, downs, dtot, triangle, squares_buf, inner_buf,
    x_sem, w_sem, c_sem, g_sem, gs_sem, gr_sem,
    zs_sem, zr_sem, ss_sem, sr_sem, cs_sem, cr_sem, ds_sem, dr_sem,
    act_sem, ing_sem, kvg_sem,
    bs_sem, ps_sem, pr_sem, ys_sem, yr_sem, es_sem, er_sem,
):
    section = lax.axis_index("section")
    shard = lax.axis_index("seq")
    rows = xa_ref.shape[0]
    width = xa_ref.shape[1]
    tile = width // KV_HEADS
    half = KV_HEADS * HEAD_DIM
    near = lax.div(2 * section, count)
    near_depth = section + near * (count - 1 - 2 * section)
    far = 1 - near
    far_depth = count - 1 - near_depth
    following = lax.rem(shard + 1, shards)
    preceding = lax.rem(shard + shards - 1, shards)
    core = lax.rem(shard, 2)
    side = lax.div(2 * shard, shards)
    sibling = shard + 1 - 2 * core
    opposite = lax.rem(shard + shards // 2, shards)
    extra = 2
    piece = width // PIECES

    def depth_of(d):
        return section + d * (count - 1 - 2 * section)

    def x_copy(d, t):
        ref = (xa_ref, xb_ref)[d]
        return pltpu.make_async_copy(
            ref.at[:, pl.ds(t * tile, tile)], hbuf.at[d, 0, t], x_sem.at[d, t]
        )

    def grad_copy(d, t):
        ref = (ga_ref, gb_ref)[d]
        return pltpu.make_async_copy(
            ref.at[:, pl.ds(t * tile, tile)], cbuf.at[d, t], c_sem.at[d, t]
        )

    def weight_copy(d, k, part):
        return pltpu.make_async_copy(
            weights_ref.at[0, d, :, pl.ds(pl.multiple_of(part * half + k * HEAD_DIM, HEAD_DIM), HEAD_DIM)],
            wbuf.at[d, k, :, pl.ds(part * HEAD_DIM, HEAD_DIM)],
            w_sem.at[d, k, part],
        )

    def gain_copy(distance):
        return pltpu.make_async_remote_copy(
            src_ref=gains_ref.at[0],
            dst_ref=gbuf.at[section],
            send_sem=gs_sem.at[distance - 1],
            recv_sem=gr_sem.at[distance - 1],
            device_id={"section": lax.rem(section + distance, count)},
            device_id_type=MESH,
        )

    def z_copy(d, l, k):
        own = kv.at[d, l, k, :, pl.ds(rows, rows), :]
        return pltpu.make_async_remote_copy(
            src_ref=own, dst_ref=own, send_sem=zs_sem.at[d, l, k], recv_sem=zr_sem.at[d, l, k],
            device_id={"section": section + 1 - 2 * d}, device_id_type=MESH,
        )

    def s_copy(d, l, k):
        return pltpu.make_async_remote_copy(
            src_ref=kv.at[d, l, k, :, pl.ds(rows, rows), :],
            dst_ref=kv.at[d, l, k, :, pl.ds(0, rows), :],
            send_sem=ss_sem.at[d, l, k], recv_sem=sr_sem.at[d, l, k],
            device_id={"seq": following}, device_id_type=MESH,
        )

    def c_copy(d, t, slot, part):
        lines = pl.ds(part * (rows // PARTS), rows // PARTS)
        return pltpu.make_async_remote_copy(
            src_ref=cbuf.at[slot, t, lines, :], dst_ref=cbuf.at[d, t, lines, :],
            send_sem=cs_sem.at[d, t, part], recv_sem=cr_sem.at[d, t, part],
            device_id={"section": section - 1 + 2 * d}, device_id_type=MESH,
        )

    def d_copy(slot, k):
        return pltpu.make_async_remote_copy(
            src_ref=dsend.at[slot, k], dst_ref=drecv.at[slot, k],
            send_sem=ds_sem.at[slot, k], recv_sem=dr_sem.at[slot, k],
            device_id={"seq": preceding}, device_id_type=MESH,
        )

    def back_copy(k):
        own = kv.at[near, 1, k, :, pl.ds(rows, rows), :]
        return pltpu.make_async_remote_copy(
            src_ref=own, dst_ref=own, send_sem=bs_sem.at[k], recv_sem=zr_sem.at[near, 1, k],
            device_id={"section": section - 1 + 2 * near}, device_id_type=MESH,
        )

    def piece_of(slot, on_side, on_core, i):
        return wbuf.at[slot, 2 * on_side + on_core, pl.ds(pl.multiple_of(i * piece, piece), piece), :]

    def quarter_copy(i):
        return pltpu.make_async_remote_copy(
            src_ref=piece_of(near, side, core, i), dst_ref=piece_of(extra, side, core, i),
            send_sem=ps_sem.at[i], recv_sem=pr_sem.at[i],
            device_id={"section": section - 1 + 2 * near}, device_id_type=MESH,
        )

    def opposite_copy(i, on_side):
        ref = piece_of(extra, on_side, core, i)
        return pltpu.make_async_remote_copy(
            src_ref=ref, dst_ref=ref, send_sem=ys_sem.at[i], recv_sem=yr_sem.at[i],
            device_id={"seq": opposite}, device_id_type=MESH,
        )

    def sibling_copy(i, part, on_core):
        ref = piece_of(extra, side + part * (1 - 2 * side), on_core, i)
        return pltpu.make_async_remote_copy(
            src_ref=ref, dst_ref=ref, send_sem=es_sem.at[part, i], recv_sem=er_sem.at[part, i],
            device_id={"seq": sibling}, device_id_type=MESH,
        )

    def column_slice(t):
        return pl.ds(pl.multiple_of(t * tile, tile), tile)

    def act_copy(d, parity, t):
        return pltpu.make_async_copy(
            hbuf.at[d, parity, t], acts_ref.at[d, 0, :, column_slice(t)], act_sem.at[d, t]
        )

    def ing_copy(d, t):
        return pltpu.make_async_copy(
            cbuf.at[3 + d, t], ingrad_ref.at[d, 0, :, column_slice(t)], ing_sem.at[d, t]
        )

    def kvg_copy(d, k, part):
        start = pl.multiple_of(part * half + k * HEAD_DIM, HEAD_DIM)
        return pltpu.make_async_copy(
            dtot.at[d, k, :, pl.ds(part * HEAD_DIM, HEAD_DIM)],
            kvgrad_ref.at[d, 0, :, pl.ds(start, HEAD_DIM)],
            kvg_sem.at[d, k, part],
        )

    for t in range(KV_HEADS):
        x_copy(0, t).start()
        x_copy(1, t).start()
    own_gain = pltpu.make_async_copy(gains_ref.at[0], gbuf.at[section], g_sem)
    own_gain.start()
    for part in range(2):
        weight_copy(near, 0, part).start()

    barrier = pltpu.get_barrier_semaphore()
    for neighbour in (following, preceding, opposite):
        pl.semaphore_signal(barrier, inc=1, device_id={"seq": neighbour}, device_id_type=MESH)
    for distance in range(1, count):
        pl.semaphore_signal(
            barrier, inc=1, device_id={"section": lax.rem(section + distance, count)},
            device_id_type=MESH,
        )

    for t in range(KV_HEADS):
        x_copy(0, t).wait()
        x_copy(1, t).wait()
    own_gain.wait()
    for d, start in ((near, 1), (far, 0)):
        for k in range(start, KV_HEADS):
            for part in range(2):
                weight_copy(d, k, part).start()
    for d, last in ((0, count - 1), (1, 0)):
        @pl.when(section == last)
        def _():
            for t in range(KV_HEADS):
                grad_copy(d, t).start()

    def gain_of(home, d, cols):
        return jnp.where(d == 0, gbuf[home, 0:1, cols], gbuf[home, 1:2, cols])

    def normalize(d, l, parity, slot):
        home = l + d * (count - 1 - 2 * l)

        @pl.when(l == 0)
        def _():
            squares = jnp.zeros((rows, HEAD_DIM), F32)
            for t in range(KV_HEADS):
                for g in range(GROUP):
                    part = hbuf[d, parity, t, :, g * HEAD_DIM:(g + 1) * HEAD_DIM].astype(F32)
                    squares = squares + part * part
            squares_buf[d] = squares

        square_mean = jnp.sum(squares_buf[d], axis=-1, keepdims=True) * (1.0 / width)
        rstd = jnp.broadcast_to(lax.rsqrt(square_mean + epsilon), (rows, HEAD_DIM))
        rstd_buf[slot] = rstd
        for t in range(KV_HEADS):
            for g in range(GROUP):
                cols = slice(g * HEAD_DIM, (g + 1) * HEAD_DIM)
                gain = gain_of(home, d, slice(t * tile + g * HEAD_DIM, t * tile + (g + 1) * HEAD_DIM))
                part = hbuf[d, parity, t, :, cols].astype(F32)
                nbuf[slot, t, :, cols] = (part * rstd * gain).astype(BF16)

    def make_masks():
        key_places = (shard - 1) * rows + lax.broadcasted_iota(jnp.int32, (2 * rows, rows), 0)
        places = shard * rows + lax.broadcasted_iota(jnp.int32, (2 * rows, rows), 1)
        for d in range(2):
            end = jnp.int32(0)
            docs_k = jnp.zeros((2 * rows, rows), jnp.int32)
            docs_q = jnp.zeros((2 * rows, rows), jnp.int32)
            for j in range(lengths_ref.shape[1]):
                end = end + lengths_ref[d, j]
                docs_k = docs_k + jnp.where(key_places >= end, 1, 0)
                docs_q = docs_q + jnp.where(places >= end, 1, 0)
            allowed = (docs_k == docs_q) & (key_places <= places) & (key_places >= 0)
            bias[d] = jnp.where(allowed, 0.0, -1e30).astype(F32)
        sublane = lax.broadcasted_iota(jnp.int32, (rows, rows), 0)
        lane = lax.broadcasted_iota(jnp.int32, (rows, rows), 1)
        triangle[0] = jnp.where(sublane > lane, 1.0, 0.0).astype(BF16)
        triangle[1] = jnp.where(sublane <= lane, 1.0, 0.0).astype(BF16)
        triangle[2] = jnp.where(lane > sublane, 1.0, 0.0).astype(BF16)
        triangle[3] = jnp.where(lane <= sublane, 1.0, 0.0).astype(BF16)

    middle = (near_depth == far_depth - 1) & (near_depth > 0)

    def arrive(d, l, depth, k):
        z_copy(d, l, k).wait_recv()
        s_copy(d, l, k).start()

        @pl.when(depth < count - 1)
        def _():
            z_copy(d, l, k).start()

    def project(d, depth):
        @pl.when(depth > 0)
        def _():
            normalize(d, depth, lax.rem(depth, 2), d)

        def chunk(k, carry):
            @pl.when(middle & (depth == near_depth))
            def _():
                arrive(far, 0, far_depth, k)

            weight_copy(d, k, 0).wait()
            weight_copy(d, k, 1).wait()
            normed = jnp.concatenate([nbuf[d, t] for t in range(KV_HEADS)], axis=1)
            pair = dot(normed, wbuf[d, k], ((1,), (0,))).astype(BF16)
            kv[d, depth, k, 0, rows:, :] = pair[:, :HEAD_DIM]
            kv[d, depth, k, 1, rows:, :] = pair[:, HEAD_DIM:]

            @pl.when(depth < count - 1)
            def _():
                z_copy(d, depth, k).start()

            @pl.when(jnp.logical_not(middle & (depth == near_depth)))
            def _():
                s_copy(d, depth, k).start()

            return carry

        lax.fori_loop(0, KV_HEADS, chunk, 0)

    def softmax(d, l, k, slot, g):
        both = dot(kv[d, l, k, 0], nbuf[slot, k, :, g * HEAD_DIM:(g + 1) * HEAD_DIM], ((1,), (1,)))
        scores = jnp.maximum(both[:rows] + bias[d, :rows, :], both[rows:] + bias[d, rows:, :])
        powers = jnp.exp2((scores - jnp.max(scores, axis=0, keepdims=True)) * (SCALE * LOG2E))
        weights = (powers * (1.0 / jnp.sum(powers, axis=0, keepdims=True))).astype(BF16)
        wsave[slot, k, g] = weights
        return weights

    def mix(d, l, depth):
        parity = lax.rem(l, 2)

        @pl.when(l < depth)
        def _():
            home = l + d * (count - 1 - 2 * l)
            gain_copy(lax.rem(section - home + count, count)).wait_recv()
            normalize(d, l, parity, d)

        squares_buf[d] = jnp.zeros((rows, HEAD_DIM), F32)

        coming = (l < depth) & ((d == near) | ((l == 0) & jnp.logical_not(middle)))
        ahead = (d == far) & (l + 1 < far_depth)

        @pl.when(coming)
        def _():
            for k in range(KV_HEADS):
                arrive(d, l, depth, k)

        def chunk(k, carry):
            s_copy(d, l, k).wait_recv()
            values = kv[d, l, k, 1]
            spreads = []
            for g in range(GROUP):
                weights = softmax(d, l, k, d, g)
                turned = weights.T
                spreads.append(jnp.concatenate([turned * triangle[2], turned * triangle[3]], axis=1))
            for g in range(GROUP):
                cols = slice(g * HEAD_DIM, (g + 1) * HEAD_DIM)
                total = hbuf[d, parity, k, :, cols].astype(F32) + dot(spreads[g], values, ((1,), (0,)))
                hbuf[d, 1 - parity, k, :, cols] = total.astype(BF16)
                squares_buf[d] += total * total

            @pl.when(l == depth)
            def _():
                act_copy(d, 1 - parity, k).start()

            @pl.when(ahead)
            def _():
                arrive(far, l + 1, far_depth, k)

            return carry

        lax.fori_loop(0, KV_HEADS, chunk, 0)

    @pl.when(near_depth == 0)
    def _():
        normalize(near, 0, 0, near)

    pl.semaphore_wait(barrier, count + 2)
    closest = lax.rem(1 - 2 * near + count, count)
    gain_copy(closest).start()

    def forward(v, carry):
        p = near_depth
        is_near = (v < p) | (v == jnp.where(p == 0, 0, count))
        d = jnp.where(is_near, near, far)
        depth = jnp.where(is_near, near_depth, far_depth)
        l = jnp.where(is_near, jnp.where(v < p, v, p), jnp.where(p == 0, v - 1, v - p))
        far_turn = jnp.where(p == 0, count, count - 1)

        @pl.when((v == p) | (v == far_turn))
        def _():
            pd = jnp.where(v == p, near, far)
            project(pd, jnp.where(v == p, near_depth, far_depth))

            @pl.when((v == far_turn) & middle)
            def _():
                for k in range(KV_HEADS):
                    s_copy(near, near_depth, k).start()

            @pl.when((v == far_turn) & (near_depth == 1))
            def _():
                for k in range(KV_HEADS):
                    back_copy(k).start()
                for i in range(PIECES):
                    quarter_copy(i).start()

        @pl.when(v == 0)
        def _():
            for further in range(1, count - 1):
                gain_copy(1 + lax.rem(closest - 1 + further, count - 1)).start()
            make_masks()

        mix(d, l, depth)
        return carry

    lax.fori_loop(0, count + 1, forward, 0)

    def drain_forward():
        for distance in range(1, count):
            gain_copy(distance).wait_send()
        for d in range(2):
            depth = depth_of(d)

            def layer_drain(l, carry):
                for k in range(KV_HEADS):
                    @pl.when(depth < count - 1)
                    def _():
                        z_copy(d, l, k).wait_send()

                    s_copy(d, l, k).wait_send()
                return carry

            lax.fori_loop(0, depth + 1, layer_drain, 0)
            for k in range(KV_HEADS):
                act_copy(d, lax.rem(depth + 1, 2), k).wait()

    def drain_reverse(d, depth):
        for k in range(KV_HEADS):
            d_copy(d, k).wait_send()

            @pl.when(depth > 0)
            def _():
                for part in range(PARTS):
                    c_copy(d, k, d, part).wait_send()

            ing_copy(d, k).wait()
            kvg_copy(d, k, 0).wait()
            kvg_copy(d, k, 1).wait()

    def pass_opposite(i, carry):
        opposite_copy(i, 1 - side).wait_recv()
        sibling_copy(i, 1, core).start()
        return carry

    def take_sibling(i, carry):
        sibling_copy(i, 0, 1 - core).wait_recv()
        sibling_copy(i, 1, 1 - core).wait_recv()
        return carry

    def prepare():
        d = near

        def pass_quarter(i, carry):
            quarter_copy(i).wait_recv()
            opposite_copy(i, side).start()
            sibling_copy(i, 0, core).start()
            return carry

        for k in range(KV_HEADS):
            back_copy(k).wait_recv()
            s_copy(d, 1, k).start()
        normalize(d, 1, 1, extra)

        def chunk(k, carry):
            s_copy(d, 1, k).wait_recv()
            for g in range(GROUP):
                softmax(d, 1, k, extra, g)
            return carry

        lax.fori_loop(0, KV_HEADS, chunk, 0)
        lax.fori_loop(0, PIECES, pass_quarter, 0)
        drain_forward()
        drain_reverse(far, far_depth)

    def backward(i, carry):
        @pl.when((i != 1) | (near_depth == 0))
        def _():
            reverse_layer(i)

        return carry

    def reverse_layer(i):
        repeated = i == 1
        local = (i == 2) & (near_depth == 0)
        d = jnp.where(i == 0, far, near)
        depth = jnp.where(i == 0, far_depth, jnp.where(repeated, 1, near_depth))
        slot = jnp.where(repeated, extra, d)
        coming = jnp.where(local, 2, d)
        leaving = jnp.where(repeated, 2, 3 + d)
        first = depth == count - 1
        streamed = (depth < count - 1) & ((i != 2) | (near_depth > 0))
        added = streamed & (i != 1)
        parity = lax.rem(depth, 2)
        step = 2 * HEAD_DIM

        @pl.when(repeated)
        def _():
            prepare()

        def settle(k):
            d_copy(slot, k).wait_recv()
            for part in range(2):
                total = downs[k, part].astype(F32) + drecv[slot, k, part].astype(F32)
                dtot[slot, k, :, part * HEAD_DIM:(part + 1) * HEAD_DIM] = total.astype(BF16)

                @pl.when(i != 1)
                def _():
                    kvg_copy(d, k, part).start()

        def grad_part(k, t, u):
            start = pl.multiple_of(t * tile + u * step, step)
            return dot(dtot[slot, k], wbuf[slot, k, pl.ds(start, step), :], ((1,), (1,)))

        def finish(k):
            settle(k)

            def part_tile(t, tile_carry):
                for u in range(tile // step):
                    cols = slice(u * step, (u + 1) * step)
                    part = grad_part(k, t, u)
                    gnbuf[t, :, cols] = jnp.where(k == 0, part, part + gnbuf[t, :, cols])
                return tile_carry

            lax.fori_loop(0, KV_HEADS, part_tile, 0)

        def chunk(k, inner_carry):
            @pl.when(streamed)
            def _():
                for part in range(PARTS):
                    c_copy(d, k, d, part).wait_recv()

                    @pl.when((depth == 1) & (i != 1))
                    def _():
                        c_copy(d, k, d, part).start()

            @pl.when(first)
            def _():
                pltpu.make_async_copy(cbuf.at[d, k], cbuf.at[d, k], c_sem.at[d, k]).wait()

            keys = kv[d, depth, k, 0]
            values = kv[d, depth, k, 1]
            earlier_s, own_s, earlier_w, own_w, queries, cots, spreads = [], [], [], [], [], [], []
            own_first = lax.broadcasted_iota(jnp.int32, (rows, rows), 0) <= (
                lax.broadcasted_iota(jnp.int32, (rows, rows), 1)
            )
            for g in range(GROUP):
                cols = slice(g * HEAD_DIM, (g + 1) * HEAD_DIM)
                cot = cbuf[coming, k, :, cols]
                both = dot(values, cot, ((1,), (1,)))
                weights = wsave[slot, k, g]
                wide = weights.astype(F32)
                grad_w = jnp.where(own_first, both[rows:], both[:rows]) * wide
                mean = jnp.sum(grad_w, axis=0, keepdims=True)
                grad_s = ((grad_w - wide * mean) * SCALE).astype(BF16)
                earlier_s.append(grad_s * triangle[0])
                own_s.append(grad_s * triangle[1])
                earlier_w.append(weights * triangle[0])
                own_w.append(weights * triangle[1])
                queries.append(nbuf[slot, k, :, cols])
                cots.append(cot)
                turned = grad_s.T
                spreads.append(jnp.concatenate([turned * triangle[2], turned * triangle[3]], axis=1))
            for g in range(GROUP):
                cols = slice(g * HEAD_DIM, (g + 1) * HEAD_DIM)
                dqbuf[k, :, cols] = dot(spreads[g], keys, ((1,), (0,))).astype(BF16)
            all_s = jnp.concatenate(
                [jnp.concatenate(earlier_s, axis=1), jnp.concatenate(own_s, axis=1)], axis=0
            )
            all_w = jnp.concatenate(
                [jnp.concatenate(earlier_w, axis=1), jnp.concatenate(own_w, axis=1)], axis=0
            )
            grad_k = dot(all_s, jnp.concatenate(queries, axis=0), ((1,), (0,)))
            grad_v = dot(all_w, jnp.concatenate(cots, axis=0), ((1,), (0,)))
            dsend[slot, k, 0] = grad_k[:rows].astype(BF16)
            dsend[slot, k, 1] = grad_v[:rows].astype(BF16)
            downs[k, 0] = grad_k[rows:].astype(BF16)
            downs[k, 1] = grad_v[rows:].astype(BF16)
            d_copy(slot, k).start()

            @pl.when((k > 0) & added)
            def _():
                finish(k - 1)

            @pl.when(repeated & (k > 0) & (k < 3))
            def _():
                lax.fori_loop((k - 1) * (PIECES // 2), k * (PIECES // 2), pass_opposite, 0)

            return inner_carry

        lax.fori_loop(0, KV_HEADS, chunk, 0)

        @pl.when(repeated)
        def _():
            lax.fori_loop(0, PIECES, take_sibling, 0)

        @pl.when(jnp.logical_not(added))
        def _():
            for k in range(KV_HEADS - 1):
                settle(k)

        settle(KV_HEADS - 1)
        home = depth + d * (count - 1 - 2 * depth)
        rstd = rstd_buf[slot]
        inner_buf[...] = jnp.zeros((rows, HEAD_DIM), F32)

        def grad_tile(heads, t, tile_carry):
            for u in range(tile // step):
                cols = slice(u * step, (u + 1) * step)
                start = pl.multiple_of(t * tile + u * step, step)
                pairs = jnp.concatenate([dtot[slot, k] for k in heads], axis=1)
                weights = jnp.concatenate([wbuf[slot, k, pl.ds(start, step), :] for k in heads], axis=1)
                grad = dot(pairs, weights, ((1,), (1,)))
                if len(heads) < KV_HEADS:
                    grad = grad + gnbuf[t, :, cols]
                grad_n = (grad + dqbuf[t, :, cols].astype(F32)) * gain_of(home, d, pl.ds(start, step))
                gnbuf[t, :, cols] = grad_n
                product = grad_n * hbuf[d, parity, t, :, cols].astype(F32)
                inner_buf[...] += product[:, :HEAD_DIM] + product[:, HEAD_DIM:]
            return tile_carry

        for whole, heads in ((False, range(KV_HEADS - 1, KV_HEADS)), (True, range(KV_HEADS))):
            @pl.when(added != whole)
            def _():
                lax.fori_loop(0, KV_HEADS, functools.partial(grad_tile, heads), 0)

        inner = inner_buf[...]
        inner = jnp.broadcast_to(jnp.sum(inner, axis=-1, keepdims=True), (rows, HEAD_DIM))
        factor = inner * (1.0 / width) * rstd * rstd * rstd

        def total_tile(t, inner_carry):
            for g in range(GROUP):
                cols = slice(g * HEAD_DIM, (g + 1) * HEAD_DIM)
                grad_h = gnbuf[t, :, cols] * rstd - hbuf[d, parity, t, :, cols].astype(F32) * factor
                cbuf[leaving, t, :, cols] = (cbuf[coming, t, :, cols].astype(F32) + grad_h).astype(BF16)

            @pl.when(depth > 1)
            def _():
                for part in range(PARTS):
                    c_copy(d, t, 3 + d, part).start()

            @pl.when(i != 1)
            def _():
                ing_copy(d, t).start()

            return inner_carry

        lax.fori_loop(0, KV_HEADS, total_tile, 0)

    lax.fori_loop(0, 3, backward, 0)

    @pl.when(near_depth == 1)
    def _():
        for k in range(KV_HEADS):
            back_copy(k).wait_send()
        for i in range(PIECES):
            quarter_copy(i).wait_send()

    @pl.when(near_depth == 0)
    def _():
        for k in range(KV_HEADS):
            s_copy(near, 1, k).wait_send()
            d_copy(extra, k).wait_send()
        for i in range(PIECES):
            opposite_copy(i, side).wait_send()
            sibling_copy(i, 0, core).wait_send()
            sibling_copy(i, 1, core).wait_send()

    @pl.when(near_depth > 0)
    def _():
        drain_forward()
        drain_reverse(far, far_depth)

    drain_reverse(near, near_depth)


def hand_over_kernel(acts_ref, ingrad_ref, kvgrad_ref, acts_out, ingrad_out, kvgrad_out, wide, narrow, in_sem, out_sem):
    lines = acts_ref.shape[2] // 2
    moves = []
    for d in range(2):
        for part in range(2):
            block = (d, 0, pl.ds(part * lines, lines))
            for a, (source, target) in enumerate(((acts_ref, acts_out), (ingrad_ref, ingrad_out))):
                moves.append((source.at[block], wide.at[a, d, part], target.at[block]))
        moves.append((kvgrad_ref.at[d, 0], narrow.at[d], kvgrad_out.at[d, 0]))
    inward = [pltpu.make_async_copy(m[0], m[1], in_sem.at[i]) for i, m in enumerate(moves)]
    outward = [pltpu.make_async_copy(m[1], m[2], out_sem.at[i]) for i, m in enumerate(moves)]
    for copy in inward:
        copy.start()
    for taken, given in zip(inward, outward):
        taken.wait()
        given.start()
    for copy in outward:
        copy.wait()


def hand_over(acts, ingrads, kvgrads):
    rows, width = acts.shape[2:]
    anywhere = pl.BlockSpec(memory_space=pl.ANY)
    return pl.pallas_call(
        hand_over_kernel,
        in_specs=[anywhere] * 3,
        out_specs=[anywhere] * 3,
        out_shape=[jax.ShapeDtypeStruct(a.shape, a.dtype) for a in (acts, ingrads, kvgrads)],
        scratch_shapes=[
            pltpu.VMEM((2, 2, 2, rows // 2, width), BF16),
            pltpu.VMEM((2, rows, kvgrads.shape[3]), BF16),
            pltpu.SemaphoreType.DMA((10,)),
            pltpu.SemaphoreType.DMA((10,)),
        ],
        compiler_params=pltpu.CompilerParams(vmem_limit_bytes=60 * 1024 * 1024),
        name="hand_over",
    )(acts, ingrads, kvgrads)


def per_device(x_a, x_b, grad_a, grad_b, gains, kv_weights, doc_lengths):
    count = lax.axis_size("section")
    shards = lax.axis_size("seq")
    rows, width = x_a.shape
    pair_width = kv_weights.shape[-1]
    tile = width // KV_HEADS
    dma = pltpu.SemaphoreType.DMA
    anywhere = pl.BlockSpec(memory_space=pl.ANY)
    results = pl.pallas_call(
        functools.partial(relay_kernel, count, shards),
        in_specs=[pl.BlockSpec(memory_space=pltpu.SMEM)] + [anywhere] * 6,
        out_specs=[anywhere] * 3,
        out_shape=[
            jax.ShapeDtypeStruct((2, 1, rows, width), BF16),
            jax.ShapeDtypeStruct((2, 1, rows, width), BF16),
            jax.ShapeDtypeStruct((2, 1, rows, pair_width), BF16),
        ],
        scratch_shapes=[
            pltpu.VMEM((3, KV_HEADS, width, 2 * HEAD_DIM), BF16),
            pltpu.VMEM((2, 2, KV_HEADS, rows, tile), BF16),
            pltpu.VMEM((3, KV_HEADS, rows, tile), BF16),
            pltpu.VMEM((2, count, KV_HEADS, 2, 2 * rows, HEAD_DIM), BF16),
            pltpu.VMEM((3, KV_HEADS, GROUP, rows, rows), BF16),
            pltpu.VMEM((5, KV_HEADS, rows, tile), BF16),
            pltpu.VMEM((KV_HEADS, rows, tile), BF16),
            pltpu.VMEM((KV_HEADS, rows, tile), F32),
            pltpu.VMEM((count, 2, width), F32),
            pltpu.VMEM((2, 2 * rows, rows), F32),
            pltpu.VMEM((3, rows, HEAD_DIM), F32),
            pltpu.VMEM((3, KV_HEADS, 2, rows, HEAD_DIM), BF16),
            pltpu.VMEM((3, KV_HEADS, 2, rows, HEAD_DIM), BF16),
            pltpu.VMEM((KV_HEADS, 2, rows, HEAD_DIM), BF16),
            pltpu.VMEM((3, KV_HEADS, rows, 2 * HEAD_DIM), BF16),
            pltpu.VMEM((4, rows, rows), BF16),
            pltpu.VMEM((2, rows, HEAD_DIM), F32),
            pltpu.VMEM((rows, HEAD_DIM), F32),
            dma((2, KV_HEADS)),
            dma((2, KV_HEADS, 2)),
            dma((2, KV_HEADS)),
            dma(()),
            dma((count - 1,)),
            dma((count - 1,)),
            dma((2, count, KV_HEADS)),
            dma((2, count, KV_HEADS)),
            dma((2, count, KV_HEADS)),
            dma((2, count, KV_HEADS)),
            dma((2, KV_HEADS, PARTS)),
            dma((2, KV_HEADS, PARTS)),
            dma((3, KV_HEADS)),
            dma((3, KV_HEADS)),
            dma((2, KV_HEADS)),
            dma((2, KV_HEADS)),
            dma((2, KV_HEADS, 2)),
            dma((KV_HEADS,)),
            dma((PIECES,)),
            dma((PIECES,)),
            dma((PIECES,)),
            dma((PIECES,)),
            dma((2, PIECES)),
            dma((2, PIECES)),
        ],
        compiler_params=pltpu.CompilerParams(
            collective_id=0, has_side_effects=True, vmem_limit_bytes=60 * 1024 * 1024
        ),
        name="relay",
    )(doc_lengths, x_a, x_b, grad_a, grad_b, gains, kv_weights)
    return hand_over(*results)


def solution(mesh):
    in_specs = (
        P("seq", None),
        P("seq", None),
        P("seq", None),
        P("seq", None),
        P("section", None, None),
        P("section", None, None, None),
        P(),
    )
    out_specs = (
        P(None, "section", "seq", None),
        P(None, "section", "seq", None),
        P(None, "section", "seq", None),
    )
    return jax.shard_map(
        per_device, mesh=mesh, in_specs=in_specs, out_specs=out_specs, check_vma=False
    )
```

```python
import functools
import math

import jax
import jax.numpy as jnp
from jax import lax
from jax.experimental import pallas as pl
from jax.experimental.pallas import tpu as pltpu
from jax.sharding import PartitionSpec as P

HEADS = 32
HEAD_DIM = 128
KV_HEADS = 4
GROUP = HEADS // KV_HEADS
SCALE = 1.0 / math.sqrt(HEAD_DIM)
LOG2E = math.log2(math.e)
PIECES = 8
PARTS = 4

epsilon = 1e-05

F32 = jnp.float32
BF16 = jnp.bfloat16
MESH = pl.DeviceIdType.MESH


def dot(a, b, dims):
    return lax.dot_general(a, b, (dims, ((), ())), preferred_element_type=F32)


def relay_kernel(
    count, shards,
    lengths_ref, xa_ref, xb_ref, ga_ref, gb_ref, gains_ref, weights_ref,
    acts_ref, ingrad_ref, kvgrad_ref,
    wbuf, hbuf, nbuf, kv, wsave, cbuf, dqbuf, gnbuf, gbuf, bias, rstd_buf,
    dsend, drecv, downs, dtot, triangle, squares_buf, inner_buf,
    x_sem, w_sem, c_sem, g_sem, gs_sem, gr_sem,
    zs_sem, zr_sem, ss_sem, sr_sem, cs_sem, cr_sem, ds_sem, dr_sem,
    act_sem, ing_sem, kvg_sem,
    bs_sem, ps_sem, pr_sem, ys_sem, yr_sem, es_sem, er_sem,
):
    section = lax.axis_index("section")
    shard = lax.axis_index("seq")
    rows = xa_ref.shape[0]
    width = xa_ref.shape[1]
    tile = width // KV_HEADS
    half = KV_HEADS * HEAD_DIM
    near = lax.div(2 * section, count)
    near_depth = section + near * (count - 1 - 2 * section)
    far = 1 - near
    far_depth = count - 1 - near_depth
    following = lax.rem(shard + 1, shards)
    preceding = lax.rem(shard + shards - 1, shards)
    core = lax.rem(shard, 2)
    side = lax.div(2 * shard, shards)
    sibling = shard + 1 - 2 * core
    opposite = lax.rem(shard + shards // 2, shards)
    extra = 2
    piece = width // PIECES

    def depth_of(d):
        return section + d * (count - 1 - 2 * section)

    def x_copy(d, t):
        ref = (xa_ref, xb_ref)[d]
        return pltpu.make_async_copy(
            ref.at[:, pl.ds(t * tile, tile)], hbuf.at[d, 0, t], x_sem.at[d, t]
        )

    def grad_copy(d, t):
        ref = (ga_ref, gb_ref)[d]
        return pltpu.make_async_copy(
            ref.at[:, pl.ds(t * tile, tile)], cbuf.at[d, t], c_sem.at[d, t]
        )

    def weight_copy(d, k, part):
        return pltpu.make_async_copy(
            weights_ref.at[0, d, :, pl.ds(pl.multiple_of(part * half + k * HEAD_DIM, HEAD_DIM), HEAD_DIM)],
            wbuf.at[d, k, :, pl.ds(part * HEAD_DIM, HEAD_DIM)],
            w_sem.at[d, k, part],
        )

    def gain_copy(distance):
        return pltpu.make_async_remote_copy(
            src_ref=gains_ref.at[0],
            dst_ref=gbuf.at[section],
            send_sem=gs_sem.at[distance - 1],
            recv_sem=gr_sem.at[distance - 1],
            device_id={"section": lax.rem(section + distance, count)},
            device_id_type=MESH,
        )

    def z_copy(d, l, k):
        own = kv.at[d, l, k, :, pl.ds(rows, rows), :]
        return pltpu.make_async_remote_copy(
            src_ref=own, dst_ref=own, send_sem=zs_sem.at[d, l, k], recv_sem=zr_sem.at[d, l, k],
            device_id={"section": section + 1 - 2 * d}, device_id_type=MESH,
        )

    def s_copy(d, l, k):
        return pltpu.make_async_remote_copy(
            src_ref=kv.at[d, l, k, :, pl.ds(rows, rows), :],
            dst_ref=kv.at[d, l, k, :, pl.ds(0, rows), :],
            send_sem=ss_sem.at[d, l, k], recv_sem=sr_sem.at[d, l, k],
            device_id={"seq": following}, device_id_type=MESH,
        )

    def c_copy(d, t, slot, part):
        lines = pl.ds(part * (rows // PARTS), rows // PARTS)
        return pltpu.make_async_remote_copy(
            src_ref=cbuf.at[slot, t, lines, :], dst_ref=cbuf.at[d, t, lines, :],
            send_sem=cs_sem.at[d, t, part], recv_sem=cr_sem.at[d, t, part],
            device_id={"section": section - 1 + 2 * d}, device_id_type=MESH,
        )

    def d_copy(slot, k):
        return pltpu.make_async_remote_copy(
            src_ref=dsend.at[slot, k], dst_ref=drecv.at[slot, k],
            send_sem=ds_sem.at[slot, k], recv_sem=dr_sem.at[slot, k],
            device_id={"seq": preceding}, device_id_type=MESH,
        )

    def back_copy(k):
        own = kv.at[near, 1, k, :, pl.ds(rows, rows), :]
        return pltpu.make_async_remote_copy(
            src_ref=own, dst_ref=own, send_sem=bs_sem.at[k], recv_sem=zr_sem.at[near, 1, k],
            device_id={"section": section - 1 + 2 * near}, device_id_type=MESH,
        )

    def piece_of(slot, on_side, on_core, i):
        return wbuf.at[slot, 2 * on_side + on_core, pl.ds(pl.multiple_of(i * piece, piece), piece), :]

    def quarter_copy(i):
        return pltpu.make_async_remote_copy(
            src_ref=piece_of(near, side, core, i), dst_ref=piece_of(extra, side, core, i),
            send_sem=ps_sem.at[i], recv_sem=pr_sem.at[i],
            device_id={"section": section - 1 + 2 * near}, device_id_type=MESH,
        )

    def opposite_copy(i, on_side):
        ref = piece_of(extra, on_side, core, i)
        return pltpu.make_async_remote_copy(
            src_ref=ref, dst_ref=ref, send_sem=ys_sem.at[i], recv_sem=yr_sem.at[i],
            device_id={"seq": opposite}, device_id_type=MESH,
        )

    def sibling_copy(i, part, on_core):
        ref = piece_of(extra, side + part * (1 - 2 * side), on_core, i)
        return pltpu.make_async_remote_copy(
            src_ref=ref, dst_ref=ref, send_sem=es_sem.at[part, i], recv_sem=er_sem.at[part, i],
            device_id={"seq": sibling}, device_id_type=MESH,
        )

    def column_slice(t):
        return pl.ds(pl.multiple_of(t * tile, tile), tile)

    def act_copy(d, parity, t):
        return pltpu.make_async_copy(
            hbuf.at[d, parity, t], acts_ref.at[d, 0, :, column_slice(t)], act_sem.at[d, t]
        )

    def ing_copy(d, t):
        return pltpu.make_async_copy(
            cbuf.at[3 + d, t], ingrad_ref.at[d, 0, :, column_slice(t)], ing_sem.at[d, t]
        )

    def kvg_copy(d, k, part):
        start = pl.multiple_of(part * half + k * HEAD_DIM, HEAD_DIM)
        return pltpu.make_async_copy(
            dtot.at[d, k, :, pl.ds(part * HEAD_DIM, HEAD_DIM)],
            kvgrad_ref.at[d, 0, :, pl.ds(start, HEAD_DIM)],
            kvg_sem.at[d, k, part],
        )

    barrier = pltpu.get_barrier_semaphore()
    for neighbour in (following, preceding, opposite):
        pl.semaphore_signal(barrier, inc=1, device_id={"seq": neighbour}, device_id_type=MESH)
    for distance in range(1, count):
        pl.semaphore_signal(
            barrier, inc=1, device_id={"section": lax.rem(section + distance, count)},
            device_id_type=MESH,
        )

    for t in range(KV_HEADS):
        x_copy(0, t).start()
        x_copy(1, t).start()
    own_gain = pltpu.make_async_copy(gains_ref.at[0], gbuf.at[section], g_sem)
    own_gain.start()
    for part in range(2):
        weight_copy(near, 0, part).start()

    for t in range(KV_HEADS):
        x_copy(0, t).wait()
        x_copy(1, t).wait()
    own_gain.wait()
    for d, start in ((near, 1), (far, 0)):
        for k in range(start, KV_HEADS):
            for part in range(2):
                weight_copy(d, k, part).start()
    for d, last in ((0, count - 1), (1, 0)):
        @pl.when(section == last)
        def _():
            for t in range(KV_HEADS):
                grad_copy(d, t).start()

    def gain_of(home, d, cols):
        return jnp.where(d == 0, gbuf[home, 0:1, cols], gbuf[home, 1:2, cols])

    def normalize(d, l, parity, slot):
        home = l + d * (count - 1 - 2 * l)

        @pl.when(l == 0)
        def _():
            squares = jnp.zeros((rows, HEAD_DIM), F32)
            for t in range(KV_HEADS):
                for g in range(GROUP):
                    part = hbuf[d, parity, t, :, g * HEAD_DIM:(g + 1) * HEAD_DIM].astype(F32)
                    squares = squares + part * part
            squares_buf[d] = squares

        square_mean = jnp.sum(squares_buf[d], axis=-1, keepdims=True) * (1.0 / width)
        rstd = jnp.broadcast_to(lax.rsqrt(square_mean + epsilon), (rows, HEAD_DIM))
        rstd_buf[slot] = rstd
        for t in range(KV_HEADS):
            for g in range(GROUP):
                cols = slice(g * HEAD_DIM, (g + 1) * HEAD_DIM)
                gain = gain_of(home, d, slice(t * tile + g * HEAD_DIM, t * tile + (g + 1) * HEAD_DIM))
                part = hbuf[d, parity, t, :, cols].astype(F32)
                nbuf[slot, t, :, cols] = (part * rstd * gain).astype(BF16)

    def make_masks():
        key_places = (shard - 1) * rows + lax.broadcasted_iota(jnp.int32, (2 * rows, rows), 0)
        places = shard * rows + lax.broadcasted_iota(jnp.int32, (2 * rows, rows), 1)
        for d in range(2):
            end = jnp.int32(0)
            docs_k = jnp.zeros((2 * rows, rows), jnp.int32)
            docs_q = jnp.zeros((2 * rows, rows), jnp.int32)
            for j in range(lengths_ref.shape[1]):
                end = end + lengths_ref[d, j]
                docs_k = docs_k + jnp.where(key_places >= end, 1, 0)
                docs_q = docs_q + jnp.where(places >= end, 1, 0)
            allowed = (docs_k == docs_q) & (key_places <= places) & (key_places >= 0)
            bias[d] = jnp.where(allowed, 0.0, -1e30).astype(F32)
        sublane = lax.broadcasted_iota(jnp.int32, (rows, rows), 0)
        lane = lax.broadcasted_iota(jnp.int32, (rows, rows), 1)
        triangle[0] = jnp.where(sublane > lane, 1.0, 0.0).astype(BF16)
        triangle[1] = jnp.where(sublane <= lane, 1.0, 0.0).astype(BF16)
        triangle[2] = jnp.where(lane > sublane, 1.0, 0.0).astype(BF16)
        triangle[3] = jnp.where(lane <= sublane, 1.0, 0.0).astype(BF16)

    middle = (near_depth == far_depth - 1) & (near_depth > 0)

    def arrive(d, l, depth, k):
        z_copy(d, l, k).wait_recv()
        s_copy(d, l, k).start()

        @pl.when(depth < count - 1)
        def _():
            z_copy(d, l, k).start()

    def project(d, depth):
        @pl.when(depth > 0)
        def _():
            normalize(d, depth, lax.rem(depth, 2), d)

        def chunk(k, carry):
            @pl.when(middle & (depth == near_depth))
            def _():
                arrive(far, 0, far_depth, k)

            weight_copy(d, k, 0).wait()
            weight_copy(d, k, 1).wait()
            normed = jnp.concatenate([nbuf[d, t] for t in range(KV_HEADS)], axis=1)
            pair = dot(normed, wbuf[d, k], ((1,), (0,))).astype(BF16)
            kv[d, depth, k, 0, rows:, :] = pair[:, :HEAD_DIM]
            kv[d, depth, k, 1, rows:, :] = pair[:, HEAD_DIM:]

            @pl.when(depth < count - 1)
            def _():
                z_copy(d, depth, k).start()

            @pl.when(jnp.logical_not(middle & (depth == near_depth)))
            def _():
                s_copy(d, depth, k).start()

            return carry

        lax.fori_loop(0, KV_HEADS, chunk, 0)

    def softmax(d, l, k, slot, g):
        both = dot(kv[d, l, k, 0], nbuf[slot, k, :, g * HEAD_DIM:(g + 1) * HEAD_DIM], ((1,), (1,)))
        scores = jnp.maximum(both[:rows] + bias[d, :rows, :], both[rows:] + bias[d, rows:, :])
        powers = jnp.exp2((scores - jnp.max(scores, axis=0, keepdims=True)) * (SCALE * LOG2E))
        weights = (powers * (1.0 / jnp.sum(powers, axis=0, keepdims=True))).astype(BF16)
        wsave[slot, k, g] = weights
        return weights

    def mix(d, l, depth):
        parity = lax.rem(l, 2)

        @pl.when(l < depth)
        def _():
            home = l + d * (count - 1 - 2 * l)
            gain_copy(lax.rem(section - home + count, count)).wait_recv()
            normalize(d, l, parity, d)

        squares_buf[d] = jnp.zeros((rows, HEAD_DIM), F32)

        coming = (l < depth) & ((d == near) | ((l == 0) & jnp.logical_not(middle)))
        ahead = (d == far) & (l + 1 < far_depth)

        @pl.when(coming)
        def _():
            for k in range(KV_HEADS):
                arrive(d, l, depth, k)

        def chunk(k, carry):
            s_copy(d, l, k).wait_recv()
            values = kv[d, l, k, 1]
            spreads = []
            for g in range(GROUP):
                weights = softmax(d, l, k, d, g)
                turned = weights.T
                spreads.append(jnp.concatenate([turned * triangle[2], turned * triangle[3]], axis=1))
            for g in range(GROUP):
                cols = slice(g * HEAD_DIM, (g + 1) * HEAD_DIM)
                total = hbuf[d, parity, k, :, cols].astype(F32) + dot(spreads[g], values, ((1,), (0,)))
                hbuf[d, 1 - parity, k, :, cols] = total.astype(BF16)
                squares_buf[d] += total * total

            @pl.when(l == depth)
            def _():
                act_copy(d, 1 - parity, k).start()

            @pl.when(ahead)
            def _():
                arrive(far, l + 1, far_depth, k)

            return carry

        lax.fori_loop(0, KV_HEADS, chunk, 0)

    @pl.when(near_depth == 0)
    def _():
        normalize(near, 0, 0, near)

    pl.semaphore_wait(barrier, count + 2)
    closest = lax.rem(1 - 2 * near + count, count)
    gain_copy(closest).start()

    def forward(v, carry):
        p = near_depth
        is_near = (v < p) | (v == jnp.where(p == 0, 0, count))
        d = jnp.where(is_near, near, far)
        depth = jnp.where(is_near, near_depth, far_depth)
        l = jnp.where(is_near, jnp.where(v < p, v, p), jnp.where(p == 0, v - 1, v - p))
        far_turn = jnp.where(p == 0, count, count - 1)

        @pl.when((v == p) | (v == far_turn))
        def _():
            pd = jnp.where(v == p, near, far)
            project(pd, jnp.where(v == p, near_depth, far_depth))

            @pl.when((v == far_turn) & middle)
            def _():
                for k in range(KV_HEADS):
                    s_copy(near, near_depth, k).start()

            @pl.when((v == far_turn) & (near_depth == 1))
            def _():
                for k in range(KV_HEADS):
                    back_copy(k).start()
                for i in range(PIECES):
                    quarter_copy(i).start()

        @pl.when(v == 0)
        def _():
            for further in range(1, count - 1):
                gain_copy(1 + lax.rem(closest - 1 + further, count - 1)).start()
            make_masks()

        mix(d, l, depth)
        return carry

    lax.fori_loop(0, count + 1, forward, 0)

    def drain_forward():
        for distance in range(1, count):
            gain_copy(distance).wait_send()
        for d in range(2):
            depth = depth_of(d)

            def layer_drain(l, carry):
                for k in range(KV_HEADS):
                    @pl.when(depth < count - 1)
                    def _():
                        z_copy(d, l, k).wait_send()

                    s_copy(d, l, k).wait_send()
                return carry

            lax.fori_loop(0, depth + 1, layer_drain, 0)
            for k in range(KV_HEADS):
                act_copy(d, lax.rem(depth + 1, 2), k).wait()

    def drain_reverse(d, depth):
        for k in range(KV_HEADS):
            d_copy(d, k).wait_send()

            @pl.when(depth > 0)
            def _():
                for part in range(PARTS):
                    c_copy(d, k, d, part).wait_send()

            ing_copy(d, k).wait()
            kvg_copy(d, k, 0).wait()
            kvg_copy(d, k, 1).wait()

    def pass_opposite(i, carry):
        opposite_copy(i, 1 - side).wait_recv()
        sibling_copy(i, 1, core).start()
        return carry

    def take_sibling(i, carry):
        sibling_copy(i, 0, 1 - core).wait_recv()
        sibling_copy(i, 1, 1 - core).wait_recv()
        return carry

    def prepare():
        d = near

        def pass_quarter(i, carry):
            quarter_copy(i).wait_recv()
            opposite_copy(i, side).start()
            sibling_copy(i, 0, core).start()
            return carry

        for k in range(KV_HEADS):
            back_copy(k).wait_recv()
            s_copy(d, 1, k).start()
        normalize(d, 1, 1, extra)

        def chunk(k, carry):
            s_copy(d, 1, k).wait_recv()
            for g in range(GROUP):
                softmax(d, 1, k, extra, g)
            return carry

        lax.fori_loop(0, KV_HEADS, chunk, 0)
        lax.fori_loop(0, PIECES, pass_quarter, 0)
        drain_forward()
        drain_reverse(far, far_depth)

    def backward(i, carry):
        @pl.when((i != 1) | (near_depth == 0))
        def _():
            reverse_layer(i)

        return carry

    def reverse_layer(i):
        repeated = i == 1
        local = (i == 2) & (near_depth == 0)
        d = jnp.where(i == 0, far, near)
        depth = jnp.where(i == 0, far_depth, jnp.where(repeated, 1, near_depth))
        slot = jnp.where(repeated, extra, d)
        coming = jnp.where(local, 2, d)
        leaving = jnp.where(repeated, 2, 3 + d)
        first = depth == count - 1
        streamed = (depth < count - 1) & ((i != 2) | (near_depth > 0))
        added = streamed & (i != 1)
        parity = lax.rem(depth, 2)
        step = 2 * HEAD_DIM

        @pl.when(repeated)
        def _():
            prepare()

        def settle(k):
            d_copy(slot, k).wait_recv()
            for part in range(2):
                total = downs[k, part].astype(F32) + drecv[slot, k, part].astype(F32)
                dtot[slot, k, :, part * HEAD_DIM:(part + 1) * HEAD_DIM] = total.astype(BF16)

                @pl.when(i != 1)
                def _():
                    kvg_copy(d, k, part).start()

        def grad_part(k, t, u):
            start = pl.multiple_of(t * tile + u * step, step)
            return dot(dtot[slot, k], wbuf[slot, k, pl.ds(start, step), :], ((1,), (1,)))

        def finish(k):
            settle(k)

            def part_tile(t, tile_carry):
                for u in range(tile // step):
                    cols = slice(u * step, (u + 1) * step)
                    part = grad_part(k, t, u)
                    gnbuf[t, :, cols] = jnp.where(k == 0, part, part + gnbuf[t, :, cols])
                return tile_carry

            lax.fori_loop(0, KV_HEADS, part_tile, 0)

        def chunk(k, inner_carry):
            @pl.when(streamed)
            def _():
                for part in range(PARTS):
                    c_copy(d, k, d, part).wait_recv()

                    @pl.when((depth == 1) & (i != 1))
                    def _():
                        c_copy(d, k, d, part).start()

            @pl.when(first)
            def _():
                pltpu.make_async_copy(cbuf.at[d, k], cbuf.at[d, k], c_sem.at[d, k]).wait()

            keys = kv[d, depth, k, 0]
            values = kv[d, depth, k, 1]
            earlier_s, own_s, earlier_w, own_w, queries, cots, spreads = [], [], [], [], [], [], []
            own_first = lax.broadcasted_iota(jnp.int32, (rows, rows), 0) <= (
                lax.broadcasted_iota(jnp.int32, (rows, rows), 1)
            )
            for g in range(GROUP):
                cols = slice(g * HEAD_DIM, (g + 1) * HEAD_DIM)
                cot = cbuf[coming, k, :, cols]
                both = dot(values, cot, ((1,), (1,)))
                weights = wsave[slot, k, g]
                wide = weights.astype(F32)
                grad_w = jnp.where(own_first, both[rows:], both[:rows]) * wide
                mean = jnp.sum(grad_w, axis=0, keepdims=True)
                grad_s = ((grad_w - wide * mean) * SCALE).astype(BF16)
                earlier_s.append(grad_s * triangle[0])
                own_s.append(grad_s * triangle[1])
                earlier_w.append(weights * triangle[0])
                own_w.append(weights * triangle[1])
                queries.append(nbuf[slot, k, :, cols])
                cots.append(cot)
                turned = grad_s.T
                spreads.append(jnp.concatenate([turned * triangle[2], turned * triangle[3]], axis=1))
            for g in range(GROUP):
                cols = slice(g * HEAD_DIM, (g + 1) * HEAD_DIM)
                dqbuf[k, :, cols] = dot(spreads[g], keys, ((1,), (0,))).astype(BF16)
            all_s = jnp.concatenate(
                [jnp.concatenate(earlier_s, axis=1), jnp.concatenate(own_s, axis=1)], axis=0
            )
            all_w = jnp.concatenate(
                [jnp.concatenate(earlier_w, axis=1), jnp.concatenate(own_w, axis=1)], axis=0
            )
            grad_k = dot(all_s, jnp.concatenate(queries, axis=0), ((1,), (0,)))
            grad_v = dot(all_w, jnp.concatenate(cots, axis=0), ((1,), (0,)))
            dsend[slot, k, 0] = grad_k[:rows].astype(BF16)
            dsend[slot, k, 1] = grad_v[:rows].astype(BF16)
            downs[k, 0] = grad_k[rows:].astype(BF16)
            downs[k, 1] = grad_v[rows:].astype(BF16)
            d_copy(slot, k).start()

            @pl.when((k > 0) & added)
            def _():
                finish(k - 1)

            @pl.when(repeated & (k > 0) & (k < 3))
            def _():
                lax.fori_loop((k - 1) * (PIECES // 2), k * (PIECES // 2), pass_opposite, 0)

            return inner_carry

        lax.fori_loop(0, KV_HEADS, chunk, 0)

        @pl.when(repeated)
        def _():
            lax.fori_loop(0, PIECES, take_sibling, 0)

        @pl.when(jnp.logical_not(added))
        def _():
            for k in range(KV_HEADS - 1):
                settle(k)

        settle(KV_HEADS - 1)
        home = depth + d * (count - 1 - 2 * depth)
        rstd = rstd_buf[slot]
        inner_buf[...] = jnp.zeros((rows, HEAD_DIM), F32)

        def grad_tile(heads, t, tile_carry):
            for u in range(tile // step):
                cols = slice(u * step, (u + 1) * step)
                start = pl.multiple_of(t * tile + u * step, step)
                pairs = jnp.concatenate([dtot[slot, k] for k in heads], axis=1)
                weights = jnp.concatenate([wbuf[slot, k, pl.ds(start, step), :] for k in heads], axis=1)
                grad = dot(pairs, weights, ((1,), (1,)))
                if len(heads) < KV_HEADS:
                    grad = grad + gnbuf[t, :, cols]
                grad_n = (grad + dqbuf[t, :, cols].astype(F32)) * gain_of(home, d, pl.ds(start, step))
                gnbuf[t, :, cols] = grad_n
                product = grad_n * hbuf[d, parity, t, :, cols].astype(F32)
                inner_buf[...] += product[:, :HEAD_DIM] + product[:, HEAD_DIM:]
            return tile_carry

        for whole, heads in ((False, range(KV_HEADS - 1, KV_HEADS)), (True, range(KV_HEADS))):
            @pl.when(added != whole)
            def _():
                lax.fori_loop(0, KV_HEADS, functools.partial(grad_tile, heads), 0)

        inner = inner_buf[...]
        inner = jnp.broadcast_to(jnp.sum(inner, axis=-1, keepdims=True), (rows, HEAD_DIM))
        factor = inner * (1.0 / width) * rstd * rstd * rstd

        def total_tile(t, inner_carry):
            for g in range(GROUP):
                cols = slice(g * HEAD_DIM, (g + 1) * HEAD_DIM)
                grad_h = gnbuf[t, :, cols] * rstd - hbuf[d, parity, t, :, cols].astype(F32) * factor
                cbuf[leaving, t, :, cols] = (cbuf[coming, t, :, cols].astype(F32) + grad_h).astype(BF16)

            @pl.when(depth > 1)
            def _():
                for part in range(PARTS):
                    c_copy(d, t, 3 + d, part).start()

            @pl.when(i != 1)
            def _():
                ing_copy(d, t).start()

            return inner_carry

        lax.fori_loop(0, KV_HEADS, total_tile, 0)

    lax.fori_loop(0, 3, backward, 0)

    @pl.when(near_depth == 1)
    def _():
        for k in range(KV_HEADS):
            back_copy(k).wait_send()
        for i in range(PIECES):
            quarter_copy(i).wait_send()

    @pl.when(near_depth == 0)
    def _():
        for k in range(KV_HEADS):
            s_copy(near, 1, k).wait_send()
            d_copy(extra, k).wait_send()
        for i in range(PIECES):
            opposite_copy(i, side).wait_send()
            sibling_copy(i, 0, core).wait_send()
            sibling_copy(i, 1, core).wait_send()

    @pl.when(near_depth > 0)
    def _():
        drain_forward()
        drain_reverse(far, far_depth)

    drain_reverse(near, near_depth)


def hand_over_kernel(acts_ref, ingrad_ref, kvgrad_ref, acts_out, ingrad_out, kvgrad_out, wide, narrow, in_sem, out_sem):
    lines = acts_ref.shape[2] // 2
    moves = []
    for d in range(2):
        for part in range(2):
            block = (d, 0, pl.ds(part * lines, lines))
            for a, (source, target) in enumerate(((acts_ref, acts_out), (ingrad_ref, ingrad_out))):
                moves.append((source.at[block], wide.at[a, d, part], target.at[block]))
        moves.append((kvgrad_ref.at[d, 0], narrow.at[d], kvgrad_out.at[d, 0]))
    inward = [pltpu.make_async_copy(m[0], m[1], in_sem.at[i]) for i, m in enumerate(moves)]
    outward = [pltpu.make_async_copy(m[1], m[2], out_sem.at[i]) for i, m in enumerate(moves)]
    for copy in inward:
        copy.start()
    for taken, given in zip(inward, outward):
        taken.wait()
        given.start()
    for copy in outward:
        copy.wait()


def hand_over(acts, ingrads, kvgrads):
    rows, width = acts.shape[2:]
    anywhere = pl.BlockSpec(memory_space=pl.ANY)
    return pl.pallas_call(
        hand_over_kernel,
        in_specs=[anywhere] * 3,
        out_specs=[anywhere] * 3,
        out_shape=[jax.ShapeDtypeStruct(a.shape, a.dtype) for a in (acts, ingrads, kvgrads)],
        scratch_shapes=[
            pltpu.VMEM((2, 2, 2, rows // 2, width), BF16),
            pltpu.VMEM((2, rows, kvgrads.shape[3]), BF16),
            pltpu.SemaphoreType.DMA((10,)),
            pltpu.SemaphoreType.DMA((10,)),
        ],
        compiler_params=pltpu.CompilerParams(vmem_limit_bytes=60 * 1024 * 1024),
        name="hand_over",
    )(acts, ingrads, kvgrads)


def per_device(x_a, x_b, grad_a, grad_b, gains, kv_weights, doc_lengths):
    count = lax.axis_size("section")
    shards = lax.axis_size("seq")
    rows, width = x_a.shape
    pair_width = kv_weights.shape[-1]
    tile = width // KV_HEADS
    dma = pltpu.SemaphoreType.DMA
    anywhere = pl.BlockSpec(memory_space=pl.ANY)
    results = pl.pallas_call(
        functools.partial(relay_kernel, count, shards),
        in_specs=[pl.BlockSpec(memory_space=pltpu.SMEM)] + [anywhere] * 6,
        out_specs=[anywhere] * 3,
        out_shape=[
            jax.ShapeDtypeStruct((2, 1, rows, width), BF16),
            jax.ShapeDtypeStruct((2, 1, rows, width), BF16),
            jax.ShapeDtypeStruct((2, 1, rows, pair_width), BF16),
        ],
        scratch_shapes=[
            pltpu.VMEM((3, KV_HEADS, width, 2 * HEAD_DIM), BF16),
            pltpu.VMEM((2, 2, KV_HEADS, rows, tile), BF16),
            pltpu.VMEM((3, KV_HEADS, rows, tile), BF16),
            pltpu.VMEM((2, count, KV_HEADS, 2, 2 * rows, HEAD_DIM), BF16),
            pltpu.VMEM((3, KV_HEADS, GROUP, rows, rows), BF16),
            pltpu.VMEM((5, KV_HEADS, rows, tile), BF16),
            pltpu.VMEM((KV_HEADS, rows, tile), BF16),
            pltpu.VMEM((KV_HEADS, rows, tile), F32),
            pltpu.VMEM((count, 2, width), F32),
            pltpu.VMEM((2, 2 * rows, rows), F32),
            pltpu.VMEM((3, rows, HEAD_DIM), F32),
            pltpu.VMEM((3, KV_HEADS, 2, rows, HEAD_DIM), BF16),
            pltpu.VMEM((3, KV_HEADS, 2, rows, HEAD_DIM), BF16),
            pltpu.VMEM((KV_HEADS, 2, rows, HEAD_DIM), BF16),
            pltpu.VMEM((3, KV_HEADS, rows, 2 * HEAD_DIM), BF16),
            pltpu.VMEM((4, rows, rows), BF16),
            pltpu.VMEM((2, rows, HEAD_DIM), F32),
            pltpu.VMEM((rows, HEAD_DIM), F32),
            dma((2, KV_HEADS)),
            dma((2, KV_HEADS, 2)),
            dma((2, KV_HEADS)),
            dma(()),
            dma((count - 1,)),
            dma((count - 1,)),
            dma((2, count, KV_HEADS)),
            dma((2, count, KV_HEADS)),
            dma((2, count, KV_HEADS)),
            dma((2, count, KV_HEADS)),
            dma((2, KV_HEADS, PARTS)),
            dma((2, KV_HEADS, PARTS)),
            dma((3, KV_HEADS)),
            dma((3, KV_HEADS)),
            dma((2, KV_HEADS)),
            dma((2, KV_HEADS)),
            dma((2, KV_HEADS, 2)),
            dma((KV_HEADS,)),
            dma((PIECES,)),
            dma((PIECES,)),
            dma((PIECES,)),
            dma((PIECES,)),
            dma((2, PIECES)),
            dma((2, PIECES)),
        ],
        compiler_params=pltpu.CompilerParams(
            collective_id=0, has_side_effects=True, vmem_limit_bytes=60 * 1024 * 1024
        ),
        name="relay",
    )(doc_lengths, x_a, x_b, grad_a, grad_b, gains, kv_weights)
    return hand_over(*results)


def solution(mesh):
    in_specs = (
        P("seq", None),
        P("seq", None),
        P("seq", None),
        P("seq", None),
        P("section", None, None),
        P("section", None, None, None),
        P(),
    )
    out_specs = (
        P(None, "section", "seq", None),
        P(None, "section", "seq", None),
        P(None, "section", "seq", None),
    )
    return jax.shard_map(
        per_device, mesh=mesh, in_specs=in_specs, out_specs=out_specs, check_vma=False
    )
```
